256 devices in a mesh: seq: 32 (over z, x), head: 8 (over y, core).
Axes of the slice: x: 4, y: 4, z: 8, core: 2. Of those that a mesh axis runs over, the one named last changes fastest.
Arguments:
- queries: bfloat16 [16384, 1024], P(('seq', 'head')), may hold values from -24 to 24
- keys: bfloat16 [16384, 1024], P(('seq', 'head')), may hold values from -6 to 6
- values: bfloat16 [16384, 1024], P(('seq', 'head')), may hold values from -6 to 6
- out_grad: bfloat16 [16384, 1024], P(('seq', 'head')), may hold values from -6 to 6
- key_blocks: int32 [128, 8], replicated, may hold values from 0 to 127, as said below
- counts: int32 [128], replicated, may hold values from 2 to 8, as said below
Outputs:
- attention: bfloat16 [16384, 1024], P('seq', 'head')
- query_grad: bfloat16 [16384, 1024], P('seq', 'head')
- key_grad: bfloat16 [16384, 1024], P('seq', 'head')
- value_grad: bfloat16 [16384, 1024], P('seq', 'head')
The draws below stay inside these ranges and needn't reach their ends.
Inputs may be any that keep to these rules, and one draw needn't show every extreme that they name: `counts`: some query block uses all 8 listed blocks. `key_blocks`: row a lists 8 different blocks, the first being block a itself and the second block (a - 1) modulo 128; only the first counts[a] of them are used.
All inputs are finite; a program needn't handle non-finite values.
Results may differ from the reference program's by a relative error of at most 0.015.
Values may be sent and summed in bfloat16 or wider, within the bound.
A program may use at most 64 MiB of HBM per device.

```python
import math
import jax
import jax.numpy as jnp
from jax import lax

HEADS = 8
HD = 128
D = 1024
BLK = 128
BLK_SEQ = 4
KMAX = 8
NB = 128
TOKENS = 16384


def key_field(key):
    full_width = HEADS * HD
    raw = jax.random.normal(jax.random.fold_in(key, 41), (TOKENS, full_width), jnp.float32)
    return jnp.clip(raw, -6.0, 6.0)


def draw_keys(key, part):
    return key_field(key).astype(jnp.bfloat16)


def draw_queries(key, part):
    full_width = HEADS * HD
    raw = jax.random.normal(jax.random.fold_in(key, 42), (TOKENS, full_width), jnp.float32)
    return jnp.clip(raw, -6.0, 6.0).astype(jnp.bfloat16)


def pattern(key):
    base = jax.random.fold_in(key, 7)
    block_ids = jnp.arange(NB)
    regions = block_ids // BLK_SEQ
    shifts = jax.random.randint(jax.random.fold_in(base, 1), (NB,), 0, 3)
    level = jnp.maximum(KMAX // jnp.left_shift(1, shifts[regions]), 1)
    raw = jax.random.randint(jax.random.fold_in(base, 2), (NB,), 0, 1 << 20)
    used = jnp.maximum(1 + raw % level, 2)
    chosen_row = jax.random.randint(jax.random.fold_in(base, 3), (), 0, NB)
    used = jnp.where(block_ids == chosen_row, KMAX, used).astype(jnp.int32)
    ranks = jax.random.randint(jax.random.fold_in(base, 4), (NB, NB), 0, 1 << 20) * NB + block_ids[None, :]
    before = (block_ids[:, None] + NB - 1) % NB
    ranks = jnp.where(block_ids[None, :] == before, (1 << 30) - 1, ranks)
    ranks = jnp.where(block_ids[:, None] == block_ids[None, :], 1 << 30, ranks)
    listed = lax.top_k(ranks, KMAX)[1].astype(jnp.int32)
    return (listed, used)


def draw_key_blocks(key, part):
    return pattern(key)[0]


def draw_counts(key, part):
    return pattern(key)[1]


def level_of(key, extent, cuts, smallest, high):
    gain = 1.0
    for axis_at, parts in cuts:
        steps = jax.random.uniform(jax.random.fold_in(jax.random.fold_in(key, 6), axis_at), (parts,), jnp.float32, smallest / len(cuts), high / len(cuts))
        gain = gain * jnp.repeat(jnp.exp(steps), extent[axis_at] // parts).reshape((-1,) + (1,) * (len(extent) - 1 - axis_at))
    return gain


def centred(stream_key, dims, width, most, split=(), held_as=jnp.bfloat16):
    array = jax.random.normal(stream_key, dims, jnp.float32) * width
    if len(split) > 0:
        array = level_of(stream_key, dims, split, -0.22, 0.18) * array
    return jnp.clip(array, min=-most, max=most).astype(held_as)


def setup_inputs(seed: int = 0) -> dict:
    arg_keys = jax.random.split(jax.random.key(seed), 7)
    queries = draw_queries(jax.random.fold_in(arg_keys[6], 71), 0)
    keys = draw_keys(jax.random.fold_in(arg_keys[6], 71), 0)
    values = centred(arg_keys[2], (TOKENS, D), 1.0, 6.0, ((0, 256),))
    out_grad = centred(arg_keys[3], (TOKENS, D), 1.0, 6.0, ((0, 256),))
    key_blocks = draw_key_blocks(jax.random.fold_in(arg_keys[6], 71), 0)
    counts = draw_counts(jax.random.fold_in(arg_keys[6], 71), 0)
    return dict(queries=queries, keys=keys, values=values, out_grad=out_grad, key_blocks=key_blocks, counts=counts)


neg_fill = -1e+30

def rounded(value):
    return lax.optimization_barrier(value.astype(jnp.bfloat16)).astype(jnp.float32)

def reference(queries, keys, values, out_grad, key_blocks, counts):
    block_count = TOKENS // BLK
    score_scale = 1.0 / math.sqrt(HD)
    query_all = queries.astype(jnp.float32).reshape(block_count, BLK, HEADS, HD)
    key_all = keys.astype(jnp.float32).reshape(block_count, BLK, HEADS, HD)
    value_all = values.astype(jnp.float32).reshape(block_count, BLK, HEADS, HD)
    grad_all = out_grad.astype(jnp.float32).reshape(block_count, BLK, HEADS, HD)
    slot_ids = jnp.arange(KMAX).astype(jnp.int32)

    def fetch(block_index):
        chosen = key_blocks[block_index]
        key_set = key_all[chosen].reshape(KMAX * BLK, HEADS, HD)
        value_set = value_all[chosen].reshape(KMAX * BLK, HEADS, HD)
        allowed = jnp.repeat(slot_ids < counts[block_index], BLK)
        scores = jnp.einsum('qhd,khd->qhk', query_all[block_index], key_set) * score_scale
        scores = jnp.where(allowed[None, None, :], scores, neg_fill)
        return (chosen, key_set, value_set, allowed, scores)

    def forward(block_index):
        chosen, key_set, value_set, allowed, scores = fetch(block_index)
        row_max = lax.optimization_barrier(jnp.max(scores, axis=2))
        weights = jnp.where(allowed[None, None, :], jnp.exp(scores - row_max[:, :, None]), 0.0)
        row_sum = lax.optimization_barrier(jnp.sum(weights, axis=2))
        mixed = jnp.einsum('qhk,khd->qhd', rounded(weights), value_set) / row_sum[:, :, None]
        return (mixed.astype(jnp.bfloat16), row_max + jnp.log(row_sum))
    attention, log_total = lax.map(forward, jnp.arange(block_count).astype(jnp.int32))
    attention_full = attention.astype(jnp.float32)

    def backward(running, block_index):
        key_acc, value_acc = running
        chosen, key_set, value_set, allowed, scores = fetch(block_index)
        grad_block = grad_all[block_index]
        grad_dot = lax.optimization_barrier(jnp.sum(grad_block * attention_full[block_index], axis=2))
        probs = jnp.where(allowed[None, None, :], jnp.exp(scores - log_total[block_index][:, :, None]), 0.0)
        dprob = jnp.einsum('qhd,khd->qhk', grad_block, value_set)
        dscore = rounded(probs * (dprob - grad_dot[:, :, None]))
        query_part = jnp.einsum('qhk,khd->qhd', dscore, key_set) * score_scale
        key_part = jnp.einsum('qhk,qhd->khd', dscore, query_all[block_index]) * score_scale
        value_part = jnp.einsum('qhk,qhd->khd', rounded(probs), grad_block)
        key_acc = key_acc.at[chosen].add(key_part.reshape(KMAX, BLK, HEADS, HD))
        value_acc = value_acc.at[chosen].add(value_part.reshape(KMAX, BLK, HEADS, HD))
        return ((key_acc, value_acc), query_part.astype(jnp.bfloat16))
    empty = jnp.zeros((block_count, BLK, HEADS, HD), jnp.float32)
    (key_acc, value_acc), query_grad = lax.scan(backward, (empty, empty), jnp.arange(block_count).astype(jnp.int32))
    full_width = HEADS * HD
    return (attention.reshape(TOKENS, full_width), query_grad.reshape(TOKENS, full_width), key_acc.astype(jnp.bfloat16).reshape(TOKENS, full_width), value_acc.astype(jnp.bfloat16).reshape(TOKENS, full_width))
```

```python
import functools
import heapq
import math

import jax
import jax.numpy as jnp
from jax import lax
from jax.experimental import pallas as pl
from jax.experimental.pallas import tpu as pltpu
from jax.sharding import PartitionSpec as P

MESH = pl.DeviceIdType.MESH
BLK = 128
HD = 128
NX = 4
NZ = 8
NH = 8
ROWS = 512
CHUNK = 64
SPLIT = 208
BF16 = jnp.bfloat16
F32 = jnp.float32
NEG = -1e30


def row_range(part):
    half_a, half_b = SPLIT // 32 * 16, SPLIT + (ROWS - SPLIT) // 32 * 16
    return {
        "A": (0, SPLIT),
        "A0": (0, half_a),
        "A1": (half_a, SPLIT),
        "B": (SPLIT, ROWS),
        "B0": (SPLIT, half_b),
        "B1": (half_b, ROWS),
    }[part]


def ring_sends(axis, sources, size, out, kind, prio):
    far = size // 2
    arrived = []
    for (offset, part, dep) in sources:
        if len(part) == 1:
            arrived.append((offset, part, dep))
            halves = [(part, +1, far - 1), (part, -1, far - 1)]
        else:
            arrived.append((offset, part, dep))
            sign = +1 if part[1] == "0" else -1
            halves = [(part, +1, far - 1), (part, -1, far - 1)]
        for (piece, sign, hops) in halves:
            last = dep
            at = offset
            for hop in range(1, hops + 1):
                out.append(dict(kind=kind, axis=axis, sign=sign, origin=at, part=piece, dep=last, left=far - hop, prio=prio))
                last = len(out) - 1
                at = step_offset(at, axis, sign)
                arrived.append((at, piece, last))
            for digit, way in (("0", +1), ("1", -1)):
                if way != sign:
                    continue
                tail = piece if len(piece) == 2 else piece + digit
                if tail[1] != digit:
                    continue
                out.append(dict(kind=kind, axis=axis, sign=sign, origin=at, part=tail, dep=last, left=0, prio=prio))
                arrived.append((step_offset(at, axis, sign), tail, len(out) - 1))
    return arrived


def step_offset(offset, axis, sign):
    ox, oz = offset
    return (ox + sign, oz) if axis == "x" else (ox, oz + sign)


def plan_sends():
    out = []
    for kind in (0, 1):
        own = -1 - kind
        first_a = ring_sends("x", [((0, 0), "A", own)], NX, out, kind, kind * 10)
        first_b = ring_sends("z", [((0, 0), "B", own)], NZ, out, kind, kind * 10)
        ring_sends("z", first_a, NZ, out, kind, kind * 10 + 1)
        ring_sends("x", first_b, NX, out, kind, kind * 10 + 1)
    rate = 46.0e3 * 1.0
    latency = 1.7
    ready_own = {-1: 4.0, -2: 8.0}
    arrival = {}
    free = {}
    start = {}
    waiting = {}
    events = []
    for i, m in enumerate(out):
        if m["dep"] < 0:
            heapq.heappush(events, (ready_own[m["dep"]], i))
    children = {}
    for i, m in enumerate(out):
        if m["dep"] >= 0:
            children.setdefault(m["dep"], []).append(i)
    queues = {("x", 1): [], ("x", -1): [], ("z", 1): [], ("z", -1): []}
    free = {k: 0.0 for k in queues}
    order = []
    while events or any(queues.values()):
        options = []
        for k, q in queues.items():
            if q:
                options.append((max(free[k], q[0][2]), k))
        next_link = min(options) if options else None
        if events and (next_link is None or events[0][0] <= next_link[0]):
            t, i = heapq.heappop(events)
            m = out[i]
            q = queues[(m["axis"], m["sign"])]
            q.append((m["prio"] // 10, -m["left"], t, i))
            q.sort(key=lambda e: (e[0], e[1], e[2], e[3]))
            continue
        t, k = next_link
        _, _, ready, i = queues[k].pop(0)
        m = out[i]
        lo, hi = row_range(m["part"])
        begin = max(free[k], ready)
        free[k] = begin + (hi - lo) * HD * 2 * 2 / rate
        start[i] = begin
        order.append((begin, ready, i))
        for c in children.get(i, []):
            heapq.heappush(events, (free[k] + latency, c))
    order.sort()
    return out, [i for (_, _, i) in order], max(free.values())


SENDS, ORDER, SPAN = plan_sends()


def exchange_kernel(q_ref, k_ref, v_ref, g_ref, kv_ref, qg_ref, send_sem, recv_sem, head_send, head_recv, own_sem):
    seq = lax.axis_index("seq")
    head = lax.axis_index("head")
    x, z = lax.rem(seq, NX), seq // NX

    def chip(cx, cz):
        return lax.rem(cz + 2 * NZ, NZ) * NX + lax.rem(cx + 2 * NX, NX)

    barrier = pltpu.get_barrier_semaphore()
    for shift in range(1, NH):
        pl.semaphore_signal(barrier, inc=1, device_id={"seq": seq, "head": lax.rem(head + shift, NH)}, device_id_type=MESH)
    for (cx, cz) in ((x + 1, z), (x - 1, z), (x, z + 1), (x, z - 1)):
        pl.semaphore_signal(barrier, inc=1, device_id={"seq": chip(cx, cz), "head": head}, device_id_type=MESH)
    pl.semaphore_wait(barrier, NH - 1 + 4)

    targets = ((k_ref, kv_ref, 0), (v_ref, kv_ref, 1), (q_ref, qg_ref, 0), (g_ref, qg_ref, 1))

    def rows_of(dst, which, h):
        return dst.at[seq, which, pl.ds(pl.multiple_of(h * CHUNK, CHUNK), CHUNK), :]

    def columns_of(src, h):
        return src.at[:, pl.ds(pl.multiple_of(h * HD, HD), HD)]

    head_copies = []
    own_copies = []
    for array, (src, dst, which) in enumerate(targets):
        for shift in range(1, NH):
            peer = lax.rem(head + shift, NH)
            copy = pltpu.make_async_remote_copy(
                src_ref=columns_of(src, peer),
                dst_ref=rows_of(dst, which, head),
                send_sem=head_send.at[array, shift],
                recv_sem=head_recv.at[array, shift],
                device_id={"seq": seq, "head": peer},
                device_id_type=MESH,
            )
            copy.start()
            head_copies.append(copy)
        own = pltpu.make_async_copy(columns_of(src, head), rows_of(dst, which, head), own_sem.at[array])
        own.start()
        own_copies.append(own)

    def wait_head(array):
        src, dst, which = targets[array]
        for shift in range(1, NH):
            peer = lax.rem(head + NH - shift, NH)
            pltpu.make_async_remote_copy(
                src_ref=columns_of(src, peer),
                dst_ref=rows_of(dst, which, peer),
                send_sem=head_send.at[array, shift],
                recv_sem=head_recv.at[array, shift],
                device_id={"seq": seq, "head": peer},
                device_id_type=MESH,
            ).wait_recv()
        own_copies[array].wait()

    buffers = (kv_ref, qg_ref)

    def piece(m, ox, oz):
        lo, hi = row_range(m["part"])
        return buffers[m["kind"]].at[chip(x - ox, z - oz), :, lo:hi, :]

    def send(i):
        m = SENDS[i]
        ox, oz = m["origin"]
        target = chip(x + m["sign"], z) if m["axis"] == "x" else chip(x, z + m["sign"])
        return pltpu.make_async_remote_copy(
            src_ref=piece(m, ox, oz),
            dst_ref=piece(m, ox, oz),
            send_sem=send_sem.at[i],
            recv_sem=recv_sem.at[i],
            device_id={"seq": target, "head": head},
            device_id_type=MESH,
        )

    def wait_recv(i):
        m = SENDS[i]
        ox, oz = step_offset(m["origin"], m["axis"], m["sign"])
        source = chip(x - m["sign"], z) if m["axis"] == "x" else chip(x, z - m["sign"])
        pltpu.make_async_remote_copy(
            src_ref=piece(m, ox, oz),
            dst_ref=piece(m, ox, oz),
            send_sem=send_sem.at[i],
            recv_sem=recv_sem.at[i],
            device_id={"seq": source, "head": head},
            device_id_type=MESH,
        ).wait_recv()

    ready = set()
    started = []
    for i in ORDER:
        dep = SENDS[i]["dep"]
        if dep not in ready:
            ready.add(dep)
            if dep < 0:
                wait_head(2 * (-1 - dep))
                wait_head(2 * (-1 - dep) + 1)
            else:
                wait_recv(dep)
        copy = send(i)
        copy.start()
        started.append(copy)
    for i in ORDER:
        if i not in ready:
            wait_recv(i)
    for copy in started:
        copy.wait_send()
    for copy in head_copies:
        copy.wait_send()


def exchange(queries, keys, values, out_grad):
    shape = jax.ShapeDtypeStruct((NX * NZ, 2, ROWS, HD), BF16)
    count = len(SENDS)
    return pl.pallas_call(
        exchange_kernel,
        out_shape=(shape, shape),
        in_specs=[pl.BlockSpec(memory_space=pltpu.VMEM)] * 4,
        out_specs=[pl.BlockSpec(memory_space=pl.ANY)] * 2,
        scratch_shapes=[
            pltpu.SemaphoreType.DMA((count,)),
            pltpu.SemaphoreType.DMA((count,)),
            pltpu.SemaphoreType.DMA((4, NH)),
            pltpu.SemaphoreType.DMA((4, NH)),
            pltpu.SemaphoreType.DMA((4,)),
        ],
        compiler_params=pltpu.CompilerParams(collective_id=0, has_side_effects=True),
    )(queries, keys, values, out_grad)


def dot_nt(a, b):
    return lax.dot_general(a, b, (((1,), (1,)), ((), ())), preferred_element_type=F32)


def dot_nn(a, b):
    return lax.dot_general(a, b, (((1,), (0,)), ((), ())), preferred_element_type=F32)


def dot_tn(a, b):
    return lax.dot_general(a, b, (((0,), (0,)), ((), ())), preferred_element_type=F32)


def attend_kernel(first_ref, touch_ref, blocks_ref, counts_ref, kv_ref, qg_ref, att_ref, dq_ref, dk_ref, dv_ref, s_ref, acc_ref, dk_acc, dv_acc):
    scale = 1.0 / math.sqrt(HD)
    dk_acc[...] = jnp.zeros_like(dk_acc)
    dv_acc[...] = jnp.zeros_like(dv_acc)
    first = first_ref[0]

    def load(ref, which, block):
        return ref[block // 4, which, pl.ds(pl.multiple_of(lax.rem(block, 4) * BLK, BLK), BLK), :]

    def query_block(a, local):
        count = counts_ref[a]
        q = load(qg_ref, 0, a)
        g = load(qg_ref, 1, a)

        def score(t, row_max):
            s = dot_nt(q, load(kv_ref, 0, blocks_ref[a, t])) * scale
            s_ref[t] = s
            return jnp.maximum(row_max, jnp.max(s, axis=1, keepdims=True))

        row_max = lax.fori_loop(0, count, score, jnp.full((BLK, 1), NEG, F32))
        acc_ref[...] = jnp.zeros_like(acc_ref)

        def mix(t, row_sum):
            w = jnp.exp(s_ref[t] - row_max)
            acc_ref[...] += dot_nn(w.astype(BF16), load(kv_ref, 1, blocks_ref[a, t]))
            return row_sum + jnp.sum(w, axis=1, keepdims=True)

        row_sum = lax.fori_loop(0, count, mix, jnp.zeros((BLK, 1), F32))
        att = (acc_ref[...] / row_sum).astype(BF16)
        total = row_max + jnp.log(row_sum)
        grad_dot = jnp.sum(g.astype(F32) * att.astype(F32), axis=1, keepdims=True)

        def pair(t):
            block = blocks_ref[a, t]
            p = jnp.exp(s_ref[t] - total)
            dp = dot_nt(g, load(kv_ref, 1, block))
            return block, p, (p * (dp - grad_dot)).astype(BF16)

        def add_key(slot, p, ds):
            dk_acc[slot] += dot_tn(ds, q)
            dv_acc[slot] += dot_tn(p.astype(BF16), g)

        if local:
            acc_ref[...] = jnp.zeros_like(acc_ref)

            def back(t, carry):
                block, p, ds = pair(t)
                acc_ref[...] += dot_nn(ds, load(kv_ref, 0, block))
                slot = block - first

                @pl.when((slot >= 0) & (slot < 4))
                def _():
                    add_key(slot, p, ds)

                return carry

            lax.fori_loop(0, count, back, 0)
            rows = pl.ds(pl.multiple_of((a - first) * BLK, BLK), BLK)
            att_ref[rows, :] = att
            dq_ref[rows, :] = (acc_ref[...] * scale).astype(BF16)
        else:

            def back(t, carry):
                slot = blocks_ref[a, t] - first

                @pl.when((slot >= 0) & (slot < 4))
                def _():
                    _, p, ds = pair(t)
                    add_key(slot, p, ds)

                return carry

            lax.fori_loop(0, count, back, 0)

    def own(i, carry):
        query_block(first + i, True)
        return carry

    lax.fori_loop(0, 4, own, 0)

    def other(a, carry):
        @pl.when(touch_ref[a] > 0)
        def _():
            query_block(a, False)

        return carry

    lax.fori_loop(0, 128, other, 0)
    for slot in range(4):
        dk_ref[slot * BLK : (slot + 1) * BLK, :] = (dk_acc[slot] * scale).astype(BF16)
        dv_ref[slot * BLK : (slot + 1) * BLK, :] = dv_acc[slot].astype(BF16)


def attend(first, touch, key_blocks, counts, kv, qg):
    shape = jax.ShapeDtypeStruct((ROWS, HD), BF16)
    smem = pl.BlockSpec(memory_space=pltpu.SMEM)
    vmem = pl.BlockSpec(memory_space=pltpu.VMEM)
    return pl.pallas_call(
        attend_kernel,
        out_shape=(shape,) * 4,
        in_specs=[smem] * 4 + [vmem] * 2,
        out_specs=[vmem] * 4,
        scratch_shapes=[
            pltpu.VMEM((8, BLK, BLK), F32),
            pltpu.VMEM((BLK, HD), F32),
            pltpu.VMEM((4, BLK, HD), F32),
            pltpu.VMEM((4, BLK, HD), F32),
        ],
    )(first, touch, key_blocks, counts, kv, qg)


def on_device(queries, keys, values, out_grad, key_blocks, counts):
    seq = lax.axis_index("seq")
    kv, qg = exchange(queries, keys, values, out_grad)
    used = jnp.arange(key_blocks.shape[1])[None, :] < counts[:, None]
    touch = jnp.any(used & (key_blocks // 4 == seq), axis=1)
    touch = (touch & (jnp.arange(key_blocks.shape[0]) // 4 != seq)).astype(jnp.int32)
    first = (seq * 4).reshape(1).astype(jnp.int32)
    return attend(first, touch, key_blocks, counts, kv, qg)


def solution(mesh):
    rows = P(("seq", "head"), None)
    out = P("seq", "head")
    return jax.shard_map(
        on_device,
        mesh=mesh,
        in_specs=(rows,) * 4 + (P(), P()),
        out_specs=(out,) * 4,
        check_vma=False,
    )
```

```python
import functools
import heapq
import math

import jax
import jax.numpy as jnp
from jax import lax
from jax.experimental import pallas as pl
from jax.experimental.pallas import tpu as pltpu
from jax.sharding import PartitionSpec as P

MESH = pl.DeviceIdType.MESH
BLK = 128
HD = 128
NX = 4
NZ = 8
NH = 8
ROWS = 512
CHUNK = 64
SPLIT = 208
BF16 = jnp.bfloat16
F32 = jnp.float32
NEG = -1e30


def row_range(part):
    half_a, half_b = SPLIT // 32 * 16, SPLIT + (ROWS - SPLIT) // 32 * 16
    return {
        "A": (0, SPLIT),
        "A0": (0, half_a),
        "A1": (half_a, SPLIT),
        "B": (SPLIT, ROWS),
        "B0": (SPLIT, half_b),
        "B1": (half_b, ROWS),
    }[part]


def ring_sends(axis, sources, size, out, kind, prio):
    far = size // 2
    arrived = []
    for (offset, part, dep) in sources:
        if len(part) == 1:
            arrived.append((offset, part, dep))
            halves = [(part, +1, far - 1), (part, -1, far - 1)]
        else:
            arrived.append((offset, part, dep))
            sign = +1 if part[1] == "0" else -1
            halves = [(part, +1, far - 1), (part, -1, far - 1)]
        for (piece, sign, hops) in halves:
            last = dep
            at = offset
            for hop in range(1, hops + 1):
                out.append(dict(kind=kind, axis=axis, sign=sign, origin=at, part=piece, dep=last, left=far - hop, prio=prio))
                last = len(out) - 1
                at = step_offset(at, axis, sign)
                arrived.append((at, piece, last))
            for digit, way in (("0", +1), ("1", -1)):
                if way != sign:
                    continue
                tail = piece if len(piece) == 2 else piece + digit
                if tail[1] != digit:
                    continue
                out.append(dict(kind=kind, axis=axis, sign=sign, origin=at, part=tail, dep=last, left=0, prio=prio))
                arrived.append((step_offset(at, axis, sign), tail, len(out) - 1))
    return arrived


def step_offset(offset, axis, sign):
    ox, oz = offset
    return (ox + sign, oz) if axis == "x" else (ox, oz + sign)


def plan_sends():
    out = []
    for kind in (0, 1):
        own = -1 - kind
        first_a = ring_sends("x", [((0, 0), "A", own)], NX, out, kind, kind * 10)
        first_b = ring_sends("z", [((0, 0), "B", own)], NZ, out, kind, kind * 10)
        ring_sends("z", first_a, NZ, out, kind, kind * 10 + 1)
        ring_sends("x", first_b, NX, out, kind, kind * 10 + 1)
    rate = 46.0e3 * 1.0
    latency = 1.7
    ready_own = {-1: 4.0, -2: 8.0}
    arrival = {}
    free = {}
    start = {}
    waiting = {}
    events = []
    for i, m in enumerate(out):
        if m["dep"] < 0:
            heapq.heappush(events, (ready_own[m["dep"]], i))
    children = {}
    for i, m in enumerate(out):
        if m["dep"] >= 0:
            children.setdefault(m["dep"], []).append(i)
    queues = {("x", 1): [], ("x", -1): [], ("z", 1): [], ("z", -1): []}
    free = {k: 0.0 for k in queues}
    order = []
    while events or any(queues.values()):
        options = []
        for k, q in queues.items():
            if q:
                options.append((max(free[k], q[0][2]), k))
        next_link = min(options) if options else None
        if events and (next_link is None or events[0][0] <= next_link[0]):
            t, i = heapq.heappop(events)
            m = out[i]
            q = queues[(m["axis"], m["sign"])]
            q.append((m["prio"] // 10, -m["left"], t, i))
            q.sort(key=lambda e: (e[0], e[1], e[2], e[3]))
            continue
        t, k = next_link
        _, _, ready, i = queues[k].pop(0)
        m = out[i]
        lo, hi = row_range(m["part"])
        begin = max(free[k], ready)
        free[k] = begin + (hi - lo) * HD * 2 * 2 / rate
        start[i] = begin
        order.append((begin, ready, i))
        for c in children.get(i, []):
            heapq.heappush(events, (free[k] + latency, c))
    order.sort()
    return out, [i for (_, _, i) in order], max(free.values())


SENDS, ORDER, SPAN = plan_sends()


def exchange_kernel(q_ref, k_ref, v_ref, g_ref, kv_ref, qg_ref, send_sem, recv_sem, head_send, head_recv, own_sem):
    seq = lax.axis_index("seq")
    head = lax.axis_index("head")
    x, z = lax.rem(seq, NX), seq // NX

    def chip(cx, cz):
        return lax.rem(cz + 2 * NZ, NZ) * NX + lax.rem(cx + 2 * NX, NX)

    barrier = pltpu.get_barrier_semaphore()
    for shift in range(1, NH):
        pl.semaphore_signal(barrier, inc=1, device_id={"seq": seq, "head": lax.rem(head + shift, NH)}, device_id_type=MESH)
    for (cx, cz) in ((x + 1, z), (x - 1, z), (x, z + 1), (x, z - 1)):
        pl.semaphore_signal(barrier, inc=1, device_id={"seq": chip(cx, cz), "head": head}, device_id_type=MESH)
    pl.semaphore_wait(barrier, NH - 1 + 4)

    targets = ((k_ref, kv_ref, 0), (v_ref, kv_ref, 1), (q_ref, qg_ref, 0), (g_ref, qg_ref, 1))

    def rows_of(dst, which, h):
        return dst.at[seq, which, pl.ds(pl.multiple_of(h * CHUNK, CHUNK), CHUNK), :]

    def columns_of(src, h):
        return src.at[:, pl.ds(pl.multiple_of(h * HD, HD), HD)]

    head_copies = []
    own_copies = []
    for array, (src, dst, which) in enumerate(targets):
        for shift in range(1, NH):
            peer = lax.rem(head + shift, NH)
            copy = pltpu.make_async_remote_copy(
                src_ref=columns_of(src, peer),
                dst_ref=rows_of(dst, which, head),
                send_sem=head_send.at[array, shift],
                recv_sem=head_recv.at[array, shift],
                device_id={"seq": seq, "head": peer},
                device_id_type=MESH,
            )
            copy.start()
            head_copies.append(copy)
        own = pltpu.make_async_copy(columns_of(src, head), rows_of(dst, which, head), own_sem.at[array])
        own.start()
        own_copies.append(own)

    def wait_head(array):
        src, dst, which = targets[array]
        for shift in range(1, NH):
            peer = lax.rem(head + NH - shift, NH)
            pltpu.make_async_remote_copy(
                src_ref=columns_of(src, peer),
                dst_ref=rows_of(dst, which, peer),
                send_sem=head_send.at[array, shift],
                recv_sem=head_recv.at[array, shift],
                device_id={"seq": seq, "head": peer},
                device_id_type=MESH,
            ).wait_recv()
        own_copies[array].wait()

    buffers = (kv_ref, qg_ref)

    def piece(m, ox, oz):
        lo, hi = row_range(m["part"])
        return buffers[m["kind"]].at[chip(x - ox, z - oz), :, lo:hi, :]

    def send(i):
        m = SENDS[i]
        ox, oz = m["origin"]
        target = chip(x + m["sign"], z) if m["axis"] == "x" else chip(x, z + m["sign"])
        return pltpu.make_async_remote_copy(
            src_ref=piece(m, ox, oz),
            dst_ref=piece(m, ox, oz),
            send_sem=send_sem.at[i],
            recv_sem=recv_sem.at[i],
            device_id={"seq": target, "head": head},
            device_id_type=MESH,
        )

    def wait_recv(i):
        m = SENDS[i]
        ox, oz = step_offset(m["origin"], m["axis"], m["sign"])
        source = chip(x - m["sign"], z) if m["axis"] == "x" else chip(x, z - m["sign"])
        pltpu.make_async_remote_copy(
            src_ref=piece(m, ox, oz),
            dst_ref=piece(m, ox, oz),
            send_sem=send_sem.at[i],
            recv_sem=recv_sem.at[i],
            device_id={"seq": source, "head": head},
            device_id_type=MESH,
        ).wait_recv()

    ready = set()
    started = []
    for i in ORDER:
        dep = SENDS[i]["dep"]
        if dep not in ready:
            ready.add(dep)
            if dep < 0:
                wait_head(2 * (-1 - dep))
                wait_head(2 * (-1 - dep) + 1)
            else:
                wait_recv(dep)
        copy = send(i)
        copy.start()
        started.append(copy)
    for i in ORDER:
        if i not in ready:
            wait_recv(i)
    for copy in started:
        copy.wait_send()
    for copy in head_copies:
        copy.wait_send()


def exchange(queries, keys, values, out_grad):
    shape = jax.ShapeDtypeStruct((NX * NZ, 2, ROWS, HD), BF16)
    count = len(SENDS)
    return pl.pallas_call(
        exchange_kernel,
        out_shape=(shape, shape),
        in_specs=[pl.BlockSpec(memory_space=pltpu.VMEM)] * 4,
        out_specs=[pl.BlockSpec(memory_space=pl.ANY)] * 2,
        scratch_shapes=[
            pltpu.SemaphoreType.DMA((count,)),
            pltpu.SemaphoreType.DMA((count,)),
            pltpu.SemaphoreType.DMA((4, NH)),
            pltpu.SemaphoreType.DMA((4, NH)),
            pltpu.SemaphoreType.DMA((4,)),
        ],
        compiler_params=pltpu.CompilerParams(collective_id=0, has_side_effects=True),
    )(queries, keys, values, out_grad)


def dot_nt(a, b):
    return lax.dot_general(a, b, (((1,), (1,)), ((), ())), preferred_element_type=F32)


def dot_nn(a, b):
    return lax.dot_general(a, b, (((1,), (0,)), ((), ())), preferred_element_type=F32)


def dot_tn(a, b):
    return lax.dot_general(a, b, (((0,), (0,)), ((), ())), preferred_element_type=F32)


def attend_kernel(first_ref, touch_ref, blocks_ref, counts_ref, kv_ref, qg_ref, att_ref, dq_ref, dk_ref, dv_ref, s_ref, acc_ref, dk_acc, dv_acc):
    scale = 1.0 / math.sqrt(HD)
    dk_acc[...] = jnp.zeros_like(dk_acc)
    dv_acc[...] = jnp.zeros_like(dv_acc)
    first = first_ref[0]

    def load(ref, which, block):
        return ref[block // 4, which, pl.ds(pl.multiple_of(lax.rem(block, 4) * BLK, BLK), BLK), :]

    def query_block(a, local):
        count = counts_ref[a]
        q = load(qg_ref, 0, a)
        g = load(qg_ref, 1, a)

        def score(t, row_max):
            s = dot_nt(q, load(kv_ref, 0, blocks_ref[a, t])) * scale
            s_ref[t] = s
            return jnp.maximum(row_max, jnp.max(s, axis=1, keepdims=True))

        row_max = lax.fori_loop(0, count, score, jnp.full((BLK, 1), NEG, F32))
        acc_ref[...] = jnp.zeros_like(acc_ref)

        def mix(t, row_sum):
            w = jnp.exp(s_ref[t] - row_max)
            acc_ref[...] += dot_nn(w.astype(BF16), load(kv_ref, 1, blocks_ref[a, t]))
            return row_sum + jnp.sum(w, axis=1, keepdims=True)

        row_sum = lax.fori_loop(0, count, mix, jnp.zeros((BLK, 1), F32))
        att = (acc_ref[...] / row_sum).astype(BF16)
        total = row_max + jnp.log(row_sum)
        grad_dot = jnp.sum(g.astype(F32) * att.astype(F32), axis=1, keepdims=True)

        def pair(t):
            block = blocks_ref[a, t]
            p = jnp.exp(s_ref[t] - total)
            dp = dot_nt(g, load(kv_ref, 1, block))
            return block, p, (p * (dp - grad_dot)).astype(BF16)

        def add_key(slot, p, ds):
            dk_acc[slot] += dot_tn(ds, q)
            dv_acc[slot] += dot_tn(p.astype(BF16), g)

        if local:
            acc_ref[...] = jnp.zeros_like(acc_ref)

            def back(t, carry):
                block, p, ds = pair(t)
                acc_ref[...] += dot_nn(ds, load(kv_ref, 0, block))
                slot = block - first

                @pl.when((slot >= 0) & (slot < 4))
                def _():
                    add_key(slot, p, ds)

                return carry

            lax.fori_loop(0, count, back, 0)
            rows = pl.ds(pl.multiple_of((a - first) * BLK, BLK), BLK)
            att_ref[rows, :] = att
            dq_ref[rows, :] = (acc_ref[...] * scale).astype(BF16)
        else:

            def back(t, carry):
                slot = blocks_ref[a, t] - first

                @pl.when((slot >= 0) & (slot < 4))
                def _():
                    _, p, ds = pair(t)
                    add_key(slot, p, ds)

                return carry

            lax.fori_loop(0, count, back, 0)

    def own(i, carry):
        query_block(first + i, True)
        return carry

    lax.fori_loop(0, 4, own, 0)

    def other(a, carry):
        @pl.when(touch_ref[a] > 0)
        def _():
            query_block(a, False)

        return carry

    lax.fori_loop(0, 128, other, 0)
    for slot in range(4):
        dk_ref[slot * BLK : (slot + 1) * BLK, :] = (dk_acc[slot] * scale).astype(BF16)
        dv_ref[slot * BLK : (slot + 1) * BLK, :] = dv_acc[slot].astype(BF16)


def attend(first, touch, key_blocks, counts, kv, qg):
    shape = jax.ShapeDtypeStruct((ROWS, HD), BF16)
    smem = pl.BlockSpec(memory_space=pltpu.SMEM)
    vmem = pl.BlockSpec(memory_space=pltpu.VMEM)
    return pl.pallas_call(
        attend_kernel,
        out_shape=(shape,) * 4,
        in_specs=[smem] * 4 + [vmem] * 2,
        out_specs=[vmem] * 4,
        scratch_shapes=[
            pltpu.VMEM((8, BLK, BLK), F32),
            pltpu.VMEM((BLK, HD), F32),
            pltpu.VMEM((4, BLK, HD), F32),
            pltpu.VMEM((4, BLK, HD), F32),
        ],
    )(first, touch, key_blocks, counts, kv, qg)


SLOTS = 26
LAG = 2
LATE = 6
CTL = 1024
AT_CODE = 64
AT_LAST = 96
AT_COUNT = 97
AT_USED = 100
AT_LIST = 128


def plan_kernel(mine_ref, used_ref, blocks_ref, counts_ref, ctl_ref, words_ref, words, where_kv, where_qg, sem):
    seq = lax.axis_index("seq")
    x, z = lax.rem(seq, NX), seq // NX
    lane = lax.broadcasted_iota(jnp.int32, (BLK, BLK), 1)
    count = counts_ref[...]
    hits = jnp.zeros((BLK, BLK), F32)
    for t in range(8):
        live = (blocks_ref[:, t : t + 1] == lane) & (count > t)
        hits = jnp.where(live, 1.0, hits)
    row = lax.broadcasted_iota(jnp.int32, (32, BLK), 0)
    col = lax.broadcasted_iota(jnp.int32, (32, BLK), 1)
    device = lax.rem(row, NZ) * NX + row // NZ
    group = jnp.where(col // 4 == device, 1.0, 0.0)
    need_kv = dot_nn(group, hits)
    need_qg = dot_nt(group, hits)
    jrow = lax.broadcasted_iota(jnp.int32, (8, BLK), 0)
    jcol = lax.broadcasted_iota(jnp.int32, (8, BLK), 1)
    mine = jcol - seq * 4
    power = jnp.where(mine == 0, 1.0, jnp.where(mine == 1, 2.0, jnp.where(mine == 2, 4.0, jnp.where(mine == 3, 8.0, 0.0))))
    bits = dot_nt(power, hits)

    origin = jcol // 16
    delta = lax.rem(jrow - origin + NZ, NZ)
    even = lax.rem(jcol, 2) == 0
    ahead = (delta >= 1) & ((delta < 4) | ((delta == 4) & even))
    behind = (delta > 4) | ((delta == 4) & jnp.logical_not(even))
    far = delta.astype(F32)
    ident = (127 - jcol).astype(F32)
    here = origin == jrow

    chains = []
    for sign in (1, -1):
        for column in range(NX):
            keys = []
            for need, base in ((need_kv, 128.0), (need_qg, 0.0)):
                part = need[column * NZ : (column + 1) * NZ, :] > 0.5
                hop = jnp.where(part & ahead, far, 0.0) if sign == 1 else jnp.where(part & behind, 8.0 - far, 0.0)
                most = jnp.max(hop, axis=0, keepdims=True)
                keys.append(jnp.where(here & (most > 0.5), most * 256.0 + base + ident, 0.0))
            chains.append(dict(sign=sign, keys=keys, sent=[], out=jnp.zeros((8, BLK), F32)))
    zero = jnp.zeros((8, BLK), F32)
    last = zero
    for t in range(SLOTS):
        for c in chains:
            if t >= LAG:
                before = c["sent"][t - LAG]
                passing = pltpu.roll(before, 1 if c["sign"] == 1 else 7, 0) - 256.0
                through = passing > 255.5
            best = c["keys"][0] if t < LATE else jnp.maximum(c["keys"][0], c["keys"][1])
            best = jnp.broadcast_to(jnp.max(best, axis=1, keepdims=True), (8, BLK))
            if t >= LAG:
                taken = jnp.where(through, -1.0, best)
                sent = jnp.where(through, passing, best)
                mark = jnp.where(through, -passing, best)
            else:
                taken, sent, mark = best, best, best
            c["keys"] = [jnp.where(k == taken, 0.0, k) for k in c["keys"]]
            c["sent"].append(sent)
            c["out"] = jnp.where(jcol == t, mark, c["out"])
    unfit = zero
    for c in chains:
        unfit = jnp.maximum(unfit, jnp.maximum(c["keys"][0], c["keys"][1]))
        for t in range(SLOTS - LAG, SLOTS):
            unfit = jnp.maximum(unfit, c["sent"][t] - 511.0)
    unfit = jnp.max(jnp.max(unfit, axis=1, keepdims=True), axis=0, keepdims=True)
    ours = []
    for half in range(2):
        pick = zero
        for column in range(NX):
            pick = jnp.where(x == column, chains[half * NX + column]["out"], pick)
        ours.append(pick)
    words_ref[0:8, :] = ours[0].astype(jnp.int32)
    words_ref[8:16, :] = ours[1].astype(jnp.int32)
    words_ref[16:24, :] = bits.astype(jnp.int32)
    words_ref[24:32, :] = jnp.broadcast_to(unfit, (8, BLK)).astype(jnp.int32)
    copy = pltpu.make_async_copy(words_ref, words, sem)
    copy.start()
    copy.wait()

    ctl_ref[AT_LAST] = words[24, 0]
    for i in range(4):
        ctl_ref[AT_USED + i] = used_ref[i]

    def clear(i, carry):
        where_kv[i] = 0
        where_qg[i] = 0
        return carry

    lax.fori_loop(0, BLK, clear, 0)
    for i in range(16):
        where_kv[z * 16 + i] = i
        where_qg[z * 16 + i] = i
    sources = (lax.rem(z + NZ - 1, NZ), lax.rem(z + 1, NZ))
    for half in range(2):

        def slot(t, carry):
            ctl_ref[half * SLOTS + t] = words[half * 8 + z, t]
            value = jnp.abs(words[half * 8 + sources[half], t])
            block = 127 - (value & 127)
            spot = 16 + half * SLOTS + t

            @pl.when((value >= 256) & ((value & 128) > 0))
            def _():
                where_kv[block] = spot

            @pl.when((value >= 256) & ((value & 128) == 0))
            def _():
                where_qg[block] = spot

            return carry

        lax.fori_loop(0, SLOTS, slot, 0)
    for i in range(4):
        for t in range(8):
            block = jnp.where(t < used_ref[i], mine_ref[i * 8 + t], seq * 4 + i)
            ctl_ref[AT_CODE + i * 8 + t] = where_kv[block]

    def entry(a, n):
        mask = words[16, a]

        @pl.when(mask > 0)
        def _():
            ctl_ref[AT_LIST + 4 * n] = a
            ctl_ref[AT_LIST + 4 * n + 1] = where_qg[a]
            ctl_ref[AT_LIST + 4 * n + 2] = mask

        return n + jnp.where(mask > 0, 1, 0)

    ctl_ref[AT_COUNT] = lax.fori_loop(0, BLK, entry, 0)


def make_plan(mine, used, key_blocks, counts):
    smem = pl.BlockSpec(memory_space=pltpu.SMEM)
    vmem = pl.BlockSpec(memory_space=pltpu.VMEM)
    return pl.pallas_call(
        plan_kernel,
        out_shape=jax.ShapeDtypeStruct((CTL,), jnp.int32),
        in_specs=[smem, smem, vmem, vmem],
        out_specs=smem,
        scratch_shapes=[
            pltpu.VMEM((32, BLK), jnp.int32),
            pltpu.SMEM((32, BLK), jnp.int32),
            pltpu.SMEM((BLK,), jnp.int32),
            pltpu.SMEM((BLK,), jnp.int32),
            pltpu.SemaphoreType.DMA,
        ],
    )(mine, used, key_blocks, counts)


def pick(cond, a, b):
    return lax.select(cond, a, b)


def route_kernel(
    ctl_ref, q_ref, k_ref, v_ref, g_ref,
    att_ref, dq_ref, kv_ref, qg_ref, recv_ref, stats_ref,
    send_ref, kcat, vcat, mine_stats,
    head_send, head_recv, own_sem, x_send, x_recv, z_send, z_recv, s_send, s_recv,
):
    seq = lax.axis_index("seq")
    head = lax.axis_index("head")
    x, z = lax.rem(seq, NX), seq // NX

    def chip(cx, cz):
        return lax.rem(cz + 2 * NZ, NZ) * NX + lax.rem(cx + 2 * NX, NX)

    barrier = pltpu.get_barrier_semaphore()
    for shift in range(1, NH):
        pl.semaphore_signal(barrier, inc=1, device_id={"seq": seq, "head": lax.rem(head + shift, NH)}, device_id_type=MESH)
    for shift in range(1, NX * NZ):
        pl.semaphore_signal(barrier, inc=1, device_id={"seq": lax.rem(seq + shift, NX * NZ), "head": head}, device_id_type=MESH)
    pl.semaphore_wait(barrier, NH - 1 + NX * NZ - 1)

    targets = ((k_ref, kv_ref, 0), (v_ref, kv_ref, 1), (q_ref, qg_ref, 0), (g_ref, qg_ref, 1))

    def rows_of(dst, which, h):
        start = pl.multiple_of(which * BLK + lax.rem(h, 2) * CHUNK, CHUNK)
        return dst.at[4 * x + h // 2, pl.ds(start, CHUNK), :]

    def columns_of(src, h):
        return src.at[:, pl.ds(pl.multiple_of(h * HD, HD), HD)]

    def head_copy(array, peer_from, peer_to, shift):
        src, dst, which = targets[array]
        return pltpu.make_async_remote_copy(
            src_ref=columns_of(src, peer_to),
            dst_ref=rows_of(dst, which, peer_from),
            send_sem=head_send.at[array, shift],
            recv_sem=head_recv.at[array, shift],
            device_id={"seq": seq, "head": peer_to},
            device_id_type=MESH,
        )

    started = []
    own_copies = []
    for array, (src, dst, which) in enumerate(targets):
        for shift in range(1, NH):
            copy = head_copy(array, head, lax.rem(head + shift, NH), shift)
            copy.start()
            started.append(copy)
        own = pltpu.make_async_copy(columns_of(src, head), rows_of(dst, which, head), own_sem.at[array])
        own.start()
        own_copies.append(own)

    def wait_head(array):
        for shift in range(1, NH):
            peer = lax.rem(head + NH - shift, NH)
            head_copy(array, peer, peer, shift).wait_recv()
        own_copies[array].wait()

    rows = (kv_ref, qg_ref)
    x_plan = ((1, 0, 0), (-1, 0, 2), (1, 0, 2), (-1, 0, 0), (1, 1, 0), (-1, -1, 2))

    def x_copy(kind, i, arriving):
        sign, offset, first = x_plan[i]
        origin = lax.rem(x - offset - (sign if arriving else 0) + 2 * NX, NX)
        piece = rows[kind].at[pl.ds(4 * origin + first, 2)]
        other = chip(x - sign, z) if arriving else chip(x + sign, z)
        return pltpu.make_async_remote_copy(
            src_ref=piece, dst_ref=piece, send_sem=x_send.at[kind, i], recv_sem=x_recv.at[kind, i],
            device_id={"seq": other, "head": head}, device_id_type=MESH,
        )

    def x_start(kind, i):
        copy = x_copy(kind, i, False)
        copy.start()
        started.append(copy)

    def z_copy(half, t, arriving):
        sign = 1 if half == 0 else -1
        other = chip(x, z - sign) if arriving else chip(x, z + sign)
        slot = half * SLOTS + t
        return pltpu.make_async_remote_copy(
            src_ref=send_ref.at[slot], dst_ref=recv_ref.at[slot], send_sem=z_send.at[slot], recv_sem=z_recv.at[slot],
            device_id={"seq": other, "head": head}, device_id_type=MESH,
        )

    wait_head(0)
    wait_head(1)
    for i in range(4):
        x_start(0, i)
    wait_head(2)
    wait_head(3)
    x_copy(0, 0, True).wait_recv()
    x_start(0, 4)
    x_copy(0, 1, True).wait_recv()
    x_start(0, 5)
    for i in range(4):
        x_start(1, i)
    for i in range(2, 6):
        x_copy(0, i, True).wait_recv()

    for t in range(SLOTS):
        if t == 2:
            x_copy(1, 0, True).wait_recv()
            x_start(1, 4)
            x_copy(1, 1, True).wait_recv()
            x_start(1, 5)
        if t == LATE:
            for i in range(2, 6):
                x_copy(1, i, True).wait_recv()
        for half in range(2):
            slot = half * SLOTS + t
            value = ctl_ref[slot]
            size = jnp.abs(value)
            index = (127 - (size & 127)) & 15
            data = kv_ref[index]
            if t >= LATE:
                data = pick((size & 128) > 0, data, qg_ref[index])
            if t >= LAG:
                z_copy(half, t - LAG, True).wait_recv()
                data = pick(value < 0, recv_ref[slot - LAG], data)
            send_ref[slot] = data
        for half in range(2):
            copy = z_copy(half, t, False)
            copy.start()
            started.append(copy)
    for t in range(SLOTS - LAG, SLOTS):
        for half in range(2):
            z_copy(half, t, True).wait_recv()

    scale = 1.0 / math.sqrt(HD)
    key_at = lax.broadcasted_iota(jnp.int32, (BLK, 8 * BLK), 1)

    def query_block(i, carry):
        for t in range(8):
            code = ctl_ref[AT_CODE + i * 8 + t]
            near = kv_ref[jnp.minimum(code, 15)]
            moved = recv_ref[jnp.maximum(code - 16, 0)]
            data = pick(code < 16, near, moved)
            kcat[t * BLK : (t + 1) * BLK, :] = data[0:BLK]
            vcat[t * BLK : (t + 1) * BLK, :] = data[BLK : 2 * BLK]
        own = qg_ref[4 * x + i]
        q, g = own[0:BLK], own[BLK : 2 * BLK]
        s = dot_nt(q, kcat[...]) * scale
        s = jnp.where(key_at < ctl_ref[AT_USED + i] * BLK, s, NEG)
        row_max = jnp.max(s, axis=1, keepdims=True)
        w = jnp.exp(s - row_max)
        row_sum = jnp.sum(w, axis=1, keepdims=True)
        att = (dot_nn(w.astype(BF16), vcat[...]) / row_sum).astype(BF16)
        total = row_max + jnp.log(row_sum)
        grad_dot = jnp.sum(g.astype(F32) * att.astype(F32), axis=1, keepdims=True)
        p = jnp.exp(s - total)
        ds = (p * (dot_nt(g, vcat[...]) - grad_dot)).astype(BF16)
        at = pl.ds(pl.multiple_of(i * BLK, BLK), BLK)
        att_ref[at, :] = att
        dq_ref[at, :] = (dot_nn(ds, kcat[...]) * scale).astype(BF16)
        mine_stats[pl.ds(i, 1), :] = jnp.transpose(jnp.broadcast_to(total, (BLK, BLK)))[0:1, :]
        mine_stats[pl.ds(i + 4, 1), :] = jnp.transpose(jnp.broadcast_to(grad_dot, (BLK, BLK)))[0:1, :]
        return carry

    lax.fori_loop(0, 4, query_block, 0)

    def stat_copy(shift, origin, target):
        return pltpu.make_async_remote_copy(
            src_ref=mine_stats, dst_ref=stats_ref.at[origin], send_sem=s_send.at[shift], recv_sem=s_recv.at[shift],
            device_id={"seq": target, "head": head}, device_id_type=MESH,
        )

    for shift in range(1, NX * NZ):
        copy = stat_copy(shift, seq, lax.rem(seq + shift, NX * NZ))
        copy.start()
        started.append(copy)
    own = pltpu.make_async_copy(mine_stats, stats_ref.at[seq], s_recv.at[0])
    own.start()
    for shift in range(1, NX * NZ):
        peer = lax.rem(seq + NX * NZ - shift, NX * NZ)
        stat_copy(shift, peer, peer).wait_recv()
    own.wait()
    for copy in started:
        copy.wait_send()


def route(ctl, queries, keys, values, out_grad):
    smem = pl.BlockSpec(memory_space=pltpu.SMEM)
    vmem = pl.BlockSpec(memory_space=pltpu.VMEM)
    out = jax.ShapeDtypeStruct((ROWS, HD), BF16)
    near = jax.ShapeDtypeStruct((16, 2 * BLK, HD), BF16)
    moved = jax.ShapeDtypeStruct((2 * SLOTS, 2 * BLK, HD), BF16)
    stats = jax.ShapeDtypeStruct((NX * NZ, 8, BLK), F32)
    dma = pltpu.SemaphoreType.DMA
    return pl.pallas_call(
        route_kernel,
        out_shape=(out, out, near, near, moved, stats),
        in_specs=[smem] + [vmem] * 4,
        out_specs=[vmem] * 6,
        scratch_shapes=[
            pltpu.VMEM((2 * SLOTS, 2 * BLK, HD), BF16),
            pltpu.VMEM((8 * BLK, HD), BF16),
            pltpu.VMEM((8 * BLK, HD), BF16),
            pltpu.VMEM((8, BLK), F32),
            dma((4, NH)), dma((4, NH)), dma((4,)),
            dma((2, 6)), dma((2, 6)),
            dma((2 * SLOTS,)), dma((2 * SLOTS,)),
            dma((NX * NZ,)), dma((NX * NZ,)),
        ],
        compiler_params=pltpu.CompilerParams(collective_id=1, has_side_effects=True),
    )(ctl, queries, keys, values, out_grad)


def keys_kernel(ctl_ref, kv_ref, qg_ref, recv_ref, stats_ref, dk_ref, dv_ref, now, dk_acc, dv_acc):
    scale = 1.0 / math.sqrt(HD)
    x = lax.rem(lax.axis_index("seq"), NX)
    dk_acc[...] = jnp.zeros_like(dk_acc)
    dv_acc[...] = jnp.zeros_like(dv_acc)

    def entry(n, carry):
        a = ctl_ref[AT_LIST + 4 * n]
        code = ctl_ref[AT_LIST + 4 * n + 1]
        mask = ctl_ref[AT_LIST + 4 * n + 2]

        @pl.when(code < 16)
        def _():
            now[...] = qg_ref[code]

        @pl.when(code >= 16)
        def _():
            now[...] = recv_ref[code - 16]

        q, g = now[0:BLK, :], now[BLK : 2 * BLK, :]
        total = stats_ref[a // 4, pl.ds(lax.rem(a, 4), 1), :]
        grad_dot = stats_ref[a // 4, pl.ds(lax.rem(a, 4) + 4, 1), :]
        for j in range(4):

            @pl.when((mask & (1 << j)) > 0)
            def _():
                k = kv_ref[4 * x + j, 0:BLK, :]
                v = kv_ref[4 * x + j, BLK : 2 * BLK, :]
                p = jnp.exp(dot_nt(k, q) * scale - total)
                ds = (p * (dot_nt(v, g) - grad_dot)).astype(BF16)
                dk_acc[j] += dot_nn(ds, q)
                dv_acc[j] += dot_nn(p.astype(BF16), g)

        return carry

    lax.fori_loop(0, ctl_ref[AT_COUNT], entry, 0)
    for j in range(4):
        dk_ref[j * BLK : (j + 1) * BLK, :] = (dk_acc[j] * scale).astype(BF16)
        dv_ref[j * BLK : (j + 1) * BLK, :] = dv_acc[j].astype(BF16)


def key_grads(ctl, kv, qg, recv, stats):
    smem = pl.BlockSpec(memory_space=pltpu.SMEM)
    vmem = pl.BlockSpec(memory_space=pltpu.VMEM)
    out = jax.ShapeDtypeStruct((ROWS, HD), BF16)
    return pl.pallas_call(
        keys_kernel,
        out_shape=(out, out),
        in_specs=[smem] + [vmem] * 4,
        out_specs=[vmem] * 2,
        scratch_shapes=[
            pltpu.VMEM((2 * BLK, HD), BF16),
            pltpu.VMEM((4, BLK, HD), F32),
            pltpu.VMEM((4, BLK, HD), F32),
        ],
    )(ctl, kv, qg, recv, stats)


def on_device(queries, keys, values, out_grad, key_blocks, counts):
    seq = lax.axis_index("seq")
    mine = lax.dynamic_slice_in_dim(key_blocks, 4 * seq, 4, 0).reshape(32)
    used = lax.dynamic_slice_in_dim(counts, 4 * seq, 4, 0)
    ctl = make_plan(mine, used, key_blocks, counts[:, None])

    def sparse(_):
        att, dq, kv, qg, recv, stats = route(ctl, queries, keys, values, out_grad)
        dk, dv = key_grads(ctl, kv, qg, recv, stats)
        return att, dq, dk, dv

    def dense(_):
        kv, qg = exchange(queries, keys, values, out_grad)
        live = jnp.arange(key_blocks.shape[1])[None, :] < counts[:, None]
        touch = jnp.any(live & (key_blocks // 4 == seq), axis=1)
        touch = (touch & (jnp.arange(key_blocks.shape[0]) // 4 != seq)).astype(jnp.int32)
        first = (seq * 4).reshape(1).astype(jnp.int32)
        return tuple(attend(first, touch, key_blocks, counts, kv, qg))

    return lax.cond(ctl[AT_LAST] <= 0, sparse, dense, 0)


def solution(mesh):
    rows = P(("seq", "head"), None)
    out = P("seq", "head")
    return jax.shard_map(
        on_device,
        mesh=mesh,
        in_specs=(rows,) * 4 + (P(), P()),
        out_specs=(out,) * 4,
        check_vma=False,
    )
```

```python
import functools
import heapq
import math

import jax
import jax.numpy as jnp
from jax import lax
from jax.experimental import pallas as pl
from jax.experimental.pallas import tpu as pltpu
from jax.sharding import PartitionSpec as P

MESH = pl.DeviceIdType.MESH
BLK = 128
HD = 128
NX = 4
NZ = 8
NH = 8
ROWS = 512
CHUNK = 64
SPLIT = 208
BF16 = jnp.bfloat16
F32 = jnp.float32
NEG = -1e30


def row_range(part):
    half_a, half_b = SPLIT // 32 * 16, SPLIT + (ROWS - SPLIT) // 32 * 16
    return {
        "A": (0, SPLIT),
        "A0": (0, half_a),
        "A1": (half_a, SPLIT),
        "B": (SPLIT, ROWS),
        "B0": (SPLIT, half_b),
        "B1": (half_b, ROWS),
    }[part]


def ring_sends(axis, sources, size, out, kind, prio):
    far = size // 2
    arrived = []
    for (offset, part, dep) in sources:
        if len(part) == 1:
            arrived.append((offset, part, dep))
            halves = [(part, +1, far - 1), (part, -1, far - 1)]
        else:
            arrived.append((offset, part, dep))
            sign = +1 if part[1] == "0" else -1
            halves = [(part, +1, far - 1), (part, -1, far - 1)]
        for (piece, sign, hops) in halves:
            last = dep
            at = offset
            for hop in range(1, hops + 1):
                out.append(dict(kind=kind, axis=axis, sign=sign, origin=at, part=piece, dep=last, left=far - hop, prio=prio))
                last = len(out) - 1
                at = step_offset(at, axis, sign)
                arrived.append((at, piece, last))
            for digit, way in (("0", +1), ("1", -1)):
                if way != sign:
                    continue
                tail = piece if len(piece) == 2 else piece + digit
                if tail[1] != digit:
                    continue
                out.append(dict(kind=kind, axis=axis, sign=sign, origin=at, part=tail, dep=last, left=0, prio=prio))
                arrived.append((step_offset(at, axis, sign), tail, len(out) - 1))
    return arrived


def step_offset(offset, axis, sign):
    ox, oz = offset
    return (ox + sign, oz) if axis == "x" else (ox, oz + sign)


def plan_sends():
    out = []
    for kind in (0, 1):
        own = -1 - kind
        first_a = ring_sends("x", [((0, 0), "A", own)], NX, out, kind, kind * 10)
        first_b = ring_sends("z", [((0, 0), "B", own)], NZ, out, kind, kind * 10)
        ring_sends("z", first_a, NZ, out, kind, kind * 10 + 1)
        ring_sends("x", first_b, NX, out, kind, kind * 10 + 1)
    rate = 46.0e3 * 1.0
    latency = 1.7
    ready_own = {-1: 4.0, -2: 8.0}
    arrival = {}
    free = {}
    start = {}
    waiting = {}
    events = []
    for i, m in enumerate(out):
        if m["dep"] < 0:
            heapq.heappush(events, (ready_own[m["dep"]], i))
    children = {}
    for i, m in enumerate(out):
        if m["dep"] >= 0:
            children.setdefault(m["dep"], []).append(i)
    queues = {("x", 1): [], ("x", -1): [], ("z", 1): [], ("z", -1): []}
    free = {k: 0.0 for k in queues}
    order = []
    while events or any(queues.values()):
        options = []
        for k, q in queues.items():
            if q:
                options.append((max(free[k], q[0][2]), k))
        next_link = min(options) if options else None
        if events and (next_link is None or events[0][0] <= next_link[0]):
            t, i = heapq.heappop(events)
            m = out[i]
            q = queues[(m["axis"], m["sign"])]
            q.append((m["prio"] // 10, -m["left"], t, i))
            q.sort(key=lambda e: (e[0], e[1], e[2], e[3]))
            continue
        t, k = next_link
        _, _, ready, i = queues[k].pop(0)
        m = out[i]
        lo, hi = row_range(m["part"])
        begin = max(free[k], ready)
        free[k] = begin + (hi - lo) * HD * 2 * 2 / rate
        start[i] = begin
        order.append((begin, ready, i))
        for c in children.get(i, []):
            heapq.heappush(events, (free[k] + latency, c))
    order.sort()
    return out, [i for (_, _, i) in order], max(free.values())


SENDS, ORDER, SPAN = plan_sends()


def exchange_kernel(q_ref, k_ref, v_ref, g_ref, kv_ref, qg_ref, send_sem, recv_sem, head_send, head_recv, own_sem):
    seq = lax.axis_index("seq")
    head = lax.axis_index("head")
    x, z = lax.rem(seq, NX), seq // NX

    def chip(cx, cz):
        return lax.rem(cz + 2 * NZ, NZ) * NX + lax.rem(cx + 2 * NX, NX)

    barrier = pltpu.get_barrier_semaphore()
    for shift in range(1, NH):
        pl.semaphore_signal(barrier, inc=1, device_id={"seq": seq, "head": lax.rem(head + shift, NH)}, device_id_type=MESH)
    for (cx, cz) in ((x + 1, z), (x - 1, z), (x, z + 1), (x, z - 1)):
        pl.semaphore_signal(barrier, inc=1, device_id={"seq": chip(cx, cz), "head": head}, device_id_type=MESH)
    pl.semaphore_wait(barrier, NH - 1 + 4)

    targets = ((k_ref, kv_ref, 0), (v_ref, kv_ref, 1), (q_ref, qg_ref, 0), (g_ref, qg_ref, 1))

    def rows_of(dst, which, h):
        return dst.at[seq, which, pl.ds(pl.multiple_of(h * CHUNK, CHUNK), CHUNK), :]

    def columns_of(src, h):
        return src.at[:, pl.ds(pl.multiple_of(h * HD, HD), HD)]

    head_copies = []
    own_copies = []
    for array, (src, dst, which) in enumerate(targets):
        for shift in range(1, NH):
            peer = lax.rem(head + shift, NH)
            copy = pltpu.make_async_remote_copy(
                src_ref=columns_of(src, peer),
                dst_ref=rows_of(dst, which, head),
                send_sem=head_send.at[array, shift],
                recv_sem=head_recv.at[array, shift],
                device_id={"seq": seq, "head": peer},
                device_id_type=MESH,
            )
            copy.start()
            head_copies.append(copy)
        own = pltpu.make_async_copy(columns_of(src, head), rows_of(dst, which, head), own_sem.at[array])
        own.start()
        own_copies.append(own)

    def wait_head(array):
        src, dst, which = targets[array]
        for shift in range(1, NH):
            peer = lax.rem(head + NH - shift, NH)
            pltpu.make_async_remote_copy(
                src_ref=columns_of(src, peer),
                dst_ref=rows_of(dst, which, peer),
                send_sem=head_send.at[array, shift],
                recv_sem=head_recv.at[array, shift],
                device_id={"seq": seq, "head": peer},
                device_id_type=MESH,
            ).wait_recv()
        own_copies[array].wait()

    buffers = (kv_ref, qg_ref)

    def piece(m, ox, oz):
        lo, hi = row_range(m["part"])
        return buffers[m["kind"]].at[chip(x - ox, z - oz), :, lo:hi, :]

    def send(i):
        m = SENDS[i]
        ox, oz = m["origin"]
        target = chip(x + m["sign"], z) if m["axis"] == "x" else chip(x, z + m["sign"])
        return pltpu.make_async_remote_copy(
            src_ref=piece(m, ox, oz),
            dst_ref=piece(m, ox, oz),
            send_sem=send_sem.at[i],
            recv_sem=recv_sem.at[i],
            device_id={"seq": target, "head": head},
            device_id_type=MESH,
        )

    def wait_recv(i):
        m = SENDS[i]
        ox, oz = step_offset(m["origin"], m["axis"], m["sign"])
        source = chip(x - m["sign"], z) if m["axis"] == "x" else chip(x, z - m["sign"])
        pltpu.make_async_remote_copy(
            src_ref=piece(m, ox, oz),
            dst_ref=piece(m, ox, oz),
            send_sem=send_sem.at[i],
            recv_sem=recv_sem.at[i],
            device_id={"seq": source, "head": head},
            device_id_type=MESH,
        ).wait_recv()

    ready = set()
    started = []
    for i in ORDER:
        dep = SENDS[i]["dep"]
        if dep not in ready:
            ready.add(dep)
            if dep < 0:
                wait_head(2 * (-1 - dep))
                wait_head(2 * (-1 - dep) + 1)
            else:
                wait_recv(dep)
        copy = send(i)
        copy.start()
        started.append(copy)
    for i in ORDER:
        if i not in ready:
            wait_recv(i)
    for copy in started:
        copy.wait_send()
    for copy in head_copies:
        copy.wait_send()


def exchange(queries, keys, values, out_grad):
    shape = jax.ShapeDtypeStruct((NX * NZ, 2, ROWS, HD), BF16)
    count = len(SENDS)
    return pl.pallas_call(
        exchange_kernel,
        out_shape=(shape, shape),
        in_specs=[pl.BlockSpec(memory_space=pltpu.VMEM)] * 4,
        out_specs=[pl.BlockSpec(memory_space=pl.ANY)] * 2,
        scratch_shapes=[
            pltpu.SemaphoreType.DMA((count,)),
            pltpu.SemaphoreType.DMA((count,)),
            pltpu.SemaphoreType.DMA((4, NH)),
            pltpu.SemaphoreType.DMA((4, NH)),
            pltpu.SemaphoreType.DMA((4,)),
        ],
        compiler_params=pltpu.CompilerParams(collective_id=0, has_side_effects=True),
    )(queries, keys, values, out_grad)


def dot_nt(a, b):
    return lax.dot_general(a, b, (((1,), (1,)), ((), ())), preferred_element_type=F32)


def dot_nn(a, b):
    return lax.dot_general(a, b, (((1,), (0,)), ((), ())), preferred_element_type=F32)


def dot_tn(a, b):
    return lax.dot_general(a, b, (((0,), (0,)), ((), ())), preferred_element_type=F32)


def attend_kernel(first_ref, touch_ref, blocks_ref, counts_ref, kv_ref, qg_ref, att_ref, dq_ref, dk_ref, dv_ref, s_ref, acc_ref, dk_acc, dv_acc):
    scale = 1.0 / math.sqrt(HD)
    dk_acc[...] = jnp.zeros_like(dk_acc)
    dv_acc[...] = jnp.zeros_like(dv_acc)
    first = first_ref[0]

    def load(ref, which, block):
        return ref[block // 4, which, pl.ds(pl.multiple_of(lax.rem(block, 4) * BLK, BLK), BLK), :]

    def query_block(a, local):
        count = counts_ref[a]
        q = load(qg_ref, 0, a)
        g = load(qg_ref, 1, a)

        def score(t, row_max):
            s = dot_nt(q, load(kv_ref, 0, blocks_ref[a, t])) * scale
            s_ref[t] = s
            return jnp.maximum(row_max, jnp.max(s, axis=1, keepdims=True))

        row_max = lax.fori_loop(0, count, score, jnp.full((BLK, 1), NEG, F32))
        acc_ref[...] = jnp.zeros_like(acc_ref)

        def mix(t, row_sum):
            w = jnp.exp(s_ref[t] - row_max)
            acc_ref[...] += dot_nn(w.astype(BF16), load(kv_ref, 1, blocks_ref[a, t]))
            return row_sum + jnp.sum(w, axis=1, keepdims=True)

        row_sum = lax.fori_loop(0, count, mix, jnp.zeros((BLK, 1), F32))
        att = (acc_ref[...] / row_sum).astype(BF16)
        total = row_max + jnp.log(row_sum)
        grad_dot = jnp.sum(g.astype(F32) * att.astype(F32), axis=1, keepdims=True)

        def pair(t):
            block = blocks_ref[a, t]
            p = jnp.exp(s_ref[t] - total)
            dp = dot_nt(g, load(kv_ref, 1, block))
            return block, p, (p * (dp - grad_dot)).astype(BF16)

        def add_key(slot, p, ds):
            dk_acc[slot] += dot_tn(ds, q)
            dv_acc[slot] += dot_tn(p.astype(BF16), g)

        if local:
            acc_ref[...] = jnp.zeros_like(acc_ref)

            def back(t, carry):
                block, p, ds = pair(t)
                acc_ref[...] += dot_nn(ds, load(kv_ref, 0, block))
                slot = block - first

                @pl.when((slot >= 0) & (slot < 4))
                def _():
                    add_key(slot, p, ds)

                return carry

            lax.fori_loop(0, count, back, 0)
            rows = pl.ds(pl.multiple_of((a - first) * BLK, BLK), BLK)
            att_ref[rows, :] = att
            dq_ref[rows, :] = (acc_ref[...] * scale).astype(BF16)
        else:

            def back(t, carry):
                slot = blocks_ref[a, t] - first

                @pl.when((slot >= 0) & (slot < 4))
                def _():
                    _, p, ds = pair(t)
                    add_key(slot, p, ds)

                return carry

            lax.fori_loop(0, count, back, 0)

    def own(i, carry):
        query_block(first + i, True)
        return carry

    lax.fori_loop(0, 4, own, 0)

    def other(a, carry):
        @pl.when(touch_ref[a] > 0)
        def _():
            query_block(a, False)

        return carry

    lax.fori_loop(0, 128, other, 0)
    for slot in range(4):
        dk_ref[slot * BLK : (slot + 1) * BLK, :] = (dk_acc[slot] * scale).astype(BF16)
        dv_ref[slot * BLK : (slot + 1) * BLK, :] = dv_acc[slot].astype(BF16)


def attend(first, touch, key_blocks, counts, kv, qg):
    shape = jax.ShapeDtypeStruct((ROWS, HD), BF16)
    smem = pl.BlockSpec(memory_space=pltpu.SMEM)
    vmem = pl.BlockSpec(memory_space=pltpu.VMEM)
    return pl.pallas_call(
        attend_kernel,
        out_shape=(shape,) * 4,
        in_specs=[smem] * 4 + [vmem] * 2,
        out_specs=[vmem] * 4,
        scratch_shapes=[
            pltpu.VMEM((8, BLK, BLK), F32),
            pltpu.VMEM((BLK, HD), F32),
            pltpu.VMEM((4, BLK, HD), F32),
            pltpu.VMEM((4, BLK, HD), F32),
        ],
    )(first, touch, key_blocks, counts, kv, qg)


LAG = 2
STEPS = 32
VARIANTS = ((27, 22), (32, 27))
OWN_QG = 4
PASS_KV = 4
ALL_KV = 8
PASS_QG = 10
ALL_QG = 14
CTL = 1024
AT_CODE = 128
AT_PICK = 160
AT_COUNT = 161
AT_USED = 164
AT_LIST = 256


def plan_kernel(blocks_ref, counts_ref, ctl_ref, words_ref, words, where_kv, where_qg, sem):
    seq = lax.axis_index("seq")
    x, z = lax.rem(seq, NX), seq // NX
    brow = lax.broadcasted_iota(jnp.int32, (BLK, BLK), 0)
    count = counts_ref[...]
    hits = jnp.zeros((BLK, BLK), F32)
    for t in range(8):
        hits = jnp.where((blocks_ref[t : t + 1, :] == brow) & (count > t), 1.0, hits)
    row = lax.broadcasted_iota(jnp.int32, (32, BLK), 0)
    col = lax.broadcasted_iota(jnp.int32, (32, BLK), 1)
    device = lax.rem(row, NZ) * NX + row // NZ
    group = jnp.where(col // 4 == device, 1.0, 0.0)
    need_kv = dot_nt(group, hits)
    need_qg = dot_nn(group, hits)
    jrow = lax.broadcasted_iota(jnp.int32, (8, BLK), 0)
    jcol = lax.broadcasted_iota(jnp.int32, (8, BLK), 1)
    mine = jcol - seq * 4
    power = jnp.where(mine == 0, 1.0, jnp.where(mine == 1, 2.0, jnp.where(mine == 2, 4.0, jnp.where(mine == 3, 8.0, 0.0))))
    bits = dot_nn(power, hits)

    origin = jcol // 16
    source_x = lax.rem(jcol, 16) // 4
    delta = lax.rem(jrow - origin + NZ, NZ)
    near = (delta >= 1) & (delta < 4)
    back = delta > 4
    tie = delta == 4
    far = delta.astype(F32)
    ident = (127 - jcol).astype(F32)
    here = origin == jrow

    chains = []
    for column in range(NX):
        parts = [need[column * NZ : (column + 1) * NZ, :] > 0.5 for need in (need_kv, need_qg)]
        lean = jnp.zeros((8, BLK), F32)
        for part in parts:
            lean = lean + jnp.where(part & near, 1.0, 0.0) - jnp.where(part & back, 1.0, 0.0)
        lean = jnp.broadcast_to(jnp.sum(lean, axis=1, keepdims=True), (8, BLK))
        ahead = near | (tie & (lean < 0.0))
        behind = back | (tie & (lean >= 0.0))
        for sign in (1, -1):
            keys = []
            for part, base in zip(parts, (2048.0, 0.0)):
                hop = jnp.where(part & ahead, far, 0.0) if sign == 1 else jnp.where(part & behind, 8.0 - far, 0.0)
                most = jnp.max(hop, axis=0, keepdims=True)
                keys.append(jnp.where(here & (most > 0.5), most * 128.0 + base + ident, 0.0))
            chains.append(dict(sign=sign, column=column, keys=keys, sent=[]))
    zero = jnp.zeros((8, BLK), F32)
    last_any, last_kv = zero, zero
    marks = [zero, zero]
    ours = [x == column for column in range(NX)]
    for t in range(STEPS):
        chosen = [zero, zero]
        for c in chains:
            own = source_x == c["column"]
            if t >= LAG:
                passing = pltpu.roll(c["sent"][t - LAG], 1 if c["sign"] == 1 else 7, 0) - 128.0
                left = jnp.where(passing >= 2048.0, passing - 2048.0, passing)
                through = left > 127.5
            kv, qg = c["keys"]
            best = jnp.where(own, kv, 0.0) if t < ALL_KV else kv
            if t >= OWN_QG:
                best = jnp.maximum(best, jnp.where(own, qg, 0.0) if t < ALL_QG else qg)
            best = jnp.broadcast_to(jnp.max(best, axis=1, keepdims=True), (8, BLK))
            if t >= LAG:
                taken = jnp.where(through, -1.0, best)
                sent = jnp.where(through, passing, best)
                mark = jnp.where(through, -passing, best)
            else:
                taken, sent, mark = best, best, best
            c["keys"] = [jnp.where(k == taken, 0.0, k) for k in c["keys"]]
            c["sent"].append(sent)
            last_any = jnp.where(sent > 0.0, t + 1.0, last_any)
            last_kv = jnp.where(sent >= 2048.0, t + 1.0, last_kv)
            half = 0 if c["sign"] == 1 else 1
            chosen[half] = jnp.where(ours[c["column"]], mark, chosen[half])
        for half in range(2):
            marks[half] = jnp.where(jcol == t, chosen[half], marks[half])
    for c in chains:
        last_any = jnp.where((c["keys"][0] + c["keys"][1]) > 0.0, 999.0, last_any)
        for t in range(STEPS - LAG, STEPS):
            sent = c["sent"][t]
            left = jnp.where(sent >= 2048.0, sent - 2048.0, sent)
            last_any = jnp.where(left > 255.5, 999.0, last_any)
    last_any = jnp.max(jnp.max(last_any, axis=1, keepdims=True), axis=0, keepdims=True)
    last_kv = jnp.max(jnp.max(last_kv, axis=1, keepdims=True), axis=0, keepdims=True)
    index = jnp.zeros((1, 1), F32)
    for steps, kv_steps in VARIANTS:
        index = index + jnp.where((last_any > steps + 0.5) | (last_kv > kv_steps + 0.5), 1.0, 0.0)
    words_ref[0:8, :] = marks[0].astype(jnp.int32)
    words_ref[8:16, :] = marks[1].astype(jnp.int32)
    words_ref[16:24, :] = bits.astype(jnp.int32)
    words_ref[24:32, :] = blocks_ref[...]
    words_ref[32:40, :] = jnp.broadcast_to(count, (8, BLK))
    words_ref[40:48, :] = jnp.broadcast_to(index, (8, BLK)).astype(jnp.int32)
    copy = pltpu.make_async_copy(words_ref, words, sem)
    copy.start()
    copy.wait()

    ctl_ref[AT_PICK] = words[40, 0]
    for i in range(16):
        where_kv[z * 16 + i] = i
        where_qg[z * 16 + i] = i
    sources = (lax.rem(z + NZ - 1, NZ), lax.rem(z + 1, NZ))

    def slot(t, carry):
        for half in range(2):
            ctl_ref[2 * t + half] = words[half * 8 + z, t]
            value = jnp.abs(words[half * 8 + sources[half], t])
            block = 127 - (value & 127)
            spot = 16 + 2 * t + half

            @pl.when(value >= 2048)
            def _():
                where_kv[block] = spot

            @pl.when((value >= 128) & (value < 2048))
            def _():
                where_qg[block] = spot

        return carry

    lax.fori_loop(0, STEPS, slot, 0)
    for i in range(4):
        live = words[32, 4 * seq + i]
        ctl_ref[AT_USED + i] = live
        for t in range(8):
            block = jnp.where(t < live, words[24 + t, 4 * seq + i], 4 * seq + i)
            ctl_ref[AT_CODE + i * 8 + t] = where_kv[block]

    def entry(a, n):
        mask = words[16, a]

        @pl.when(mask > 0)
        def _():
            ctl_ref[AT_LIST + 4 * n] = a
            ctl_ref[AT_LIST + 4 * n + 1] = where_qg[a]
            ctl_ref[AT_LIST + 4 * n + 2] = mask

        return n + jnp.where(mask > 0, 1, 0)

    ctl_ref[AT_COUNT] = lax.fori_loop(0, BLK, entry, 0)


def make_plan(key_blocks, counts):
    vmem = pl.BlockSpec(memory_space=pltpu.VMEM)
    return pl.pallas_call(
        plan_kernel,
        out_shape=jax.ShapeDtypeStruct((CTL,), jnp.int32),
        in_specs=[vmem, vmem],
        out_specs=pl.BlockSpec(memory_space=pltpu.SMEM),
        scratch_shapes=[
            pltpu.VMEM((48, BLK), jnp.int32),
            pltpu.SMEM((48, BLK), jnp.int32),
            pltpu.SMEM((BLK,), jnp.int32),
            pltpu.SMEM((BLK,), jnp.int32),
            pltpu.SemaphoreType.DMA,
        ],
    )(key_blocks, counts)


def route_kernel(
    steps, kv_steps,
    ctl_ref, q_ref, k_ref, v_ref, g_ref,
    att_ref, dq_ref, own_kv, row_qg, recv_ref, late_ref, stats_ref,
    own_qg, row_kv, send_ref, kcat, vcat, probs, dots, mine_stats,
    head_send, head_recv, own_sem, x_send, x_recv, z_send, z_recv, s_send, s_recv,
):
    seq = lax.axis_index("seq")
    head = lax.axis_index("head")
    x, z = lax.rem(seq, NX), seq // NX

    def chip(cx, cz):
        return lax.rem(cz + 2 * NZ, NZ) * NX + lax.rem(cx + 2 * NX, NX)

    barrier = pltpu.get_barrier_semaphore()
    for shift in range(1, NH):
        pl.semaphore_signal(barrier, inc=1, device_id={"seq": seq, "head": lax.rem(head + shift, NH)}, device_id_type=MESH)
    for (cx, cz) in ((x + 1, z), (x - 1, z), (x, z + 1), (x, z - 1)):
        pl.semaphore_signal(barrier, inc=1, device_id={"seq": chip(cx, cz), "head": head}, device_id_type=MESH)
    pl.semaphore_wait(barrier, NH - 1 + 4)

    targets = ((k_ref, own_kv, 0), (v_ref, own_kv, 1), (q_ref, own_qg, 0), (g_ref, own_qg, 1))

    def rows_of(dst, which, h):
        start = pl.multiple_of(which * BLK + lax.rem(h, 2) * CHUNK, CHUNK)
        return dst.at[h // 2, pl.ds(start, CHUNK), :]

    def columns_of(src, h):
        return src.at[:, pl.ds(pl.multiple_of(h * HD, HD), HD)]

    def head_copy(array, peer_from, peer_to, shift):
        src, dst, which = targets[array]
        return pltpu.make_async_remote_copy(
            src_ref=columns_of(src, peer_to),
            dst_ref=rows_of(dst, which, peer_from),
            send_sem=head_send.at[array, shift],
            recv_sem=head_recv.at[array, shift],
            device_id={"seq": seq, "head": peer_to},
            device_id_type=MESH,
        )

    started = []
    own_copies = []
    for array, (src, dst, which) in enumerate(targets):
        for shift in range(1, NH):
            copy = head_copy(array, head, lax.rem(head + shift, NH), shift)
            copy.start()
            started.append(copy)
        own = pltpu.make_async_copy(columns_of(src, head), rows_of(dst, which, head), own_sem.at[array])
        own.start()
        own_copies.append(own)

    def wait_head(array):
        for shift in range(1, NH):
            peer = lax.rem(head + NH - shift, NH)
            head_copy(array, peer, peer, shift).wait_recv()
        own_copies[array].wait()

    owned = (own_kv, own_qg)
    rows = (row_kv, row_qg)
    x_plan = ((1, 0, 0), (-1, 0, 2), (1, 0, 2), (-1, 0, 0), (1, 1, 0), (-1, -1, 2))

    def x_copy(kind, i, arriving):
        sign, offset, first = x_plan[i]
        origin = lax.rem(x - offset - (sign if arriving else 0) + 2 * NX, NX)
        piece = rows[kind].at[pl.ds(4 * origin + first, 2)]
        other = chip(x - sign, z) if arriving else chip(x + sign, z)
        return pltpu.make_async_remote_copy(
            src_ref=piece if arriving or offset != 0 else owned[kind].at[pl.ds(first, 2)],
            dst_ref=piece, send_sem=x_send.at[kind, i], recv_sem=x_recv.at[kind, i],
            device_id={"seq": other, "head": head}, device_id_type=MESH,
        )

    def x_start(kind, i):
        copy = x_copy(kind, i, False)
        copy.start()
        started.append(copy)

    def landing(t, half):
        return recv_ref.at[2 * t + half] if t < kv_steps else late_ref.at[2 * (t - kv_steps) + half]

    def z_copy(half, t, arriving):
        sign = 1 if half == 0 else -1
        other = chip(x, z - sign) if arriving else chip(x, z + sign)
        slot = 2 * t + half
        return pltpu.make_async_remote_copy(
            src_ref=send_ref.at[slot], dst_ref=landing(t, half), send_sem=z_send.at[slot], recv_sem=z_recv.at[slot],
            device_id={"seq": other, "head": head}, device_id_type=MESH,
        )

    scale = 1.0 / math.sqrt(HD)
    key_at = lax.broadcasted_iota(jnp.int32, (BLK, 8 * BLK), 1)

    def attend_block(i):
        for t in range(8):
            code = ctl_ref[AT_CODE + i * 8 + t]
            near = row_kv[jnp.minimum(code, 15)]
            moved = recv_ref[jnp.clip(code - 16, 0, 2 * kv_steps - 1)]
            data = lax.select(code < 16, near, moved)
            kcat[t * BLK : (t + 1) * BLK, :] = data[0:BLK]
            vcat[t * BLK : (t + 1) * BLK, :] = data[BLK : 2 * BLK]
        q, g = own_qg[i, 0:BLK], own_qg[i, BLK : 2 * BLK]
        s = dot_nt(q, kcat[...]) * scale
        s = jnp.where(key_at < ctl_ref[AT_USED + i] * BLK, s, NEG)
        row_max = jnp.max(s, axis=1, keepdims=True)
        w = jnp.exp(s - row_max)
        row_sum = jnp.sum(w, axis=1, keepdims=True)
        att = (dot_nn(w.astype(BF16), vcat[...]) / row_sum).astype(BF16)
        total = row_max + jnp.log(row_sum)
        grad_dot = jnp.sum(g.astype(F32) * att.astype(F32), axis=1, keepdims=True)
        probs[...] = jnp.exp(s - total)
        dots[...] = jnp.broadcast_to(grad_dot, (BLK, BLK))
        att_ref[i * BLK : (i + 1) * BLK, :] = att
        mine_stats[i : i + 1, :] = jnp.transpose(jnp.broadcast_to(total, (BLK, BLK)))[0:1, :]
        mine_stats[i + 4 : i + 5, :] = jnp.transpose(jnp.broadcast_to(grad_dot, (BLK, BLK)))[0:1, :]

    def query_grad(i):
        g = own_qg[i, BLK : 2 * BLK]
        ds = (probs[...] * (dot_nt(g, vcat[...]) - dots[:, 0:1])).astype(BF16)
        dq_ref[i * BLK : (i + 1) * BLK, :] = (dot_nn(ds, kcat[...]) * scale).astype(BF16)

    def stat_copy(shift, origin, target):
        return pltpu.make_async_remote_copy(
            src_ref=mine_stats, dst_ref=stats_ref.at[origin], send_sem=s_send.at[shift], recv_sem=s_recv.at[shift],
            device_id={"seq": target, "head": head}, device_id_type=MESH,
        )

    def keep_own(kind):
        for i in range(4):
            rows[kind][4 * x + i] = owned[kind][i]

    wait_head(0)
    wait_head(1)
    for i in range(4):
        x_start(0, i)

    work = []
    for i in range(4):
        work.append(functools.partial(attend_block, i))
        work.append(functools.partial(query_grad, i))

    def send_stats():
        for shift in range(1, NX * NZ):
            copy = stat_copy(shift, seq, lax.rem(seq + shift, NX * NZ))
            copy.start()
            started.append(copy)
        own = pltpu.make_async_copy(mine_stats, stats_ref.at[seq], s_recv.at[0])
        own.start()
        own_copies.append(own)

    for t in range(steps):
        if t == PASS_KV:
            wait_head(2)
            wait_head(3)
            x_copy(0, 0, True).wait_recv()
            x_start(0, 4)
            x_copy(0, 1, True).wait_recv()
            x_start(0, 5)
            for i in range(4):
                x_start(1, i)
            keep_own(0)
            keep_own(1)
        elif t == ALL_KV:
            for i in range(2, 6):
                x_copy(0, i, True).wait_recv()
        elif t == PASS_QG:
            x_copy(1, 0, True).wait_recv()
            x_start(1, 4)
            x_copy(1, 1, True).wait_recv()
            x_start(1, 5)
        elif t == ALL_QG:
            for i in range(2, 6):
                x_copy(1, i, True).wait_recv()
        for half in range(2):
            slot = 2 * t + half
            value = ctl_ref[slot]
            size = jnp.abs(value)
            index = (127 - (size & 127)) & 15
            data = row_kv[index] if t >= ALL_KV else own_kv[index & 3]
            if t >= OWN_QG:
                other = row_qg[index] if t >= ALL_QG else own_qg[index & 3]
                data = lax.select(size >= 2048, data, other)
            if t >= LAG:
                z_copy(half, t - LAG, True).wait_recv()
                data = lax.select(value < 0, landing(t - LAG, half)[...], data)
            send_ref[slot] = data
        for half in range(2):
            copy = z_copy(half, t, False)
            copy.start()
            started.append(copy)
        if t >= kv_steps + LAG:
            if work:
                work.pop(0)()
                if not work:
                    send_stats()
    for t in range(steps - LAG, steps):
        for half in range(2):
            z_copy(half, t, True).wait_recv()
    while work:
        work.pop(0)()
        if not work:
            send_stats()
    for shift in range(1, NX * NZ):
        peer = lax.rem(seq + NX * NZ - shift, NX * NZ)
        stat_copy(shift, peer, peer).wait_recv()
    own_copies[-1].wait()
    for copy in started:
        copy.wait_send()


def route(variant, ctl, queries, keys, values, out_grad):
    steps, kv_steps = VARIANTS[variant]
    smem = pl.BlockSpec(memory_space=pltpu.SMEM)
    vmem = pl.BlockSpec(memory_space=pltpu.VMEM)
    out = jax.ShapeDtypeStruct((ROWS, HD), BF16)
    own = (4, 2 * BLK, HD)
    near = (16, 2 * BLK, HD)
    moved = (2 * steps, 2 * BLK, HD)
    early = (2 * kv_steps, 2 * BLK, HD)
    late = (2 * (steps - kv_steps), 2 * BLK, HD)
    stats = jax.ShapeDtypeStruct((NX * NZ, 8, BLK), F32)
    dma = pltpu.SemaphoreType.DMA
    return pl.pallas_call(
        functools.partial(route_kernel, steps, kv_steps),
        out_shape=(out, out, jax.ShapeDtypeStruct(own, BF16), jax.ShapeDtypeStruct(near, BF16), jax.ShapeDtypeStruct(early, BF16), jax.ShapeDtypeStruct(late, BF16), stats),
        in_specs=[smem] + [vmem] * 4,
        out_specs=[vmem] * 7,
        scratch_shapes=[
            pltpu.VMEM(own, BF16),
            pltpu.VMEM(near, BF16),
            pltpu.VMEM(moved, BF16),
            pltpu.VMEM((8 * BLK, HD), BF16),
            pltpu.VMEM((8 * BLK, HD), BF16),
            pltpu.VMEM((BLK, 8 * BLK), F32),
            pltpu.VMEM((BLK, BLK), F32),
            pltpu.VMEM((8, BLK), F32),
            dma((4, NH)), dma((4, NH)), dma((4,)),
            dma((2, 6)), dma((2, 6)),
            dma((2 * steps,)), dma((2 * steps,)),
            dma((NX * NZ,)), dma((NX * NZ,)),
        ],
        compiler_params=pltpu.CompilerParams(collective_id=1 + variant, has_side_effects=True),
    )(ctl, queries, keys, values, out_grad)


def keys_kernel(ctl_ref, kv_ref, qg_ref, recv_ref, late_ref, stats_ref, dk_ref, dv_ref, now, dk_acc, dv_acc):
    scale = 1.0 / math.sqrt(HD)
    dk_acc[...] = jnp.zeros_like(dk_acc)
    dv_acc[...] = jnp.zeros_like(dv_acc)

    def entry(n, carry):
        a = ctl_ref[AT_LIST + 4 * n]
        code = ctl_ref[AT_LIST + 4 * n + 1]
        mask = ctl_ref[AT_LIST + 4 * n + 2]

        @pl.when(code < 16)
        def _():
            now[...] = qg_ref[code]

        first_late = 16 + recv_ref.shape[0]

        @pl.when((code >= 16) & (code < first_late))
        def _():
            now[...] = recv_ref[code - 16]

        @pl.when(code >= first_late)
        def _():
            now[...] = late_ref[code - first_late]

        q, g = now[0:BLK, :], now[BLK : 2 * BLK, :]
        total = stats_ref[a // 4, pl.ds(lax.rem(a, 4), 1), :]
        grad_dot = stats_ref[a // 4, pl.ds(lax.rem(a, 4) + 4, 1), :]
        for j in range(4):

            @pl.when((mask & (1 << j)) > 0)
            def _():
                k = kv_ref[j, 0:BLK, :]
                v = kv_ref[j, BLK : 2 * BLK, :]
                p = jnp.exp(dot_nt(k, q) * scale - total)
                ds = (p * (dot_nt(v, g) - grad_dot)).astype(BF16)
                dk_acc[j] += dot_nn(ds, q)
                dv_acc[j] += dot_nn(p.astype(BF16), g)

        return carry

    lax.fori_loop(0, ctl_ref[AT_COUNT], entry, 0)
    for j in range(4):
        dk_ref[j * BLK : (j + 1) * BLK, :] = (dk_acc[j] * scale).astype(BF16)
        dv_ref[j * BLK : (j + 1) * BLK, :] = dv_acc[j].astype(BF16)


def key_grads(ctl, kv, qg, recv, late, stats):
    smem = pl.BlockSpec(memory_space=pltpu.SMEM)
    vmem = pl.BlockSpec(memory_space=pltpu.VMEM)
    out = jax.ShapeDtypeStruct((ROWS, HD), BF16)
    return pl.pallas_call(
        keys_kernel,
        out_shape=(out, out),
        in_specs=[smem] + [vmem] * 5,
        out_specs=[vmem] * 2,
        scratch_shapes=[
            pltpu.VMEM((2 * BLK, HD), BF16),
            pltpu.VMEM((4, BLK, HD), F32),
            pltpu.VMEM((4, BLK, HD), F32),
        ],
    )(ctl, kv, qg, recv, late, stats)


def on_device(queries, keys, values, out_grad, key_blocks, counts):
    seq = lax.axis_index("seq")
    ctl = make_plan(jnp.transpose(key_blocks), counts[None, :])

    def sparse(variant):
        att, dq, kv, qg, recv, late, stats = route(variant, ctl, queries, keys, values, out_grad)
        dk, dv = key_grads(ctl, kv, qg, recv, late, stats)
        return att, dq, dk, dv

    def dense():
        kv, qg = exchange(queries, keys, values, out_grad)
        live = jnp.arange(key_blocks.shape[1])[None, :] < counts[:, None]
        touch = jnp.any(live & (key_blocks // 4 == seq), axis=1)
        touch = (touch & (jnp.arange(key_blocks.shape[0]) // 4 != seq)).astype(jnp.int32)
        first = (seq * 4).reshape(1).astype(jnp.int32)
        return tuple(attend(first, touch, key_blocks, counts, kv, qg))

    branches = [functools.partial(sparse, variant) for variant in range(len(VARIANTS))] + [dense]
    return lax.switch(ctl[AT_PICK], branches)


def solution(mesh):
    rows = P(("seq", "head"), None)
    out = P("seq", "head")
    return jax.shard_map(
        on_device,
        mesh=mesh,
        in_specs=(rows,) * 4 + (P(), P()),
        out_specs=(out,) * 4,
        check_vma=False,
    )
```

```python
import functools
import heapq
import math

import jax
import jax.numpy as jnp
from jax import lax
from jax.experimental import pallas as pl
from jax.experimental.pallas import tpu as pltpu
from jax.sharding import PartitionSpec as P

MESH = pl.DeviceIdType.MESH
BLK = 128
HD = 128
NX = 4
NZ = 8
NH = 8
ROWS = 512
CHUNK = 64
SPLIT = 208
BF16 = jnp.bfloat16
F32 = jnp.float32
NEG = -1e30


def row_range(part):
    half_a, half_b = SPLIT // 32 * 16, SPLIT + (ROWS - SPLIT) // 32 * 16
    return {
        "A": (0, SPLIT),
        "A0": (0, half_a),
        "A1": (half_a, SPLIT),
        "B": (SPLIT, ROWS),
        "B0": (SPLIT, half_b),
        "B1": (half_b, ROWS),
    }[part]


def ring_sends(axis, sources, size, out, kind, prio):
    far = size // 2
    arrived = []
    for (offset, part, dep) in sources:
        if len(part) == 1:
            arrived.append((offset, part, dep))
            halves = [(part, +1, far - 1), (part, -1, far - 1)]
        else:
            arrived.append((offset, part, dep))
            sign = +1 if part[1] == "0" else -1
            halves = [(part, +1, far - 1), (part, -1, far - 1)]
        for (piece, sign, hops) in halves:
            last = dep
            at = offset
            for hop in range(1, hops + 1):
                out.append(dict(kind=kind, axis=axis, sign=sign, origin=at, part=piece, dep=last, left=far - hop, prio=prio))
                last = len(out) - 1
                at = step_offset(at, axis, sign)
                arrived.append((at, piece, last))
            for digit, way in (("0", +1), ("1", -1)):
                if way != sign:
                    continue
                tail = piece if len(piece) == 2 else piece + digit
                if tail[1] != digit:
                    continue
                out.append(dict(kind=kind, axis=axis, sign=sign, origin=at, part=tail, dep=last, left=0, prio=prio))
                arrived.append((step_offset(at, axis, sign), tail, len(out) - 1))
    return arrived


def step_offset(offset, axis, sign):
    ox, oz = offset
    return (ox + sign, oz) if axis == "x" else (ox, oz + sign)


def plan_sends():
    out = []
    for kind in (0, 1):
        own = -1 - kind
        first_a = ring_sends("x", [((0, 0), "A", own)], NX, out, kind, kind * 10)
        first_b = ring_sends("z", [((0, 0), "B", own)], NZ, out, kind, kind * 10)
        ring_sends("z", first_a, NZ, out, kind, kind * 10 + 1)
        ring_sends("x", first_b, NX, out, kind, kind * 10 + 1)
    rate = 46.0e3 * 1.0
    latency = 1.7
    ready_own = {-1: 4.0, -2: 8.0}
    arrival = {}
    free = {}
    start = {}
    waiting = {}
    events = []
    for i, m in enumerate(out):
        if m["dep"] < 0:
            heapq.heappush(events, (ready_own[m["dep"]], i))
    children = {}
    for i, m in enumerate(out):
        if m["dep"] >= 0:
            children.setdefault(m["dep"], []).append(i)
    queues = {("x", 1): [], ("x", -1): [], ("z", 1): [], ("z", -1): []}
    free = {k: 0.0 for k in queues}
    order = []
    while events or any(queues.values()):
        options = []
        for k, q in queues.items():
            if q:
                options.append((max(free[k], q[0][2]), k))
        next_link = min(options) if options else None
        if events and (next_link is None or events[0][0] <= next_link[0]):
            t, i = heapq.heappop(events)
            m = out[i]
            q = queues[(m["axis"], m["sign"])]
            q.append((m["prio"] // 10, -m["left"], t, i))
            q.sort(key=lambda e: (e[0], e[1], e[2], e[3]))
            continue
        t, k = next_link
        _, _, ready, i = queues[k].pop(0)
        m = out[i]
        lo, hi = row_range(m["part"])
        begin = max(free[k], ready)
        free[k] = begin + (hi - lo) * HD * 2 * 2 / rate
        start[i] = begin
        order.append((begin, ready, i))
        for c in children.get(i, []):
            heapq.heappush(events, (free[k] + latency, c))
    order.sort()
    return out, [i for (_, _, i) in order], max(free.values())


SENDS, ORDER, SPAN = plan_sends()


def exchange_kernel(q_ref, k_ref, v_ref, g_ref, kv_ref, qg_ref, send_sem, recv_sem, head_send, head_recv, own_sem):
    seq = lax.axis_index("seq")
    head = lax.axis_index("head")
    x, z = lax.rem(seq, NX), seq // NX

    def chip(cx, cz):
        return lax.rem(cz + 2 * NZ, NZ) * NX + lax.rem(cx + 2 * NX, NX)

    barrier = pltpu.get_barrier_semaphore()
    for shift in range(1, NH):
        pl.semaphore_signal(barrier, inc=1, device_id={"seq": seq, "head": lax.rem(head + shift, NH)}, device_id_type=MESH)
    for (cx, cz) in ((x + 1, z), (x - 1, z), (x, z + 1), (x, z - 1)):
        pl.semaphore_signal(barrier, inc=1, device_id={"seq": chip(cx, cz), "head": head}, device_id_type=MESH)
    pl.semaphore_wait(barrier, NH - 1 + 4)

    targets = ((k_ref, kv_ref, 0), (v_ref, kv_ref, 1), (q_ref, qg_ref, 0), (g_ref, qg_ref, 1))

    def rows_of(dst, which, h):
        return dst.at[seq, which, pl.ds(pl.multiple_of(h * CHUNK, CHUNK), CHUNK), :]

    def columns_of(src, h):
        return src.at[:, pl.ds(pl.multiple_of(h * HD, HD), HD)]

    head_copies = []
    own_copies = []
    for array, (src, dst, which) in enumerate(targets):
        for shift in range(1, NH):
            peer = lax.rem(head + shift, NH)
            copy = pltpu.make_async_remote_copy(
                src_ref=columns_of(src, peer),
                dst_ref=rows_of(dst, which, head),
                send_sem=head_send.at[array, shift],
                recv_sem=head_recv.at[array, shift],
                device_id={"seq": seq, "head": peer},
                device_id_type=MESH,
            )
            copy.start()
            head_copies.append(copy)
        own = pltpu.make_async_copy(columns_of(src, head), rows_of(dst, which, head), own_sem.at[array])
        own.start()
        own_copies.append(own)

    def wait_head(array):
        src, dst, which = targets[array]
        for shift in range(1, NH):
            peer = lax.rem(head + NH - shift, NH)
            pltpu.make_async_remote_copy(
                src_ref=columns_of(src, peer),
                dst_ref=rows_of(dst, which, peer),
                send_sem=head_send.at[array, shift],
                recv_sem=head_recv.at[array, shift],
                device_id={"seq": seq, "head": peer},
                device_id_type=MESH,
            ).wait_recv()
        own_copies[array].wait()

    buffers = (kv_ref, qg_ref)

    def piece(m, ox, oz):
        lo, hi = row_range(m["part"])
        return buffers[m["kind"]].at[chip(x - ox, z - oz), :, lo:hi, :]

    def send(i):
        m = SENDS[i]
        ox, oz = m["origin"]
        target = chip(x + m["sign"], z) if m["axis"] == "x" else chip(x, z + m["sign"])
        return pltpu.make_async_remote_copy(
            src_ref=piece(m, ox, oz),
            dst_ref=piece(m, ox, oz),
            send_sem=send_sem.at[i],
            recv_sem=recv_sem.at[i],
            device_id={"seq": target, "head": head},
            device_id_type=MESH,
        )

    def wait_recv(i):
        m = SENDS[i]
        ox, oz = step_offset(m["origin"], m["axis"], m["sign"])
        source = chip(x - m["sign"], z) if m["axis"] == "x" else chip(x, z - m["sign"])
        pltpu.make_async_remote_copy(
            src_ref=piece(m, ox, oz),
            dst_ref=piece(m, ox, oz),
            send_sem=send_sem.at[i],
            recv_sem=recv_sem.at[i],
            device_id={"seq": source, "head": head},
            device_id_type=MESH,
        ).wait_recv()

    ready = set()
    started = []
    for i in ORDER:
        dep = SENDS[i]["dep"]
        if dep not in ready:
            ready.add(dep)
            if dep < 0:
                wait_head(2 * (-1 - dep))
                wait_head(2 * (-1 - dep) + 1)
            else:
                wait_recv(dep)
        copy = send(i)
        copy.start()
        started.append(copy)
    for i in ORDER:
        if i not in ready:
            wait_recv(i)
    for copy in started:
        copy.wait_send()
    for copy in head_copies:
        copy.wait_send()


def exchange(queries, keys, values, out_grad):
    shape = jax.ShapeDtypeStruct((NX * NZ, 2, ROWS, HD), BF16)
    count = len(SENDS)
    return pl.pallas_call(
        exchange_kernel,
        out_shape=(shape, shape),
        in_specs=[pl.BlockSpec(memory_space=pltpu.VMEM)] * 4,
        out_specs=[pl.BlockSpec(memory_space=pl.ANY)] * 2,
        scratch_shapes=[
            pltpu.SemaphoreType.DMA((count,)),
            pltpu.SemaphoreType.DMA((count,)),
            pltpu.SemaphoreType.DMA((4, NH)),
            pltpu.SemaphoreType.DMA((4, NH)),
            pltpu.SemaphoreType.DMA((4,)),
        ],
        compiler_params=pltpu.CompilerParams(collective_id=0, has_side_effects=True),
    )(queries, keys, values, out_grad)


def dot_nt(a, b):
    return lax.dot_general(a, b, (((1,), (1,)), ((), ())), preferred_element_type=F32)


def dot_nn(a, b):
    return lax.dot_general(a, b, (((1,), (0,)), ((), ())), preferred_element_type=F32)


def dot_tn(a, b):
    return lax.dot_general(a, b, (((0,), (0,)), ((), ())), preferred_element_type=F32)


def attend_kernel(first_ref, touch_ref, blocks_ref, counts_ref, kv_ref, qg_ref, att_ref, dq_ref, dk_ref, dv_ref, s_ref, acc_ref, dk_acc, dv_acc):
    scale = 1.0 / math.sqrt(HD)
    dk_acc[...] = jnp.zeros_like(dk_acc)
    dv_acc[...] = jnp.zeros_like(dv_acc)
    first = first_ref[0]

    def load(ref, which, block):
        return ref[block // 4, which, pl.ds(pl.multiple_of(lax.rem(block, 4) * BLK, BLK), BLK), :]

    def query_block(a, local):
        count = counts_ref[a]
        q = load(qg_ref, 0, a)
        g = load(qg_ref, 1, a)

        def score(t, row_max):
            s = dot_nt(q, load(kv_ref, 0, blocks_ref[a, t])) * scale
            s_ref[t] = s
            return jnp.maximum(row_max, jnp.max(s, axis=1, keepdims=True))

        row_max = lax.fori_loop(0, count, score, jnp.full((BLK, 1), NEG, F32))
        acc_ref[...] = jnp.zeros_like(acc_ref)

        def mix(t, row_sum):
            w = jnp.exp(s_ref[t] - row_max)
            acc_ref[...] += dot_nn(w.astype(BF16), load(kv_ref, 1, blocks_ref[a, t]))
            return row_sum + jnp.sum(w, axis=1, keepdims=True)

        row_sum = lax.fori_loop(0, count, mix, jnp.zeros((BLK, 1), F32))
        att = (acc_ref[...] / row_sum).astype(BF16)
        total = row_max + jnp.log(row_sum)
        grad_dot = jnp.sum(g.astype(F32) * att.astype(F32), axis=1, keepdims=True)

        def pair(t):
            block = blocks_ref[a, t]
            p = jnp.exp(s_ref[t] - total)
            dp = dot_nt(g, load(kv_ref, 1, block))
            return block, p, (p * (dp - grad_dot)).astype(BF16)

        def add_key(slot, p, ds):
            dk_acc[slot] += dot_tn(ds, q)
            dv_acc[slot] += dot_tn(p.astype(BF16), g)

        if local:
            acc_ref[...] = jnp.zeros_like(acc_ref)

            def back(t, carry):
                block, p, ds = pair(t)
                acc_ref[...] += dot_nn(ds, load(kv_ref, 0, block))
                slot = block - first

                @pl.when((slot >= 0) & (slot < 4))
                def _():
                    add_key(slot, p, ds)

                return carry

            lax.fori_loop(0, count, back, 0)
            rows = pl.ds(pl.multiple_of((a - first) * BLK, BLK), BLK)
            att_ref[rows, :] = att
            dq_ref[rows, :] = (acc_ref[...] * scale).astype(BF16)
        else:

            def back(t, carry):
                slot = blocks_ref[a, t] - first

                @pl.when((slot >= 0) & (slot < 4))
                def _():
                    _, p, ds = pair(t)
                    add_key(slot, p, ds)

                return carry

            lax.fori_loop(0, count, back, 0)

    def own(i, carry):
        query_block(first + i, True)
        return carry

    lax.fori_loop(0, 4, own, 0)

    def other(a, carry):
        @pl.when(touch_ref[a] > 0)
        def _():
            query_block(a, False)

        return carry

    lax.fori_loop(0, 128, other, 0)
    for slot in range(4):
        dk_ref[slot * BLK : (slot + 1) * BLK, :] = (dk_acc[slot] * scale).astype(BF16)
        dv_ref[slot * BLK : (slot + 1) * BLK, :] = dv_acc[slot].astype(BF16)


def attend(first, touch, key_blocks, counts, kv, qg):
    shape = jax.ShapeDtypeStruct((ROWS, HD), BF16)
    smem = pl.BlockSpec(memory_space=pltpu.SMEM)
    vmem = pl.BlockSpec(memory_space=pltpu.VMEM)
    return pl.pallas_call(
        attend_kernel,
        out_shape=(shape,) * 4,
        in_specs=[smem] * 4 + [vmem] * 2,
        out_specs=[vmem] * 4,
        scratch_shapes=[
            pltpu.VMEM((8, BLK, BLK), F32),
            pltpu.VMEM((BLK, HD), F32),
            pltpu.VMEM((4, BLK, HD), F32),
            pltpu.VMEM((4, BLK, HD), F32),
        ],
    )(first, touch, key_blocks, counts, kv, qg)


LAG = 2
STEPS = 36
VARIANTS = ((26, 21), (29, 25), (36, 31))
PACK = 24
OWN_QG = 4
PASS_KV = 4
ALL_KV = 8
PASS_QG = 10
ALL_QG = 14
CTL = 1024
AT_CODE = 128
AT_PICK = 160
AT_COUNT = 161
AT_USED = 164
AT_LIST = 256


def plan_kernel(blocks_ref, counts_ref, ctl_ref, words_ref, words, where_kv, where_qg, sem):
    seq = lax.axis_index("seq")
    x, z = lax.rem(seq, NX), seq // NX
    brow = lax.broadcasted_iota(jnp.int32, (BLK, BLK), 0)
    count = counts_ref[...]
    hits = jnp.zeros((BLK, BLK), F32)
    for t in range(8):
        hits = jnp.where((blocks_ref[t : t + 1, :] == brow) & (count > t), 1.0, hits)
    row = lax.broadcasted_iota(jnp.int32, (32, BLK), 0)
    col = lax.broadcasted_iota(jnp.int32, (32, BLK), 1)
    device = lax.rem(row, NZ) * NX + row // NZ
    group = jnp.where(col // 4 == device, 1.0, 0.0)
    need_kv = dot_nt(group, hits)
    need_qg = dot_nn(group, hits)
    jrow = lax.broadcasted_iota(jnp.int32, (8, BLK), 0)
    jcol = lax.broadcasted_iota(jnp.int32, (8, BLK), 1)
    mine = jcol - seq * 4
    power = jnp.where(mine == 0, 1.0, jnp.where(mine == 1, 2.0, jnp.where(mine == 2, 4.0, jnp.where(mine == 3, 8.0, 0.0))))
    bits = dot_nn(power, hits)

    origin = jcol // 16
    source_x = lax.rem(jcol, 16) // 4
    delta = lax.rem(jrow - origin + NZ, NZ)
    near = (delta >= 1) & (delta < 4)
    back = delta > 4
    tie = delta == 4
    far = delta.astype(F32)
    ident = (127 - jcol).astype(F32)
    here = origin == jrow

    chains = []
    for column in range(NX):
        parts = [need[column * NZ : (column + 1) * NZ, :] > 0.5 for need in (need_kv, need_qg)]
        lean = jnp.zeros((8, BLK), F32)
        for part in parts:
            lean = lean + jnp.where(part & near, 1.0, 0.0) - jnp.where(part & back, 1.0, 0.0)
        lean = jnp.broadcast_to(jnp.sum(lean, axis=1, keepdims=True), (8, BLK))
        ahead = near | (tie & (lean < 0.0))
        behind = back | (tie & (lean >= 0.0))
        for sign in (1, -1):
            keys = []
            for part, base in zip(parts, (2048.0, 0.0)):
                hop = jnp.where(part & ahead, far, 0.0) if sign == 1 else jnp.where(part & behind, 8.0 - far, 0.0)
                most = jnp.max(hop, axis=0, keepdims=True)
                keys.append(jnp.where(here & (most > 0.5), most * 128.0 + base + ident, 0.0))
            chains.append(dict(sign=sign, column=column, keys=keys, sent=[]))
    zero = jnp.zeros((8, BLK), F32)
    last_any, last_kv = zero, zero
    marks = [zero, zero]
    ours = [x == column for column in range(NX)]
    for t in range(STEPS):
        chosen = [zero, zero]
        for c in chains:
            own = source_x == c["column"]
            if t >= LAG:
                passing = pltpu.roll(c["sent"][t - LAG], 1 if c["sign"] == 1 else 7, 0) - 128.0
                left = jnp.where(passing >= 2048.0, passing - 2048.0, passing)
                through = left > 127.5
            kv, qg = c["keys"]
            best = jnp.where(own, kv, 0.0) if t < ALL_KV else kv
            if t >= OWN_QG:
                best = jnp.maximum(best, jnp.where(own, qg, 0.0) if t < ALL_QG else qg)
            best = jnp.broadcast_to(jnp.max(best, axis=1, keepdims=True), (8, BLK))
            if t >= LAG:
                taken = jnp.where(through, -1.0, best)
                sent = jnp.where(through, passing, best)
                mark = jnp.where(through, -passing, best)
            else:
                taken, sent, mark = best, best, best
            c["keys"] = [jnp.where(k == taken, 0.0, k) for k in c["keys"]]
            c["sent"].append(sent)
            last_any = jnp.where(sent > 0.0, t + 1.0, last_any)
            last_kv = jnp.where(sent >= 2048.0, t + 1.0, last_kv)
            half = 0 if c["sign"] == 1 else 1
            chosen[half] = jnp.where(ours[c["column"]], mark, chosen[half])
        for half in range(2):
            marks[half] = jnp.where(jcol == t, chosen[half], marks[half])
    for c in chains:
        last_any = jnp.where((c["keys"][0] + c["keys"][1]) > 0.0, 999.0, last_any)
        for t in range(STEPS - LAG, STEPS):
            sent = c["sent"][t]
            left = jnp.where(sent >= 2048.0, sent - 2048.0, sent)
            last_any = jnp.where(left > 255.5, 999.0, last_any)
    last_any = jnp.max(jnp.max(last_any, axis=1, keepdims=True), axis=0, keepdims=True)
    last_kv = jnp.max(jnp.max(last_kv, axis=1, keepdims=True), axis=0, keepdims=True)
    index = jnp.zeros((1, 1), F32)
    for steps, kv_steps in VARIANTS:
        index = index + jnp.where((last_any > steps + 0.5) | (last_kv > kv_steps + 0.5), 1.0, 0.0)
    crowd = jnp.max(jnp.sum(jnp.where(need_qg > 0.5, 1.0, 0.0), axis=1, keepdims=True), axis=0, keepdims=True)
    index = jnp.where(crowd > PACK + 0.5, float(len(VARIANTS)), index)
    words_ref[0:8, :] = marks[0].astype(jnp.int32)
    words_ref[8:16, :] = marks[1].astype(jnp.int32)
    words_ref[16:24, :] = bits.astype(jnp.int32)
    words_ref[24:32, :] = blocks_ref[...]
    words_ref[32:40, :] = jnp.broadcast_to(count, (8, BLK))
    words_ref[40:48, :] = jnp.broadcast_to(index, (8, BLK)).astype(jnp.int32)
    copy = pltpu.make_async_copy(words_ref, words, sem)
    copy.start()
    copy.wait()

    ctl_ref[AT_PICK] = words[40, 0]
    for i in range(16):
        where_kv[z * 16 + i] = i
        where_qg[z * 16 + i] = i
    sources = (lax.rem(z + NZ - 1, NZ), lax.rem(z + 1, NZ))

    def slot(t, carry):
        for half in range(2):
            ctl_ref[2 * t + half] = words[half * 8 + z, t]
            value = jnp.abs(words[half * 8 + sources[half], t])
            block = 127 - (value & 127)
            spot = 16 + 2 * t + half

            @pl.when(value >= 2048)
            def _():
                where_kv[block] = spot

            @pl.when((value >= 128) & (value < 2048))
            def _():
                where_qg[block] = spot

        return carry

    lax.fori_loop(0, STEPS, slot, 0)
    for i in range(4):
        live = words[32, 4 * seq + i]
        ctl_ref[AT_USED + i] = live
        for t in range(8):
            block = jnp.where(t < live, words[24 + t, 4 * seq + i], 4 * seq + i)
            ctl_ref[AT_CODE + i * 8 + t] = where_kv[block]

    def entry(a, n):
        mask = words[16, a]

        @pl.when(mask > 0)
        def _():
            ctl_ref[AT_LIST + 4 * n] = a
            ctl_ref[AT_LIST + 4 * n + 1] = where_qg[a]
            ctl_ref[AT_LIST + 4 * n + 2] = mask

        return n + jnp.where(mask > 0, 1, 0)

    ctl_ref[AT_COUNT] = lax.fori_loop(0, BLK, entry, 0)


def make_plan(key_blocks, counts):
    vmem = pl.BlockSpec(memory_space=pltpu.VMEM)
    return pl.pallas_call(
        plan_kernel,
        out_shape=jax.ShapeDtypeStruct((CTL,), jnp.int32),
        in_specs=[vmem, vmem],
        out_specs=pl.BlockSpec(memory_space=pltpu.SMEM),
        scratch_shapes=[
            pltpu.VMEM((48, BLK), jnp.int32),
            pltpu.SMEM((48, BLK), jnp.int32),
            pltpu.SMEM((BLK,), jnp.int32),
            pltpu.SMEM((BLK,), jnp.int32),
            pltpu.SemaphoreType.DMA,
        ],
    )(key_blocks, counts)


def route_kernel(
    steps, kv_steps,
    ctl_ref, q_ref, k_ref, v_ref, g_ref,
    att_ref, dq_ref, own_kv, pack_ref, stats_ref,
    own_qg, row_kv, row_qg, recv_ref, late_ref, send_ref, kcat, vcat, probs, dots, mine_stats,
    head_send, head_recv, own_sem, x_send, x_recv, z_send, z_recv, s_send, s_recv,
):
    seq = lax.axis_index("seq")
    head = lax.axis_index("head")
    x, z = lax.rem(seq, NX), seq // NX

    def chip(cx, cz):
        return lax.rem(cz + 2 * NZ, NZ) * NX + lax.rem(cx + 2 * NX, NX)

    barrier = pltpu.get_barrier_semaphore()
    for shift in range(1, NH):
        pl.semaphore_signal(barrier, inc=1, device_id={"seq": seq, "head": lax.rem(head + shift, NH)}, device_id_type=MESH)
    for (cx, cz) in ((x + 1, z), (x - 1, z), (x, z + 1), (x, z - 1)):
        pl.semaphore_signal(barrier, inc=1, device_id={"seq": chip(cx, cz), "head": head}, device_id_type=MESH)
    pl.semaphore_wait(barrier, NH - 1 + 4)

    targets = ((k_ref, own_kv, 0), (v_ref, own_kv, 1), (q_ref, own_qg, 0), (g_ref, own_qg, 1))

    def rows_of(dst, which, h):
        start = pl.multiple_of(which * BLK + lax.rem(h, 2) * CHUNK, CHUNK)
        return dst.at[h // 2, pl.ds(start, CHUNK), :]

    def columns_of(src, h):
        return src.at[:, pl.ds(pl.multiple_of(h * HD, HD), HD)]

    def head_copy(array, peer_from, peer_to, shift):
        src, dst, which = targets[array]
        return pltpu.make_async_remote_copy(
            src_ref=columns_of(src, peer_to),
            dst_ref=rows_of(dst, which, peer_from),
            send_sem=head_send.at[array, shift],
            recv_sem=head_recv.at[array, shift],
            device_id={"seq": seq, "head": peer_to},
            device_id_type=MESH,
        )

    started = []
    own_copies = []
    for array, (src, dst, which) in enumerate(targets):
        for shift in range(1, NH):
            copy = head_copy(array, head, lax.rem(head + shift, NH), shift)
            copy.start()
            started.append(copy)
        own = pltpu.make_async_copy(columns_of(src, head), rows_of(dst, which, head), own_sem.at[array])
        own.start()
        own_copies.append(own)

    def wait_head(array):
        for shift in range(1, NH):
            peer = lax.rem(head + NH - shift, NH)
            head_copy(array, peer, peer, shift).wait_recv()
        own_copies[array].wait()

    owned = (own_kv, own_qg)
    rows = (row_kv, row_qg)
    x_plan = ((1, 0, 0), (-1, 0, 2), (1, 0, 2), (-1, 0, 0), (1, 1, 0), (-1, -1, 2))

    def x_copy(kind, i, arriving):
        sign, offset, first = x_plan[i]
        origin = lax.rem(x - offset - (sign if arriving else 0) + 2 * NX, NX)
        piece = rows[kind].at[pl.ds(4 * origin + first, 2)]
        other = chip(x - sign, z) if arriving else chip(x + sign, z)
        return pltpu.make_async_remote_copy(
            src_ref=piece if arriving or offset != 0 else owned[kind].at[pl.ds(first, 2)],
            dst_ref=piece, send_sem=x_send.at[kind, i], recv_sem=x_recv.at[kind, i],
            device_id={"seq": other, "head": head}, device_id_type=MESH,
        )

    def x_start(kind, i):
        copy = x_copy(kind, i, False)
        copy.start()
        started.append(copy)

    def landing(t, half):
        return recv_ref.at[2 * t + half] if t < kv_steps else late_ref.at[2 * (t - kv_steps) + half]

    def z_copy(half, t, part, arriving):
        sign = 1 if half == 0 else -1
        other = chip(x, z - sign) if arriving else chip(x, z + sign)
        slot = 2 * t + half
        rows = slice(part * BLK, part * BLK + BLK)
        return pltpu.make_async_remote_copy(
            src_ref=send_ref.at[slot, rows], dst_ref=landing(t, half).at[rows],
            send_sem=z_send.at[slot, part], recv_sem=z_recv.at[slot, part],
            device_id={"seq": other, "head": head}, device_id_type=MESH,
        )

    scale = 1.0 / math.sqrt(HD)
    key_at = lax.broadcasted_iota(jnp.int32, (BLK, 8 * BLK), 1)

    def attend_block(i):
        for t in range(8):
            code = ctl_ref[AT_CODE + i * 8 + t]
            near = row_kv[jnp.minimum(code, 15)]
            moved = recv_ref[jnp.clip(code - 16, 0, 2 * kv_steps - 1)]
            data = lax.select(code < 16, near, moved)
            kcat[t * BLK : (t + 1) * BLK, :] = data[0:BLK]
            vcat[t * BLK : (t + 1) * BLK, :] = data[BLK : 2 * BLK]
        q, g = own_qg[i, 0:BLK], own_qg[i, BLK : 2 * BLK]
        s = dot_nt(q, kcat[...]) * scale
        s = jnp.where(key_at < ctl_ref[AT_USED + i] * BLK, s, NEG)
        row_max = jnp.max(s, axis=1, keepdims=True)
        w = jnp.exp(s - row_max)
        row_sum = jnp.sum(w, axis=1, keepdims=True)
        att = (dot_nn(w.astype(BF16), vcat[...]) / row_sum).astype(BF16)
        total = row_max + jnp.log(row_sum)
        grad_dot = jnp.sum(g.astype(F32) * att.astype(F32), axis=1, keepdims=True)
        probs[...] = jnp.exp(s - total)
        dots[...] = jnp.broadcast_to(grad_dot, (BLK, BLK))
        att_ref[i * BLK : (i + 1) * BLK, :] = att
        mine_stats[i : i + 1, :] = jnp.transpose(jnp.broadcast_to(total, (BLK, BLK)))[0:1, :]
        mine_stats[i + 4 : i + 5, :] = jnp.transpose(jnp.broadcast_to(grad_dot, (BLK, BLK)))[0:1, :]

    def query_grad(i):
        g = own_qg[i, BLK : 2 * BLK]
        ds = (probs[...] * (dot_nt(g, vcat[...]) - dots[:, 0:1])).astype(BF16)
        dq_ref[i * BLK : (i + 1) * BLK, :] = (dot_nn(ds, kcat[...]) * scale).astype(BF16)

    def stat_copy(shift, origin, target):
        return pltpu.make_async_remote_copy(
            src_ref=mine_stats, dst_ref=stats_ref.at[origin], send_sem=s_send.at[shift], recv_sem=s_recv.at[shift],
            device_id={"seq": target, "head": head}, device_id_type=MESH,
        )

    def keep_own(kind):
        for i in range(4):
            rows[kind][4 * x + i] = owned[kind][i]

    wait_head(0)
    wait_head(1)
    for i in range(4):
        x_start(0, i)

    work = []
    for i in range(4):
        work.append(functools.partial(attend_block, i))
        work.append(functools.partial(query_grad, i))

    def send_stats():
        for shift in range(1, NX * NZ):
            copy = stat_copy(shift, seq, lax.rem(seq + shift, NX * NZ))
            copy.start()
            started.append(copy)
        own = pltpu.make_async_copy(mine_stats, stats_ref.at[seq], s_recv.at[0])
        own.start()
        own_copies.append(own)

    for t in range(steps):
        if t == PASS_KV:
            wait_head(2)
            wait_head(3)
            x_copy(0, 0, True).wait_recv()
            x_start(0, 4)
            x_copy(0, 1, True).wait_recv()
            x_start(0, 5)
            for i in range(4):
                x_start(1, i)
            keep_own(0)
            keep_own(1)
        elif t == ALL_KV:
            for i in range(2, 6):
                x_copy(0, i, True).wait_recv()
        elif t == PASS_QG:
            x_copy(1, 0, True).wait_recv()
            x_start(1, 4)
            x_copy(1, 1, True).wait_recv()
            x_start(1, 5)
        elif t == ALL_QG:
            for i in range(2, 6):
                x_copy(1, i, True).wait_recv()
        for part in range(2):
            rows_at = slice(part * BLK, part * BLK + BLK)
            for half in range(2):
                slot = 2 * t + half
                value = ctl_ref[slot]
                size = jnp.abs(value)
                index = (127 - (size & 127)) & 15
                data = row_kv[index, rows_at] if t >= ALL_KV else own_kv[index & 3, rows_at]
                if t >= OWN_QG:
                    other = row_qg[index, rows_at] if t >= ALL_QG else own_qg[index & 3, rows_at]
                    data = lax.select(size >= 2048, data, other)
                if t >= LAG:
                    z_copy(half, t - LAG, part, True).wait_recv()
                    data = lax.select(value < 0, landing(t - LAG, half)[rows_at], data)
                send_ref[slot, rows_at] = data
            for half in range(2):
                copy = z_copy(half, t, part, False)
                copy.start()
                started.append(copy)
        if t >= kv_steps + LAG:
            if work:
                work.pop(0)()
                if not work:
                    send_stats()
    for t in range(steps - LAG, steps):
        for half in range(2):
            for part in range(2):
                z_copy(half, t, part, True).wait_recv()
    while work:
        work.pop(0)()
        if not work:
            send_stats()
    for n in range(PACK):
        code = ctl_ref[AT_LIST + 4 * n + 1]
        data = lax.select(code < 16, row_qg[jnp.clip(code, 0, 15)], recv_ref[jnp.clip(code - 16, 0, 2 * kv_steps - 1)])
        last = 16 + 2 * kv_steps
        pack_ref[n] = lax.select(code < last, data, late_ref[jnp.clip(code - last, 0, 2 * (steps - kv_steps) - 1)])
    for shift in range(1, NX * NZ):
        peer = lax.rem(seq + NX * NZ - shift, NX * NZ)
        stat_copy(shift, peer, peer).wait_recv()
    own_copies[-1].wait()
    for copy in started:
        copy.wait_send()


def route(variant, ctl, queries, keys, values, out_grad):
    steps, kv_steps = VARIANTS[variant]
    smem = pl.BlockSpec(memory_space=pltpu.SMEM)
    vmem = pl.BlockSpec(memory_space=pltpu.VMEM)
    out = jax.ShapeDtypeStruct((ROWS, HD), BF16)
    own = (4, 2 * BLK, HD)
    near = (16, 2 * BLK, HD)
    moved = (2 * steps, 2 * BLK, HD)
    early = (2 * kv_steps, 2 * BLK, HD)
    late = (2 * (steps - kv_steps), 2 * BLK, HD)
    stats = jax.ShapeDtypeStruct((NX * NZ, 8, BLK), F32)
    dma = pltpu.SemaphoreType.DMA
    return pl.pallas_call(
        functools.partial(route_kernel, steps, kv_steps),
        out_shape=(out, out, jax.ShapeDtypeStruct(own, BF16), jax.ShapeDtypeStruct((PACK, 2 * BLK, HD), BF16), stats),
        in_specs=[smem] + [vmem] * 4,
        out_specs=[vmem] * 5,
        scratch_shapes=[
            pltpu.VMEM(own, BF16),
            pltpu.VMEM(near, BF16),
            pltpu.VMEM(near, BF16),
            pltpu.VMEM(early, BF16),
            pltpu.VMEM(late, BF16),
            pltpu.VMEM(moved, BF16),
            pltpu.VMEM((8 * BLK, HD), BF16),
            pltpu.VMEM((8 * BLK, HD), BF16),
            pltpu.VMEM((BLK, 8 * BLK), F32),
            pltpu.VMEM((BLK, BLK), F32),
            pltpu.VMEM((8, BLK), F32),
            dma((4, NH)), dma((4, NH)), dma((4,)),
            dma((2, 6)), dma((2, 6)),
            dma((2 * steps, 2)), dma((2 * steps, 2)),
            dma((NX * NZ,)), dma((NX * NZ,)),
        ],
        compiler_params=pltpu.CompilerParams(collective_id=1 + variant, has_side_effects=True),
    )(ctl, queries, keys, values, out_grad)


def keys_kernel(ctl_ref, kv_ref, pack_ref, stats_ref, dk_ref, dv_ref, dk_acc, dv_acc):
    scale = 1.0 / math.sqrt(HD)
    dk_acc[...] = jnp.zeros_like(dk_acc)
    dv_acc[...] = jnp.zeros_like(dv_acc)

    def entry(n, carry):
        a = ctl_ref[AT_LIST + 4 * n]
        mask = ctl_ref[AT_LIST + 4 * n + 2]

        q, g = pack_ref[n, 0:BLK, :], pack_ref[n, BLK : 2 * BLK, :]
        total = stats_ref[a // 4, pl.ds(lax.rem(a, 4), 1), :]
        grad_dot = stats_ref[a // 4, pl.ds(lax.rem(a, 4) + 4, 1), :]
        for j in range(4):

            @pl.when((mask & (1 << j)) > 0)
            def _():
                k = kv_ref[j, 0:BLK, :]
                v = kv_ref[j, BLK : 2 * BLK, :]
                p = jnp.exp(dot_nt(k, q) * scale - total)
                ds = (p * (dot_nt(v, g) - grad_dot)).astype(BF16)
                dk_acc[j] += dot_nn(ds, q)
                dv_acc[j] += dot_nn(p.astype(BF16), g)

        return carry

    lax.fori_loop(0, ctl_ref[AT_COUNT], entry, 0)
    for j in range(4):
        dk_ref[j * BLK : (j + 1) * BLK, :] = (dk_acc[j] * scale).astype(BF16)
        dv_ref[j * BLK : (j + 1) * BLK, :] = dv_acc[j].astype(BF16)


def key_grads(ctl, kv, pack, stats):
    smem = pl.BlockSpec(memory_space=pltpu.SMEM)
    vmem = pl.BlockSpec(memory_space=pltpu.VMEM)
    out = jax.ShapeDtypeStruct((ROWS, HD), BF16)
    return pl.pallas_call(
        keys_kernel,
        out_shape=(out, out),
        in_specs=[smem] + [vmem] * 3,
        out_specs=[vmem] * 2,
        scratch_shapes=[
            pltpu.VMEM((4, BLK, HD), F32),
            pltpu.VMEM((4, BLK, HD), F32),
        ],
    )(ctl, kv, pack, stats)


def on_device(queries, keys, values, out_grad, key_blocks, counts):
    seq = lax.axis_index("seq")
    ctl = make_plan(jnp.transpose(key_blocks), counts[None, :])

    def sparse(variant):
        att, dq, kv, pack, stats = route(variant, ctl, queries, keys, values, out_grad)
        dk, dv = key_grads(ctl, kv, pack, stats)
        return att, dq, dk, dv

    def dense():
        kv, qg = exchange(queries, keys, values, out_grad)
        live = jnp.arange(key_blocks.shape[1])[None, :] < counts[:, None]
        touch = jnp.any(live & (key_blocks // 4 == seq), axis=1)
        touch = (touch & (jnp.arange(key_blocks.shape[0]) // 4 != seq)).astype(jnp.int32)
        first = (seq * 4).reshape(1).astype(jnp.int32)
        return tuple(attend(first, touch, key_blocks, counts, kv, qg))

    branches = [functools.partial(sparse, variant) for variant in range(len(VARIANTS))] + [dense]
    return lax.switch(ctl[AT_PICK], branches)


def solution(mesh):
    rows = P(("seq", "head"), None)
    out = P("seq", "head")
    return jax.shard_map(
        on_device,
        mesh=mesh,
        in_specs=(rows,) * 4 + (P(), P()),
        out_specs=(out,) * 4,
        check_vma=False,
    )
```

```python
import functools
import heapq
import math

import jax
import jax.numpy as jnp
from jax import lax
from jax.experimental import pallas as pl
from jax.experimental.pallas import tpu as pltpu
from jax.sharding import PartitionSpec as P

MESH = pl.DeviceIdType.MESH
BLK = 128
HD = 128
NX = 4
NZ = 8
NH = 8
ROWS = 512
CHUNK = 64
SPLIT = 208
BF16 = jnp.bfloat16
F32 = jnp.float32
NEG = -1e30


def row_range(part):
    half_a, half_b = SPLIT // 32 * 16, SPLIT + (ROWS - SPLIT) // 32 * 16
    return {
        "A": (0, SPLIT),
        "A0": (0, half_a),
        "A1": (half_a, SPLIT),
        "B": (SPLIT, ROWS),
        "B0": (SPLIT, half_b),
        "B1": (half_b, ROWS),
    }[part]


def ring_sends(axis, sources, size, out, kind, prio):
    far = size // 2
    arrived = []
    for (offset, part, dep) in sources:
        if len(part) == 1:
            arrived.append((offset, part, dep))
            halves = [(part, +1, far - 1), (part, -1, far - 1)]
        else:
            arrived.append((offset, part, dep))
            sign = +1 if part[1] == "0" else -1
            halves = [(part, +1, far - 1), (part, -1, far - 1)]
        for (piece, sign, hops) in halves:
            last = dep
            at = offset
            for hop in range(1, hops + 1):
                out.append(dict(kind=kind, axis=axis, sign=sign, origin=at, part=piece, dep=last, left=far - hop, prio=prio))
                last = len(out) - 1
                at = step_offset(at, axis, sign)
                arrived.append((at, piece, last))
            for digit, way in (("0", +1), ("1", -1)):
                if way != sign:
                    continue
                tail = piece if len(piece) == 2 else piece + digit
                if tail[1] != digit:
                    continue
                out.append(dict(kind=kind, axis=axis, sign=sign, origin=at, part=tail, dep=last, left=0, prio=prio))
                arrived.append((step_offset(at, axis, sign), tail, len(out) - 1))
    return arrived


def step_offset(offset, axis, sign):
    ox, oz = offset
    return (ox + sign, oz) if axis == "x" else (ox, oz + sign)


def plan_sends():
    out = []
    for kind in (0, 1):
        own = -1 - kind
        first_a = ring_sends("x", [((0, 0), "A", own)], NX, out, kind, kind * 10)
        first_b = ring_sends("z", [((0, 0), "B", own)], NZ, out, kind, kind * 10)
        ring_sends("z", first_a, NZ, out, kind, kind * 10 + 1)
        ring_sends("x", first_b, NX, out, kind, kind * 10 + 1)
    rate = 46.0e3 * 1.0
    latency = 1.7
    ready_own = {-1: 4.0, -2: 8.0}
    arrival = {}
    free = {}
    start = {}
    waiting = {}
    events = []
    for i, m in enumerate(out):
        if m["dep"] < 0:
            heapq.heappush(events, (ready_own[m["dep"]], i))
    children = {}
    for i, m in enumerate(out):
        if m["dep"] >= 0:
            children.setdefault(m["dep"], []).append(i)
    queues = {("x", 1): [], ("x", -1): [], ("z", 1): [], ("z", -1): []}
    free = {k: 0.0 for k in queues}
    order = []
    while events or any(queues.values()):
        options = []
        for k, q in queues.items():
            if q:
                options.append((max(free[k], q[0][2]), k))
        next_link = min(options) if options else None
        if events and (next_link is None or events[0][0] <= next_link[0]):
            t, i = heapq.heappop(events)
            m = out[i]
            q = queues[(m["axis"], m["sign"])]
            q.append((m["prio"] // 10, -m["left"], t, i))
            q.sort(key=lambda e: (e[0], e[1], e[2], e[3]))
            continue
        t, k = next_link
        _, _, ready, i = queues[k].pop(0)
        m = out[i]
        lo, hi = row_range(m["part"])
        begin = max(free[k], ready)
        free[k] = begin + (hi - lo) * HD * 2 * 2 / rate
        start[i] = begin
        order.append((begin, ready, i))
        for c in children.get(i, []):
            heapq.heappush(events, (free[k] + latency, c))
    order.sort()
    return out, [i for (_, _, i) in order], max(free.values())


SENDS, ORDER, SPAN = plan_sends()


def exchange_kernel(q_ref, k_ref, v_ref, g_ref, kv_ref, qg_ref, send_sem, recv_sem, head_send, head_recv, own_sem):
    seq = lax.axis_index("seq")
    head = lax.axis_index("head")
    x, z = lax.rem(seq, NX), seq // NX

    def chip(cx, cz):
        return lax.rem(cz + 2 * NZ, NZ) * NX + lax.rem(cx + 2 * NX, NX)

    barrier = pltpu.get_barrier_semaphore()
    for shift in range(1, NH):
        pl.semaphore_signal(barrier, inc=1, device_id={"seq": seq, "head": lax.rem(head + shift, NH)}, device_id_type=MESH)
    for (cx, cz) in ((x + 1, z), (x - 1, z), (x, z + 1), (x, z - 1)):
        pl.semaphore_signal(barrier, inc=1, device_id={"seq": chip(cx, cz), "head": head}, device_id_type=MESH)
    pl.semaphore_wait(barrier, NH - 1 + 4)

    targets = ((k_ref, kv_ref, 0), (v_ref, kv_ref, 1), (q_ref, qg_ref, 0), (g_ref, qg_ref, 1))

    def rows_of(dst, which, h):
        return dst.at[seq, which, pl.ds(pl.multiple_of(h * CHUNK, CHUNK), CHUNK), :]

    def columns_of(src, h):
        return src.at[:, pl.ds(pl.multiple_of(h * HD, HD), HD)]

    head_copies = []
    own_copies = []
    for array, (src, dst, which) in enumerate(targets):
        for shift in range(1, NH):
            peer = lax.rem(head + shift, NH)
            copy = pltpu.make_async_remote_copy(
                src_ref=columns_of(src, peer),
                dst_ref=rows_of(dst, which, head),
                send_sem=head_send.at[array, shift],
                recv_sem=head_recv.at[array, shift],
                device_id={"seq": seq, "head": peer},
                device_id_type=MESH,
            )
            copy.start()
            head_copies.append(copy)
        own = pltpu.make_async_copy(columns_of(src, head), rows_of(dst, which, head), own_sem.at[array])
        own.start()
        own_copies.append(own)

    def wait_head(array):
        src, dst, which = targets[array]
        for shift in range(1, NH):
            peer = lax.rem(head + NH - shift, NH)
            pltpu.make_async_remote_copy(
                src_ref=columns_of(src, peer),
                dst_ref=rows_of(dst, which, peer),
                send_sem=head_send.at[array, shift],
                recv_sem=head_recv.at[array, shift],
                device_id={"seq": seq, "head": peer},
                device_id_type=MESH,
            ).wait_recv()
        own_copies[array].wait()

    buffers = (kv_ref, qg_ref)

    def piece(m, ox, oz):
        lo, hi = row_range(m["part"])
        return buffers[m["kind"]].at[chip(x - ox, z - oz), :, lo:hi, :]

    def send(i):
        m = SENDS[i]
        ox, oz = m["origin"]
        target = chip(x + m["sign"], z) if m["axis"] == "x" else chip(x, z + m["sign"])
        return pltpu.make_async_remote_copy(
            src_ref=piece(m, ox, oz),
            dst_ref=piece(m, ox, oz),
            send_sem=send_sem.at[i],
            recv_sem=recv_sem.at[i],
            device_id={"seq": target, "head": head},
            device_id_type=MESH,
        )

    def wait_recv(i):
        m = SENDS[i]
        ox, oz = step_offset(m["origin"], m["axis"], m["sign"])
        source = chip(x - m["sign"], z) if m["axis"] == "x" else chip(x, z - m["sign"])
        pltpu.make_async_remote_copy(
            src_ref=piece(m, ox, oz),
            dst_ref=piece(m, ox, oz),
            send_sem=send_sem.at[i],
            recv_sem=recv_sem.at[i],
            device_id={"seq": source, "head": head},
            device_id_type=MESH,
        ).wait_recv()

    ready = set()
    started = []
    for i in ORDER:
        dep = SENDS[i]["dep"]
        if dep not in ready:
            ready.add(dep)
            if dep < 0:
                wait_head(2 * (-1 - dep))
                wait_head(2 * (-1 - dep) + 1)
            else:
                wait_recv(dep)
        copy = send(i)
        copy.start()
        started.append(copy)
    for i in ORDER:
        if i not in ready:
            wait_recv(i)
    for copy in started:
        copy.wait_send()
    for copy in head_copies:
        copy.wait_send()


def exchange(queries, keys, values, out_grad):
    shape = jax.ShapeDtypeStruct((NX * NZ, 2, ROWS, HD), BF16)
    count = len(SENDS)
    return pl.pallas_call(
        exchange_kernel,
        out_shape=(shape, shape),
        in_specs=[pl.BlockSpec(memory_space=pltpu.VMEM)] * 4,
        out_specs=[pl.BlockSpec(memory_space=pl.ANY)] * 2,
        scratch_shapes=[
            pltpu.SemaphoreType.DMA((count,)),
            pltpu.SemaphoreType.DMA((count,)),
            pltpu.SemaphoreType.DMA((4, NH)),
            pltpu.SemaphoreType.DMA((4, NH)),
            pltpu.SemaphoreType.DMA((4,)),
        ],
        compiler_params=pltpu.CompilerParams(collective_id=0, has_side_effects=True),
    )(queries, keys, values, out_grad)


def dot_nt(a, b):
    return lax.dot_general(a, b, (((1,), (1,)), ((), ())), preferred_element_type=F32)


def dot_nn(a, b):
    return lax.dot_general(a, b, (((1,), (0,)), ((), ())), preferred_element_type=F32)


def dot_tn(a, b):
    return lax.dot_general(a, b, (((0,), (0,)), ((), ())), preferred_element_type=F32)


def attend_kernel(first_ref, touch_ref, blocks_ref, counts_ref, kv_ref, qg_ref, att_ref, dq_ref, dk_ref, dv_ref, s_ref, acc_ref, dk_acc, dv_acc):
    scale = 1.0 / math.sqrt(HD)
    dk_acc[...] = jnp.zeros_like(dk_acc)
    dv_acc[...] = jnp.zeros_like(dv_acc)
    first = first_ref[0]

    def load(ref, which, block):
        return ref[block // 4, which, pl.ds(pl.multiple_of(lax.rem(block, 4) * BLK, BLK), BLK), :]

    def query_block(a, local):
        count = counts_ref[a]
        q = load(qg_ref, 0, a)
        g = load(qg_ref, 1, a)

        def score(t, row_max):
            s = dot_nt(q, load(kv_ref, 0, blocks_ref[a, t])) * scale
            s_ref[t] = s
            return jnp.maximum(row_max, jnp.max(s, axis=1, keepdims=True))

        row_max = lax.fori_loop(0, count, score, jnp.full((BLK, 1), NEG, F32))
        acc_ref[...] = jnp.zeros_like(acc_ref)

        def mix(t, row_sum):
            w = jnp.exp(s_ref[t] - row_max)
            acc_ref[...] += dot_nn(w.astype(BF16), load(kv_ref, 1, blocks_ref[a, t]))
            return row_sum + jnp.sum(w, axis=1, keepdims=True)

        row_sum = lax.fori_loop(0, count, mix, jnp.zeros((BLK, 1), F32))
        att = (acc_ref[...] / row_sum).astype(BF16)
        total = row_max + jnp.log(row_sum)
        grad_dot = jnp.sum(g.astype(F32) * att.astype(F32), axis=1, keepdims=True)

        def pair(t):
            block = blocks_ref[a, t]
            p = jnp.exp(s_ref[t] - total)
            dp = dot_nt(g, load(kv_ref, 1, block))
            return block, p, (p * (dp - grad_dot)).astype(BF16)

        def add_key(slot, p, ds):
            dk_acc[slot] += dot_tn(ds, q)
            dv_acc[slot] += dot_tn(p.astype(BF16), g)

        if local:
            acc_ref[...] = jnp.zeros_like(acc_ref)

            def back(t, carry):
                block, p, ds = pair(t)
                acc_ref[...] += dot_nn(ds, load(kv_ref, 0, block))
                slot = block - first

                @pl.when((slot >= 0) & (slot < 4))
                def _():
                    add_key(slot, p, ds)

                return carry

            lax.fori_loop(0, count, back, 0)
            rows = pl.ds(pl.multiple_of((a - first) * BLK, BLK), BLK)
            att_ref[rows, :] = att
            dq_ref[rows, :] = (acc_ref[...] * scale).astype(BF16)
        else:

            def back(t, carry):
                slot = blocks_ref[a, t] - first

                @pl.when((slot >= 0) & (slot < 4))
                def _():
                    _, p, ds = pair(t)
                    add_key(slot, p, ds)

                return carry

            lax.fori_loop(0, count, back, 0)

    def own(i, carry):
        query_block(first + i, True)
        return carry

    lax.fori_loop(0, 4, own, 0)

    def other(a, carry):
        @pl.when(touch_ref[a] > 0)
        def _():
            query_block(a, False)

        return carry

    lax.fori_loop(0, 128, other, 0)
    for slot in range(4):
        dk_ref[slot * BLK : (slot + 1) * BLK, :] = (dk_acc[slot] * scale).astype(BF16)
        dv_ref[slot * BLK : (slot + 1) * BLK, :] = dv_acc[slot].astype(BF16)


def attend(first, touch, key_blocks, counts, kv, qg):
    shape = jax.ShapeDtypeStruct((ROWS, HD), BF16)
    smem = pl.BlockSpec(memory_space=pltpu.SMEM)
    vmem = pl.BlockSpec(memory_space=pltpu.VMEM)
    return pl.pallas_call(
        attend_kernel,
        out_shape=(shape,) * 4,
        in_specs=[smem] * 4 + [vmem] * 2,
        out_specs=[vmem] * 4,
        scratch_shapes=[
            pltpu.VMEM((8, BLK, BLK), F32),
            pltpu.VMEM((BLK, HD), F32),
            pltpu.VMEM((4, BLK, HD), F32),
            pltpu.VMEM((4, BLK, HD), F32),
        ],
    )(first, touch, key_blocks, counts, kv, qg)


LAG = 2
STEPS = 34
VARIANTS = ((24, 20), (27, 23), (34, 30))
PACK = 24
GROUP = 4
OWN_QG = 4
PASS_KV = 4
NEAR_KV = 6
ALL_KV = 8
PASS_QG = 10
NEAR_QG = 12
ALL_QG = 14
CTL = 2048
AT_CODE = 128
AT_PICK = 160
AT_COUNT = 161
AT_USED = 164
AT_LIST = 256
AT_PAIRS = 1024


def plan_kernel(blocks_ref, counts_ref, ctl_ref, pick_ref, words_ref, words, where_kv, where_qg, sem):
    seq = lax.axis_index("seq")
    x, z = lax.rem(seq, NX), seq // NX
    brow = lax.broadcasted_iota(jnp.int32, (BLK, BLK), 0)
    count = counts_ref[...]
    hits = jnp.zeros((BLK, BLK), F32)
    for t in range(8):
        hits = jnp.where((blocks_ref[t : t + 1, :] == brow) & (count > t), 1.0, hits)
    row = lax.broadcasted_iota(jnp.int32, (32, BLK), 0)
    col = lax.broadcasted_iota(jnp.int32, (32, BLK), 1)
    device = lax.rem(row, NZ) * NX + row // NZ
    group = jnp.where(col // 4 == device, 1.0, 0.0)
    need_kv = dot_nt(group, hits)
    need_qg = dot_nn(group, hits)
    jrow = lax.broadcasted_iota(jnp.int32, (8, BLK), 0)
    jcol = lax.broadcasted_iota(jnp.int32, (8, BLK), 1)
    mine = jcol - seq * 4
    power = jnp.where(mine == 0, 1.0, jnp.where(mine == 1, 2.0, jnp.where(mine == 2, 4.0, jnp.where(mine == 3, 8.0, 0.0))))
    bits = dot_nn(power, hits)

    origin = jcol // 16
    source_x = lax.rem(jcol, 16) // 4
    delta = lax.rem(jrow - origin + NZ, NZ)
    near = (delta >= 1) & (delta < 4)
    back = delta > 4
    tie = delta == 4
    far = delta.astype(F32)
    ident = (127 - jcol).astype(F32)
    here = origin == jrow

    chains = []
    for column in range(NX):
        parts = [need[column * NZ : (column + 1) * NZ, :] > 0.5 for need in (need_kv, need_qg)]
        lean = jnp.zeros((8, BLK), F32)
        for part in parts:
            lean = lean + jnp.where(part & near, 1.0, 0.0) - jnp.where(part & back, 1.0, 0.0)
        lean = jnp.broadcast_to(jnp.sum(lean, axis=1, keepdims=True), (8, BLK))
        ahead = near | (tie & (lean < 0.0))
        behind = back | (tie & (lean >= 0.0))
        for sign in (1, -1):
            keys = []
            for part, base in zip(parts, (2048.0, 0.0)):
                hop = jnp.where(part & ahead, far, 0.0) if sign == 1 else jnp.where(part & behind, 8.0 - far, 0.0)
                most = jnp.max(hop, axis=0, keepdims=True)
                keys.append(jnp.where(here & (most > 0.5), most * 128.0 + base + ident, 0.0))
            chains.append(dict(sign=sign, column=column, keys=keys, sent=[]))
    zero = jnp.zeros((8, BLK), F32)
    last_any, last_kv = zero, zero
    marks = [zero, zero]
    ours = [x == column for column in range(NX)]
    for t in range(STEPS):
        chosen = [zero, zero]
        for c in chains:
            apart = lax.rem(source_x - c["column"] + NX, NX)
            own, close = apart == 0, apart != 2
            if t >= LAG:
                passing = pltpu.roll(c["sent"][t - LAG], 1 if c["sign"] == 1 else 7, 0) - 128.0
                left = jnp.where(passing >= 2048.0, passing - 2048.0, passing)
                through = left > 127.5
            kv, qg = c["keys"]
            best = kv if t >= ALL_KV else jnp.where(close if t >= NEAR_KV else own, kv, 0.0)
            if t >= OWN_QG:
                best = jnp.maximum(best, qg if t >= ALL_QG else jnp.where(close if t >= NEAR_QG else own, qg, 0.0))
            best = jnp.broadcast_to(jnp.max(best, axis=1, keepdims=True), (8, BLK))
            if t >= LAG:
                taken = jnp.where(through, -1.0, best)
                sent = jnp.where(through, passing, best)
                mark = jnp.where(through, -passing, best)
            else:
                taken, sent, mark = best, best, best
            c["keys"] = [jnp.where(k == taken, 0.0, k) for k in c["keys"]]
            c["sent"].append(sent)
            last_any = jnp.where(sent > 0.0, t + 1.0, last_any)
            last_kv = jnp.where(sent >= 2048.0, t + 1.0, last_kv)
            half = 0 if c["sign"] == 1 else 1
            chosen[half] = jnp.where(ours[c["column"]], mark, chosen[half])
        for half in range(2):
            marks[half] = jnp.where(jcol == t, chosen[half], marks[half])
    for c in chains:
        last_any = jnp.where((c["keys"][0] + c["keys"][1]) > 0.0, 999.0, last_any)
        for t in range(STEPS - LAG, STEPS):
            sent = c["sent"][t]
            left = jnp.where(sent >= 2048.0, sent - 2048.0, sent)
            last_any = jnp.where(left > 255.5, 999.0, last_any)
    last_any = jnp.max(jnp.max(last_any, axis=1, keepdims=True), axis=0, keepdims=True)
    last_kv = jnp.max(jnp.max(last_kv, axis=1, keepdims=True), axis=0, keepdims=True)
    index = jnp.zeros((1, 1), F32)
    for steps, kv_steps in VARIANTS:
        index = index + jnp.where((last_any > steps + 0.5) | (last_kv > kv_steps + 0.5), 1.0, 0.0)
    crowd = jnp.max(jnp.sum(jnp.where(need_qg > 0.5, 1.0, 0.0), axis=1, keepdims=True), axis=0, keepdims=True)
    index = jnp.where(crowd > PACK + 0.5, float(len(VARIANTS)), index)
    words_ref[0:8, :] = marks[0].astype(jnp.int32)
    words_ref[8:16, :] = marks[1].astype(jnp.int32)
    words_ref[16:24, :] = bits.astype(jnp.int32)
    words_ref[24:32, :] = blocks_ref[...]
    words_ref[32:40, :] = jnp.broadcast_to(count, (8, BLK))
    words_ref[40:48, :] = jnp.broadcast_to(index, (8, BLK)).astype(jnp.int32)
    copy = pltpu.make_async_copy(words_ref, words, sem)
    copy.start()
    copy.wait()

    pick_ref[0] = words[40, 0]
    for i in range(16):
        where_kv[z * 16 + i] = i
        where_qg[z * 16 + i] = i
    sources = (lax.rem(z + NZ - 1, NZ), lax.rem(z + 1, NZ))

    def slot(t, carry):
        for half in range(2):
            ctl_ref[2 * t + half] = words[half * 8 + z, t]
            value = jnp.abs(words[half * 8 + sources[half], t])
            block = 127 - (value & 127)
            spot = 16 + 2 * t + half

            @pl.when(value >= 2048)
            def _():
                where_kv[block] = spot

            @pl.when((value >= 128) & (value < 2048))
            def _():
                where_qg[block] = spot

        return carry

    lax.fori_loop(0, STEPS, slot, 0)
    for i in range(4):
        live = words[32, 4 * seq + i]
        ctl_ref[AT_USED + i] = live
        for t in range(8):
            block = jnp.where(t < live, words[24 + t, 4 * seq + i], 4 * seq + i)
            ctl_ref[AT_CODE + i * 8 + t] = where_kv[block]

    def entry(a, totals):
        mask = words[16, a]
        n, pairs = totals

        @pl.when(mask > 0)
        def _():
            ctl_ref[AT_LIST + n] = where_qg[a]
            at = pairs
            for j in range(4):
                bit = (mask >> j) & 1
                ctl_ref[AT_PAIRS + at] = n + a * 256 + j * 65536
                at = at + bit

        ones = (mask & 1) + ((mask >> 1) & 1) + ((mask >> 2) & 1) + ((mask >> 3) & 1)
        return n + jnp.where(mask > 0, 1, 0), pairs + ones

    ctl_ref[AT_COUNT] = lax.fori_loop(0, BLK, entry, (0, 0))[1]


def make_plan(key_blocks, counts):
    vmem = pl.BlockSpec(memory_space=pltpu.VMEM)
    return pl.pallas_call(
        plan_kernel,
        out_shape=(jax.ShapeDtypeStruct((CTL,), jnp.int32), jax.ShapeDtypeStruct((1,), jnp.int32)),
        in_specs=[vmem, vmem],
        out_specs=[pl.BlockSpec(memory_space=pltpu.SMEM)] * 2,
        scratch_shapes=[
            pltpu.VMEM((48, BLK), jnp.int32),
            pltpu.SMEM((48, BLK), jnp.int32),
            pltpu.SMEM((BLK,), jnp.int32),
            pltpu.SMEM((BLK,), jnp.int32),
            pltpu.SemaphoreType.DMA,
        ],
    )(key_blocks, counts)


def route_kernel(
    steps, kv_steps,
    ctl_ref, q_ref, k_ref, v_ref, g_ref,
    att_ref, dq_ref, own_kv, pack_ref, stats_ref,
    own_qg, row_kv, row_qg, far_kv, far_qg, recv_ref, late_ref, send_ref, kcat, vcat, probs, dots, mine_stats,
    head_send, head_recv, own_sem, x_send, x_recv, z_send, z_recv, s_send, s_recv,
):
    seq = lax.axis_index("seq")
    head = lax.axis_index("head")
    x, z = lax.rem(seq, NX), seq // NX

    def chip(cx, cz):
        return lax.rem(cz + 2 * NZ, NZ) * NX + lax.rem(cx + 2 * NX, NX)

    barrier = pltpu.get_barrier_semaphore()
    for shift in range(1, NH):
        pl.semaphore_signal(barrier, inc=1, device_id={"seq": seq, "head": lax.rem(head + shift, NH)}, device_id_type=MESH)
    for (cx, cz) in ((x + 1, z), (x - 1, z), (x, z + 1), (x, z - 1)):
        pl.semaphore_signal(barrier, inc=1, device_id={"seq": chip(cx, cz), "head": head}, device_id_type=MESH)
    pl.semaphore_wait(barrier, NH - 1 + 4)

    targets = ((k_ref, own_kv, 0), (v_ref, own_kv, 1), (q_ref, own_qg, 0), (g_ref, own_qg, 1))

    def rows_of(dst, which, h):
        start = pl.multiple_of(which * BLK + lax.rem(h, 2) * CHUNK, CHUNK)
        return dst.at[h // 2, pl.ds(start, CHUNK), :]

    def columns_of(src, h):
        return src.at[:, pl.ds(pl.multiple_of(h * HD, HD), HD)]

    def head_copy(array, peer_from, peer_to, shift):
        src, dst, which = targets[array]
        return pltpu.make_async_remote_copy(
            src_ref=columns_of(src, peer_to),
            dst_ref=rows_of(dst, which, peer_from),
            send_sem=head_send.at[array, shift],
            recv_sem=head_recv.at[array, shift],
            device_id={"seq": seq, "head": peer_to},
            device_id_type=MESH,
        )

    started = []
    own_copies = []
    for array, (src, dst, which) in enumerate(targets):
        for shift in range(1, NH):
            copy = head_copy(array, head, lax.rem(head + shift, NH), shift)
            copy.start()
            started.append(copy)
        own = pltpu.make_async_copy(columns_of(src, head), rows_of(dst, which, head), own_sem.at[array])
        own.start()
        own_copies.append(own)

    def wait_head(array):
        for shift in range(1, NH):
            peer = lax.rem(head + NH - shift, NH)
            head_copy(array, peer, peer, shift).wait_recv()
        own_copies[array].wait()

    owned = (own_kv, own_qg)
    rows = (row_kv, row_qg)
    x_plan = ((1, 0, 0), (-1, 0, 2), (1, 0, 2), (-1, 0, 0), (1, 1, 0), (-1, -1, 2))

    def x_copy(kind, i, arriving):
        sign, offset, first = x_plan[i]
        origin = lax.rem(x - offset - (sign if arriving else 0) + 2 * NX, NX)
        piece = rows[kind].at[pl.ds(4 * origin + first, 2)]
        landed = (far_kv, far_qg)[kind].at[pl.ds(first, 2)] if offset != 0 else piece
        other = chip(x - sign, z) if arriving else chip(x + sign, z)
        return pltpu.make_async_remote_copy(
            src_ref=landed if arriving else piece if offset != 0 else owned[kind].at[pl.ds(first, 2)],
            dst_ref=landed, send_sem=x_send.at[kind, i], recv_sem=x_recv.at[kind, i],
            device_id={"seq": other, "head": head}, device_id_type=MESH,
        )

    def x_start(kind, i):
        copy = x_copy(kind, i, False)
        copy.start()
        started.append(copy)

    def landing(t, half):
        return recv_ref.at[2 * t + half] if t < kv_steps else late_ref.at[2 * (t - kv_steps) + half]

    def z_copy(half, t, part, arriving):
        sign = 1 if half == 0 else -1
        other = chip(x, z - sign) if arriving else chip(x, z + sign)
        slot = 2 * t + half
        rows = slice(part * BLK, part * BLK + BLK)
        return pltpu.make_async_remote_copy(
            src_ref=send_ref.at[slot, rows], dst_ref=landing(t, half).at[rows],
            send_sem=z_send.at[slot, part], recv_sem=z_recv.at[slot, part],
            device_id={"seq": other, "head": head}, device_id_type=MESH,
        )

    scale = 1.0 / math.sqrt(HD)
    key_at = lax.broadcasted_iota(jnp.int32, (1, 8 * BLK), 1)

    def attend_block(i):
        for t in range(8):
            code = ctl_ref[AT_CODE + i * 8 + t]
            near = row_kv[jnp.minimum(code, 15)]
            moved = recv_ref[jnp.clip(code - 16, 0, 2 * kv_steps - 1)]
            data = lax.select(code < 16, near, moved)
            kcat[t * BLK : (t + 1) * BLK, :] = data[0:BLK]
            vcat[t * BLK : (t + 1) * BLK, :] = data[BLK : 2 * BLK]
        q, g = own_qg[i, 0:BLK], own_qg[i, BLK : 2 * BLK]
        s = dot_nt(q, kcat[...]) * scale + jnp.where(key_at < ctl_ref[AT_USED + i] * BLK, 0.0, NEG)
        row_max = jnp.max(s, axis=1, keepdims=True)
        w = jnp.exp(s - row_max)
        row_sum = jnp.sum(w, axis=1, keepdims=True)
        scaled = 1.0 / row_sum
        att = (dot_nn(w.astype(BF16), vcat[...]) * scaled).astype(BF16)
        total = row_max + jnp.log(row_sum)
        grad_dot = jnp.sum(g.astype(F32) * att.astype(F32), axis=1, keepdims=True)
        probs[...] = w * scaled
        dots[...] = jnp.broadcast_to(grad_dot, (BLK, BLK))
        att_ref[i * BLK : (i + 1) * BLK, :] = att
        mine_stats[i : i + 1, :] = jnp.transpose(jnp.broadcast_to(total, (BLK, BLK)))[0:1, :]
        mine_stats[i + 4 : i + 5, :] = jnp.transpose(jnp.broadcast_to(grad_dot, (BLK, BLK)))[0:1, :]

    def query_grad(i):
        g = own_qg[i, BLK : 2 * BLK]
        ds = (probs[...] * (dot_nt(g, vcat[...]) - dots[:, 0:1])).astype(BF16)
        dq_ref[i * BLK : (i + 1) * BLK, :] = (dot_nn(ds, kcat[...]) * scale).astype(BF16)

    def stat_copy(shift, origin, target):
        return pltpu.make_async_remote_copy(
            src_ref=mine_stats, dst_ref=stats_ref.at[origin], send_sem=s_send.at[shift], recv_sem=s_recv.at[shift],
            device_id={"seq": target, "head": head}, device_id_type=MESH,
        )

    def keep_own(kind):
        for i in range(4):
            rows[kind][4 * x + i] = owned[kind][i]

    def keep_far(kind):
        for i in range(4, 6):
            x_copy(kind, i, True).wait_recv()
        for i in range(4):
            rows[kind][4 * lax.rem(x + 2, NX) + i] = (far_kv, far_qg)[kind][i]

    wait_head(0)
    wait_head(1)
    for i in range(4):
        x_start(0, i)

    work = []
    for i in range(4):
        work.append(functools.partial(attend_block, i))
        work.append(functools.partial(query_grad, i))

    def send_stats():
        for shift in range(1, NX * NZ):
            copy = stat_copy(shift, seq, lax.rem(seq + shift, NX * NZ))
            copy.start()
            started.append(copy)
        own = pltpu.make_async_copy(mine_stats, stats_ref.at[seq], s_recv.at[0])
        own.start()
        own_copies.append(own)

    for t in range(steps):
        if t == PASS_KV:
            wait_head(2)
            wait_head(3)
            x_copy(0, 0, True).wait_recv()
            x_start(0, 4)
            x_copy(0, 1, True).wait_recv()
            x_start(0, 5)
            for i in range(4):
                x_start(1, i)
            keep_own(0)
            keep_own(1)
        elif t == NEAR_KV:
            for i in range(2, 4):
                x_copy(0, i, True).wait_recv()
        elif t == ALL_KV:
            keep_far(0)
        elif t == PASS_QG:
            x_copy(1, 0, True).wait_recv()
            x_start(1, 4)
            x_copy(1, 1, True).wait_recv()
            x_start(1, 5)
        elif t == NEAR_QG:
            for i in range(2, 4):
                x_copy(1, i, True).wait_recv()
        elif t == ALL_QG:
            keep_far(1)
        for part in range(2):
            rows_at = slice(part * BLK, part * BLK + BLK)
            for half in range(2):
                slot = 2 * t + half
                value = ctl_ref[slot]
                size = jnp.abs(value)
                index = (127 - (size & 127)) & 15
                data = row_kv[index, rows_at] if t >= NEAR_KV else own_kv[index & 3, rows_at]
                if t >= OWN_QG:
                    other = row_qg[index, rows_at] if t >= NEAR_QG else own_qg[index & 3, rows_at]
                    data = lax.select(size >= 2048, data, other)
                if t >= LAG:
                    z_copy(half, t - LAG, part, True).wait_recv()
                    data = lax.select(value < 0, landing(t - LAG, half)[rows_at], data)
                send_ref[slot, rows_at] = data
            for half in range(2):
                copy = z_copy(half, t, part, False)
                copy.start()
                started.append(copy)
        if t >= kv_steps + LAG:
            if work:
                work.pop(0)()
                if not work:
                    send_stats()
    for t in range(steps - LAG, steps):
        for half in range(2):
            for part in range(2):
                z_copy(half, t, part, True).wait_recv()
    while work:
        work.pop(0)()
        if not work:
            send_stats()
    for n in range(PACK):
        code = ctl_ref[AT_LIST + n]
        data = lax.select(code < 16, row_qg[jnp.clip(code, 0, 15)], recv_ref[jnp.clip(code - 16, 0, 2 * kv_steps - 1)])
        last = 16 + 2 * kv_steps
        pack_ref[n] = lax.select(code < last, data, late_ref[jnp.clip(code - last, 0, 2 * (steps - kv_steps) - 1)])
    for shift in range(1, NX * NZ):
        peer = lax.rem(seq + NX * NZ - shift, NX * NZ)
        stat_copy(shift, peer, peer).wait_recv()
    own_copies[-1].wait()
    for copy in started:
        copy.wait_send()


def route(variant, ctl, queries, keys, values, out_grad):
    steps, kv_steps = VARIANTS[variant]
    smem = pl.BlockSpec(memory_space=pltpu.SMEM)
    vmem = pl.BlockSpec(memory_space=pltpu.VMEM)
    out = jax.ShapeDtypeStruct((ROWS, HD), BF16)
    own = (4, 2 * BLK, HD)
    near = (16, 2 * BLK, HD)
    moved = (2 * steps, 2 * BLK, HD)
    early = (2 * kv_steps, 2 * BLK, HD)
    late = (2 * (steps - kv_steps), 2 * BLK, HD)
    stats = jax.ShapeDtypeStruct((NX * NZ, 8, BLK), F32)
    dma = pltpu.SemaphoreType.DMA
    return pl.pallas_call(
        functools.partial(route_kernel, steps, kv_steps),
        out_shape=(out, out, jax.ShapeDtypeStruct(own, BF16), jax.ShapeDtypeStruct((PACK, 2 * BLK, HD), BF16), stats),
        in_specs=[smem] + [vmem] * 4,
        out_specs=[vmem] * 5,
        scratch_shapes=[
            pltpu.VMEM(own, BF16),
            pltpu.VMEM(near, BF16),
            pltpu.VMEM(near, BF16),
            pltpu.VMEM(own, BF16),
            pltpu.VMEM(own, BF16),
            pltpu.VMEM(early, BF16),
            pltpu.VMEM(late, BF16),
            pltpu.VMEM(moved, BF16),
            pltpu.VMEM((8 * BLK, HD), BF16),
            pltpu.VMEM((8 * BLK, HD), BF16),
            pltpu.VMEM((BLK, 8 * BLK), F32),
            pltpu.VMEM((BLK, BLK), F32),
            pltpu.VMEM((8, BLK), F32),
            dma((4, NH)), dma((4, NH)), dma((4,)),
            dma((2, 6)), dma((2, 6)),
            dma((2 * steps, 2)), dma((2 * steps, 2)),
            dma((NX * NZ,)), dma((NX * NZ,)),
        ],
        compiler_params=pltpu.CompilerParams(collective_id=1 + variant, has_side_effects=True),
    )(ctl, queries, keys, values, out_grad)


def keys_kernel(ctl_ref, kv_ref, pack_ref, stats_ref, att_ref, dq_ref, att_out, dq_out, dk_ref, dv_ref, dk_acc, dv_acc):
    scale = 1.0 / math.sqrt(HD)
    att_out[...] = att_ref[...]
    dq_out[...] = dq_ref[...]
    dk_acc[...] = jnp.zeros_like(dk_acc)
    dv_acc[...] = jnp.zeros_like(dv_acc)
    pairs = ctl_ref[AT_COUNT]

    def trip(i, carry):
        sums = []
        for u in range(GROUP):
            at = GROUP * i + u
            word = ctl_ref[AT_PAIRS + jnp.minimum(at, pairs - 1)]
            n, a, j = word & 255, (word >> 8) & 255, word >> 16
            unused = jnp.where(at < pairs, 0.0, 1e30)
            q, g = pack_ref[n, 0:BLK, :], pack_ref[n, BLK : 2 * BLK, :]
            total = stats_ref[a // 4, pl.ds(lax.rem(a, 4), 1), :] + unused
            grad_dot = stats_ref[a // 4, pl.ds(lax.rem(a, 4) + 4, 1), :]
            p = jnp.exp(dot_nt(kv_ref[j, 0:BLK, :], q) * scale - total)
            ds = (p * (dot_nt(kv_ref[j, BLK : 2 * BLK, :], g) - grad_dot)).astype(BF16)
            sums.append((j, dot_nn(ds, q), dot_nn(p.astype(BF16), g)))
        for j, dk, dv in sums:
            dk_acc[j] += dk
            dv_acc[j] += dv
        return carry

    lax.fori_loop(0, (pairs + GROUP - 1) // GROUP, trip, 0)
    for j in range(4):
        dk_ref[j * BLK : (j + 1) * BLK, :] = (dk_acc[j] * scale).astype(BF16)
        dv_ref[j * BLK : (j + 1) * BLK, :] = dv_acc[j].astype(BF16)


def key_grads(ctl, kv, pack, stats, att, dq):
    smem = pl.BlockSpec(memory_space=pltpu.SMEM)
    vmem = pl.BlockSpec(memory_space=pltpu.VMEM)
    out = jax.ShapeDtypeStruct((ROWS, HD), BF16)
    return pl.pallas_call(
        keys_kernel,
        out_shape=(out,) * 4,
        in_specs=[smem] + [vmem] * 5,
        out_specs=[vmem] * 4,
        scratch_shapes=[
            pltpu.VMEM((4, BLK, HD), F32),
            pltpu.VMEM((4, BLK, HD), F32),
        ],
    )(ctl, kv, pack, stats, att, dq)


def on_device(queries, keys, values, out_grad, key_blocks, counts):
    seq = lax.axis_index("seq")
    ctl, choice = make_plan(jnp.transpose(key_blocks), counts[None, :])

    def sparse(variant):
        att, dq, kv, pack, stats = route(variant, ctl, queries, keys, values, out_grad)
        return tuple(key_grads(ctl, kv, pack, stats, att, dq))

    def dense():
        kv, qg = exchange(queries, keys, values, out_grad)
        live = jnp.arange(key_blocks.shape[1])[None, :] < counts[:, None]
        touch = jnp.any(live & (key_blocks // 4 == seq), axis=1)
        touch = (touch & (jnp.arange(key_blocks.shape[0]) // 4 != seq)).astype(jnp.int32)
        first = (seq * 4).reshape(1).astype(jnp.int32)
        return tuple(attend(first, touch, key_blocks, counts, kv, qg))

    branches = [functools.partial(sparse, variant) for variant in range(len(VARIANTS))] + [dense]
    return lax.switch(choice[0], branches)


def solution(mesh):
    rows = P(("seq", "head"), None)
    out = P("seq", "head")
    return jax.shard_map(
        on_device,
        mesh=mesh,
        in_specs=(rows,) * 4 + (P(), P()),
        out_specs=(out,) * 4,
        check_vma=False,
    )
```

```python
import functools
import heapq
import math

import jax
import jax.numpy as jnp
from jax import lax
from jax.experimental import pallas as pl
from jax.experimental.pallas import tpu as pltpu
from jax.sharding import PartitionSpec as P

MESH = pl.DeviceIdType.MESH
BLK = 128
HD = 128
NX = 4
NZ = 8
NH = 8
ROWS = 512
CHUNK = 64
SPLIT = 208
BF16 = jnp.bfloat16
F32 = jnp.float32
NEG = -1e30


def row_range(part):
    half_a, half_b = SPLIT // 32 * 16, SPLIT + (ROWS - SPLIT) // 32 * 16
    return {
        "A": (0, SPLIT),
        "A0": (0, half_a),
        "A1": (half_a, SPLIT),
        "B": (SPLIT, ROWS),
        "B0": (SPLIT, half_b),
        "B1": (half_b, ROWS),
    }[part]


def ring_sends(axis, sources, size, out, kind, prio):
    far = size // 2
    arrived = []
    for (offset, part, dep) in sources:
        if len(part) == 1:
            arrived.append((offset, part, dep))
            halves = [(part, +1, far - 1), (part, -1, far - 1)]
        else:
            arrived.append((offset, part, dep))
            sign = +1 if part[1] == "0" else -1
            halves = [(part, +1, far - 1), (part, -1, far - 1)]
        for (piece, sign, hops) in halves:
            last = dep
            at = offset
            for hop in range(1, hops + 1):
                out.append(dict(kind=kind, axis=axis, sign=sign, origin=at, part=piece, dep=last, left=far - hop, prio=prio))
                last = len(out) - 1
                at = step_offset(at, axis, sign)
                arrived.append((at, piece, last))
            for digit, way in (("0", +1), ("1", -1)):
                if way != sign:
                    continue
                tail = piece if len(piece) == 2 else piece + digit
                if tail[1] != digit:
                    continue
                out.append(dict(kind=kind, axis=axis, sign=sign, origin=at, part=tail, dep=last, left=0, prio=prio))
                arrived.append((step_offset(at, axis, sign), tail, len(out) - 1))
    return arrived


def step_offset(offset, axis, sign):
    ox, oz = offset
    return (ox + sign, oz) if axis == "x" else (ox, oz + sign)


def plan_sends():
    out = []
    for kind in (0, 1):
        own = -1 - kind
        first_a = ring_sends("x", [((0, 0), "A", own)], NX, out, kind, kind * 10)
        first_b = ring_sends("z", [((0, 0), "B", own)], NZ, out, kind, kind * 10)
        ring_sends("z", first_a, NZ, out, kind, kind * 10 + 1)
        ring_sends("x", first_b, NX, out, kind, kind * 10 + 1)
    rate = 46.0e3 * 1.0
    latency = 1.7
    ready_own = {-1: 4.0, -2: 8.0}
    arrival = {}
    free = {}
    start = {}
    waiting = {}
    events = []
    for i, m in enumerate(out):
        if m["dep"] < 0:
            heapq.heappush(events, (ready_own[m["dep"]], i))
    children = {}
    for i, m in enumerate(out):
        if m["dep"] >= 0:
            children.setdefault(m["dep"], []).append(i)
    queues = {("x", 1): [], ("x", -1): [], ("z", 1): [], ("z", -1): []}
    free = {k: 0.0 for k in queues}
    order = []
    while events or any(queues.values()):
        options = []
        for k, q in queues.items():
            if q:
                options.append((max(free[k], q[0][2]), k))
        next_link = min(options) if options else None
        if events and (next_link is None or events[0][0] <= next_link[0]):
            t, i = heapq.heappop(events)
            m = out[i]
            q = queues[(m["axis"], m["sign"])]
            q.append((m["prio"] // 10, -m["left"], t, i))
            q.sort(key=lambda e: (e[0], e[1], e[2], e[3]))
            continue
        t, k = next_link
        _, _, ready, i = queues[k].pop(0)
        m = out[i]
        lo, hi = row_range(m["part"])
        begin = max(free[k], ready)
        free[k] = begin + (hi - lo) * HD * 2 * 2 / rate
        start[i] = begin
        order.append((begin, ready, i))
        for c in children.get(i, []):
            heapq.heappush(events, (free[k] + latency, c))
    order.sort()
    return out, [i for (_, _, i) in order], max(free.values())


SENDS, ORDER, SPAN = plan_sends()


def exchange_kernel(q_ref, k_ref, v_ref, g_ref, kv_ref, qg_ref, send_sem, recv_sem, head_send, head_recv, own_sem):
    seq = lax.axis_index("seq")
    head = lax.axis_index("head")
    x, z = lax.rem(seq, NX), seq // NX

    def chip(cx, cz):
        return lax.rem(cz + 2 * NZ, NZ) * NX + lax.rem(cx + 2 * NX, NX)

    barrier = pltpu.get_barrier_semaphore()
    for shift in range(1, NH):
        pl.semaphore_signal(barrier, inc=1, device_id={"seq": seq, "head": lax.rem(head + shift, NH)}, device_id_type=MESH)
    for (cx, cz) in ((x + 1, z), (x - 1, z), (x, z + 1), (x, z - 1)):
        pl.semaphore_signal(barrier, inc=1, device_id={"seq": chip(cx, cz), "head": head}, device_id_type=MESH)
    pl.semaphore_wait(barrier, NH - 1 + 4)

    targets = ((k_ref, kv_ref, 0), (v_ref, kv_ref, 1), (q_ref, qg_ref, 0), (g_ref, qg_ref, 1))

    def rows_of(dst, which, h):
        return dst.at[seq, which, pl.ds(pl.multiple_of(h * CHUNK, CHUNK), CHUNK), :]

    def columns_of(src, h):
        return src.at[:, pl.ds(pl.multiple_of(h * HD, HD), HD)]

    head_copies = []
    own_copies = []
    for array, (src, dst, which) in enumerate(targets):
        for shift in range(1, NH):
            peer = lax.rem(head + shift, NH)
            copy = pltpu.make_async_remote_copy(
                src_ref=columns_of(src, peer),
                dst_ref=rows_of(dst, which, head),
                send_sem=head_send.at[array, shift],
                recv_sem=head_recv.at[array, shift],
                device_id={"seq": seq, "head": peer},
                device_id_type=MESH,
            )
            copy.start()
            head_copies.append(copy)
        own = pltpu.make_async_copy(columns_of(src, head), rows_of(dst, which, head), own_sem.at[array])
        own.start()
        own_copies.append(own)

    def wait_head(array):
        src, dst, which = targets[array]
        for shift in range(1, NH):
            peer = lax.rem(head + NH - shift, NH)
            pltpu.make_async_remote_copy(
                src_ref=columns_of(src, peer),
                dst_ref=rows_of(dst, which, peer),
                send_sem=head_send.at[array, shift],
                recv_sem=head_recv.at[array, shift],
                device_id={"seq": seq, "head": peer},
                device_id_type=MESH,
            ).wait_recv()
        own_copies[array].wait()

    buffers = (kv_ref, qg_ref)

    def piece(m, ox, oz):
        lo, hi = row_range(m["part"])
        return buffers[m["kind"]].at[chip(x - ox, z - oz), :, lo:hi, :]

    def send(i):
        m = SENDS[i]
        ox, oz = m["origin"]
        target = chip(x + m["sign"], z) if m["axis"] == "x" else chip(x, z + m["sign"])
        return pltpu.make_async_remote_copy(
            src_ref=piece(m, ox, oz),
            dst_ref=piece(m, ox, oz),
            send_sem=send_sem.at[i],
            recv_sem=recv_sem.at[i],
            device_id={"seq": target, "head": head},
            device_id_type=MESH,
        )

    def wait_recv(i):
        m = SENDS[i]
        ox, oz = step_offset(m["origin"], m["axis"], m["sign"])
        source = chip(x - m["sign"], z) if m["axis"] == "x" else chip(x, z - m["sign"])
        pltpu.make_async_remote_copy(
            src_ref=piece(m, ox, oz),
            dst_ref=piece(m, ox, oz),
            send_sem=send_sem.at[i],
            recv_sem=recv_sem.at[i],
            device_id={"seq": source, "head": head},
            device_id_type=MESH,
        ).wait_recv()

    ready = set()
    started = []
    for i in ORDER:
        dep = SENDS[i]["dep"]
        if dep not in ready:
            ready.add(dep)
            if dep < 0:
                wait_head(2 * (-1 - dep))
                wait_head(2 * (-1 - dep) + 1)
            else:
                wait_recv(dep)
        copy = send(i)
        copy.start()
        started.append(copy)
    for i in ORDER:
        if i not in ready:
            wait_recv(i)
    for copy in started:
        copy.wait_send()
    for copy in head_copies:
        copy.wait_send()


def exchange(queries, keys, values, out_grad):
    shape = jax.ShapeDtypeStruct((NX * NZ, 2, ROWS, HD), BF16)
    count = len(SENDS)
    return pl.pallas_call(
        exchange_kernel,
        out_shape=(shape, shape),
        in_specs=[pl.BlockSpec(memory_space=pltpu.VMEM)] * 4,
        out_specs=[pl.BlockSpec(memory_space=pl.ANY)] * 2,
        scratch_shapes=[
            pltpu.SemaphoreType.DMA((count,)),
            pltpu.SemaphoreType.DMA((count,)),
            pltpu.SemaphoreType.DMA((4, NH)),
            pltpu.SemaphoreType.DMA((4, NH)),
            pltpu.SemaphoreType.DMA((4,)),
        ],
        compiler_params=pltpu.CompilerParams(collective_id=0, has_side_effects=True),
    )(queries, keys, values, out_grad)


def dot_nt(a, b):
    return lax.dot_general(a, b, (((1,), (1,)), ((), ())), preferred_element_type=F32)


def dot_nn(a, b):
    return lax.dot_general(a, b, (((1,), (0,)), ((), ())), preferred_element_type=F32)


def dot_tn(a, b):
    return lax.dot_general(a, b, (((0,), (0,)), ((), ())), preferred_element_type=F32)


def attend_kernel(first_ref, touch_ref, blocks_ref, counts_ref, kv_ref, qg_ref, att_ref, dq_ref, dk_ref, dv_ref, s_ref, acc_ref, dk_acc, dv_acc):
    scale = 1.0 / math.sqrt(HD)
    dk_acc[...] = jnp.zeros_like(dk_acc)
    dv_acc[...] = jnp.zeros_like(dv_acc)
    first = first_ref[0]

    def load(ref, which, block):
        return ref[block // 4, which, pl.ds(pl.multiple_of(lax.rem(block, 4) * BLK, BLK), BLK), :]

    def query_block(a, local):
        count = counts_ref[a]
        q = load(qg_ref, 0, a)
        g = load(qg_ref, 1, a)

        def score(t, row_max):
            s = dot_nt(q, load(kv_ref, 0, blocks_ref[a, t])) * scale
            s_ref[t] = s
            return jnp.maximum(row_max, jnp.max(s, axis=1, keepdims=True))

        row_max = lax.fori_loop(0, count, score, jnp.full((BLK, 1), NEG, F32))
        acc_ref[...] = jnp.zeros_like(acc_ref)

        def mix(t, row_sum):
            w = jnp.exp(s_ref[t] - row_max)
            acc_ref[...] += dot_nn(w.astype(BF16), load(kv_ref, 1, blocks_ref[a, t]))
            return row_sum + jnp.sum(w, axis=1, keepdims=True)

        row_sum = lax.fori_loop(0, count, mix, jnp.zeros((BLK, 1), F32))
        att = (acc_ref[...] / row_sum).astype(BF16)
        total = row_max + jnp.log(row_sum)
        grad_dot = jnp.sum(g.astype(F32) * att.astype(F32), axis=1, keepdims=True)

        def pair(t):
            block = blocks_ref[a, t]
            p = jnp.exp(s_ref[t] - total)
            dp = dot_nt(g, load(kv_ref, 1, block))
            return block, p, (p * (dp - grad_dot)).astype(BF16)

        def add_key(slot, p, ds):
            dk_acc[slot] += dot_tn(ds, q)
            dv_acc[slot] += dot_tn(p.astype(BF16), g)

        if local:
            acc_ref[...] = jnp.zeros_like(acc_ref)

            def back(t, carry):
                block, p, ds = pair(t)
                acc_ref[...] += dot_nn(ds, load(kv_ref, 0, block))
                slot = block - first

                @pl.when((slot >= 0) & (slot < 4))
                def _():
                    add_key(slot, p, ds)

                return carry

            lax.fori_loop(0, count, back, 0)
            rows = pl.ds(pl.multiple_of((a - first) * BLK, BLK), BLK)
            att_ref[rows, :] = att
            dq_ref[rows, :] = (acc_ref[...] * scale).astype(BF16)
        else:

            def back(t, carry):
                slot = blocks_ref[a, t] - first

                @pl.when((slot >= 0) & (slot < 4))
                def _():
                    _, p, ds = pair(t)
                    add_key(slot, p, ds)

                return carry

            lax.fori_loop(0, count, back, 0)

    def own(i, carry):
        query_block(first + i, True)
        return carry

    lax.fori_loop(0, 4, own, 0)

    def other(a, carry):
        @pl.when(touch_ref[a] > 0)
        def _():
            query_block(a, False)

        return carry

    lax.fori_loop(0, 128, other, 0)
    for slot in range(4):
        dk_ref[slot * BLK : (slot + 1) * BLK, :] = (dk_acc[slot] * scale).astype(BF16)
        dv_ref[slot * BLK : (slot + 1) * BLK, :] = dv_acc[slot].astype(BF16)


def attend(first, touch, key_blocks, counts, kv, qg):
    shape = jax.ShapeDtypeStruct((ROWS, HD), BF16)
    smem = pl.BlockSpec(memory_space=pltpu.SMEM)
    vmem = pl.BlockSpec(memory_space=pltpu.VMEM)
    return pl.pallas_call(
        attend_kernel,
        out_shape=(shape,) * 4,
        in_specs=[smem] * 4 + [vmem] * 2,
        out_specs=[vmem] * 4,
        scratch_shapes=[
            pltpu.VMEM((8, BLK, BLK), F32),
            pltpu.VMEM((BLK, HD), F32),
            pltpu.VMEM((4, BLK, HD), F32),
            pltpu.VMEM((4, BLK, HD), F32),
        ],
    )(first, touch, key_blocks, counts, kv, qg)


LAG = 2
STEPS = 34
VARIANTS = ((25, 21), (28, 24), (34, 30))
PACK = 24
GROUP = 4
OWN_QG = 4
PASS_KV = 4
NEAR_KV = 6
ALL_KV = 8
PASS_QG = 10
NEAR_QG = 12
ALL_QG = 14
CTL = 2048
AT_CODE = 128
AT_PICK = 160
AT_COUNT = 161
AT_USED = 164
AT_LIST = 256
AT_PAIRS = 1024


def plan_kernel(blocks_ref, counts_ref, ctl_ref, pick_ref, words_ref, words, where_kv, where_qg, sem):
    seq = lax.axis_index("seq")
    x, z = lax.rem(seq, NX), seq // NX
    brow = lax.broadcasted_iota(jnp.int32, (BLK, BLK), 0)
    count = counts_ref[...]
    hits = jnp.zeros((BLK, BLK), F32)
    for t in range(8):
        hits = jnp.where((blocks_ref[t : t + 1, :] == brow) & (count > t), 1.0, hits)
    row = lax.broadcasted_iota(jnp.int32, (32, BLK), 0)
    col = lax.broadcasted_iota(jnp.int32, (32, BLK), 1)
    device = lax.rem(row, NZ) * NX + row // NZ
    group = jnp.where(col // 4 == device, 1.0, 0.0)
    need_kv = dot_nt(group, hits)
    need_qg = dot_nn(group, hits)
    jrow = lax.broadcasted_iota(jnp.int32, (8, BLK), 0)
    jcol = lax.broadcasted_iota(jnp.int32, (8, BLK), 1)
    mine = jcol - seq * 4
    power = jnp.where(mine == 0, 1.0, jnp.where(mine == 1, 2.0, jnp.where(mine == 2, 4.0, jnp.where(mine == 3, 8.0, 0.0))))
    quad = lax.rem(lax.broadcasted_iota(jnp.int32, (BLK, BLK), 1), 4)
    digit = jnp.where(quad == 0, 1.0, jnp.where(quad == 1, 16.0, jnp.where(quad == 2, 256.0, 4096.0)))
    digit = jnp.where(lax.broadcasted_iota(jnp.int32, (BLK, BLK), 1) // 4 == brow, digit, 0.0)
    bits = dot_nt(dot_nn(power, hits), digit)

    origin = jcol // 16
    source_x = lax.rem(jcol, 16) // 4
    delta = lax.rem(jrow - origin + NZ, NZ)
    near = (delta >= 1) & (delta < 4)
    back = delta > 4
    tie = delta == 4
    far = delta.astype(F32)
    ident = (127 - jcol).astype(F32)
    here = origin == jrow

    chains = []
    for column in range(NX):
        parts = [need[column * NZ : (column + 1) * NZ, :] > 0.5 for need in (need_kv, need_qg)]
        lean = jnp.zeros((8, BLK), F32)
        for part in parts:
            lean = lean + jnp.where(part & near, 1.0, 0.0) - jnp.where(part & back, 1.0, 0.0)
        lean = jnp.broadcast_to(jnp.sum(lean, axis=1, keepdims=True), (8, BLK))
        ahead = near | (tie & (lean < 0.0))
        behind = back | (tie & (lean >= 0.0))
        for sign in (1, -1):
            keys = []
            for part, base in zip(parts, (2048.0, 0.0)):
                hop = jnp.where(part & ahead, far, 0.0) if sign == 1 else jnp.where(part & behind, 8.0 - far, 0.0)
                most = jnp.max(hop, axis=0, keepdims=True)
                keys.append(jnp.where(here & (most > 0.5), most * 128.0 + base + ident, 0.0))
            chains.append(dict(sign=sign, column=column, keys=keys, sent=[]))
    zero = jnp.zeros((8, BLK), F32)
    last_any, last_kv = zero, zero
    marks = [zero, zero]
    ours = [x == column for column in range(NX)]
    for t in range(STEPS):
        chosen = [zero, zero]
        for c in chains:
            apart = lax.rem(source_x - c["column"] + NX, NX)
            own, close = apart == 0, apart != 2
            if t >= LAG:
                passing = pltpu.roll(c["sent"][t - LAG], 1 if c["sign"] == 1 else 7, 0) - 128.0
                left = jnp.where(passing >= 2048.0, passing - 2048.0, passing)
                through = left > 127.5
            kv, qg = c["keys"]
            best = kv if t >= ALL_KV else jnp.where(close if t >= NEAR_KV else own, kv, 0.0)
            if t >= OWN_QG:
                best = jnp.maximum(best, qg if t >= ALL_QG else jnp.where(close if t >= NEAR_QG else own, qg, 0.0))
            best = jnp.broadcast_to(jnp.max(best, axis=1, keepdims=True), (8, BLK))
            if t >= LAG:
                taken = jnp.where(through, -1.0, best)
                sent = jnp.where(through, passing, best)
                mark = jnp.where(through, -passing, best)
            else:
                taken, sent, mark = best, best, best
            c["keys"] = [jnp.where(k == taken, 0.0, k) for k in c["keys"]]
            c["sent"].append(sent)
            last_any = jnp.where(sent > 0.0, t + 1.0, last_any)
            last_kv = jnp.where(sent >= 2048.0, t + 1.0, last_kv)
            half = 0 if c["sign"] == 1 else 1
            chosen[half] = jnp.where(ours[c["column"]], mark, chosen[half])
        for half in range(2):
            marks[half] = jnp.where(jcol == t, chosen[half], marks[half])
    for c in chains:
        last_any = jnp.where((c["keys"][0] + c["keys"][1]) > 0.0, 999.0, last_any)
        for t in range(STEPS - LAG, STEPS):
            sent = c["sent"][t]
            left = jnp.where(sent >= 2048.0, sent - 2048.0, sent)
            last_any = jnp.where(left > 255.5, 999.0, last_any)
    last_any = jnp.max(jnp.max(last_any, axis=1, keepdims=True), axis=0, keepdims=True)
    last_kv = jnp.max(jnp.max(last_kv, axis=1, keepdims=True), axis=0, keepdims=True)
    index = jnp.zeros((1, 1), F32)
    for steps, kv_steps in VARIANTS:
        index = index + jnp.where((last_any > steps + 0.5) | (last_kv > kv_steps + 0.5), 1.0, 0.0)
    crowd = jnp.max(jnp.sum(jnp.where(need_qg > 0.5, 1.0, 0.0), axis=1, keepdims=True), axis=0, keepdims=True)
    index = jnp.where(crowd > PACK + 0.5, float(len(VARIANTS)), index)
    words_ref[0:8, :] = marks[0].astype(jnp.int32)
    words_ref[8:16, :] = marks[1].astype(jnp.int32)
    words_ref[16:24, :] = bits.astype(jnp.int32)
    words_ref[24:32, :] = blocks_ref[...]
    words_ref[32:40, :] = jnp.broadcast_to(count, (8, BLK))
    words_ref[40:48, :] = jnp.broadcast_to(index, (8, BLK)).astype(jnp.int32)
    copy = pltpu.make_async_copy(words_ref, words, sem)
    copy.start()
    copy.wait()

    pick_ref[0] = words[40, 0]
    for i in range(16):
        where_kv[z * 16 + i] = i
        where_qg[z * 16 + i] = i
    sources = (lax.rem(z + NZ - 1, NZ), lax.rem(z + 1, NZ))

    def slot(t, carry):
        for half in range(2):
            ctl_ref[2 * t + half] = words[half * 8 + z, t]
            value = jnp.abs(words[half * 8 + sources[half], t])
            block = 127 - (value & 127)
            spot = 16 + 2 * t + half

            @pl.when(value >= 2048)
            def _():
                where_kv[block] = spot

            @pl.when((value >= 128) & (value < 2048))
            def _():
                where_qg[block] = spot

        return carry

    lax.fori_loop(0, STEPS, slot, 0)
    for i in range(4):
        live = words[32, 4 * seq + i]
        ctl_ref[AT_USED + i] = live
        for t in range(8):
            block = jnp.where(t < live, words[24 + t, 4 * seq + i], 4 * seq + i)
            ctl_ref[AT_CODE + i * 8 + t] = where_kv[block]

    def entry(group, totals):
        word = words[16, group]

        def listed(totals):
            n, pairs = totals
            for r in range(4):
                a = 4 * group + r
                mask = (word >> (4 * r)) & 15
                ctl_ref[AT_LIST + n] = where_qg[a]
                for j in range(4):
                    ctl_ref[AT_PAIRS + pairs] = n + a * 256 + j * 65536
                    pairs = pairs + ((mask >> j) & 1)
                n = n + jnp.where(mask > 0, 1, 0)
            return n, pairs

        return lax.cond(word > 0, listed, lambda totals: totals, totals)

    ctl_ref[AT_COUNT] = lax.fori_loop(0, BLK // 4, entry, (0, 0))[1]


def make_plan(key_blocks, counts):
    vmem = pl.BlockSpec(memory_space=pltpu.VMEM)
    return pl.pallas_call(
        plan_kernel,
        out_shape=(jax.ShapeDtypeStruct((CTL,), jnp.int32), jax.ShapeDtypeStruct((1,), jnp.int32)),
        in_specs=[vmem, vmem],
        out_specs=[pl.BlockSpec(memory_space=pltpu.SMEM)] * 2,
        scratch_shapes=[
            pltpu.VMEM((48, BLK), jnp.int32),
            pltpu.SMEM((48, BLK), jnp.int32),
            pltpu.SMEM((BLK,), jnp.int32),
            pltpu.SMEM((BLK,), jnp.int32),
            pltpu.SemaphoreType.DMA,
        ],
    )(key_blocks, counts)


def route_kernel(
    steps, kv_steps,
    ctl_ref, q_ref, k_ref, v_ref, g_ref,
    att_ref, dq_ref, own_kv, pack_ref, stats_ref,
    own_qg, row_kv, row_qg, far_kv, far_qg, recv_ref, late_ref, send_ref, kcat, vcat, probs, dots, mine_stats,
    head_send, head_recv, own_sem, x_send, x_recv, z_send, z_recv, s_send, s_recv,
):
    seq = lax.axis_index("seq")
    head = lax.axis_index("head")
    x, z = lax.rem(seq, NX), seq // NX

    def chip(cx, cz):
        return lax.rem(cz + 2 * NZ, NZ) * NX + lax.rem(cx + 2 * NX, NX)

    barrier = pltpu.get_barrier_semaphore()
    for shift in range(1, NH):
        pl.semaphore_signal(barrier, inc=1, device_id={"seq": seq, "head": lax.rem(head + shift, NH)}, device_id_type=MESH)
    for (cx, cz) in ((x + 1, z), (x - 1, z), (x, z + 1), (x, z - 1)):
        pl.semaphore_signal(barrier, inc=1, device_id={"seq": chip(cx, cz), "head": head}, device_id_type=MESH)
    pl.semaphore_wait(barrier, NH - 1 + 4)

    targets = ((k_ref, own_kv, 0), (v_ref, own_kv, 1), (q_ref, own_qg, 0), (g_ref, own_qg, 1))

    def rows_of(dst, which, h):
        start = pl.multiple_of(which * BLK + lax.rem(h, 2) * CHUNK, CHUNK)
        return dst.at[h // 2, pl.ds(start, CHUNK), :]

    def columns_of(src, h):
        return src.at[:, pl.ds(pl.multiple_of(h * HD, HD), HD)]

    def head_copy(array, peer_from, peer_to, shift):
        src, dst, which = targets[array]
        return pltpu.make_async_remote_copy(
            src_ref=columns_of(src, peer_to),
            dst_ref=rows_of(dst, which, peer_from),
            send_sem=head_send.at[array, shift],
            recv_sem=head_recv.at[array, shift],
            device_id={"seq": seq, "head": peer_to},
            device_id_type=MESH,
        )

    started = []
    own_copies = []
    for array, (src, dst, which) in enumerate(targets):
        for shift in range(1, NH):
            copy = head_copy(array, head, lax.rem(head + shift, NH), shift)
            copy.start()
            started.append(copy)
        own = pltpu.make_async_copy(columns_of(src, head), rows_of(dst, which, head), own_sem.at[array])
        own.start()
        own_copies.append(own)

    def wait_head(array):
        for shift in range(1, NH):
            peer = lax.rem(head + NH - shift, NH)
            head_copy(array, peer, peer, shift).wait_recv()
        own_copies[array].wait()

    owned = (own_kv, own_qg)
    rows = (row_kv, row_qg)
    x_plan = ((1, 0, 0), (-1, 0, 2), (1, 0, 2), (-1, 0, 0), (1, 1, 0), (-1, -1, 2))

    def x_copy(kind, i, arriving):
        sign, offset, first = x_plan[i]
        origin = lax.rem(x - offset - (sign if arriving else 0) + 2 * NX, NX)
        piece = rows[kind].at[pl.ds(4 * origin + first, 2)]
        landed = (far_kv, far_qg)[kind].at[pl.ds(first, 2)] if offset != 0 else piece
        other = chip(x - sign, z) if arriving else chip(x + sign, z)
        return pltpu.make_async_remote_copy(
            src_ref=landed if arriving else piece if offset != 0 else owned[kind].at[pl.ds(first, 2)],
            dst_ref=landed, send_sem=x_send.at[kind, i], recv_sem=x_recv.at[kind, i],
            device_id={"seq": other, "head": head}, device_id_type=MESH,
        )

    def x_start(kind, i):
        copy = x_copy(kind, i, False)
        copy.start()
        started.append(copy)

    def landing(t, half):
        return recv_ref.at[2 * t + half] if t < kv_steps else late_ref.at[2 * (t - kv_steps) + half]

    def z_copy(half, t, part, arriving):
        sign = 1 if half == 0 else -1
        other = chip(x, z - sign) if arriving else chip(x, z + sign)
        slot = 2 * t + half
        rows = slice(part * BLK, part * BLK + BLK)
        return pltpu.make_async_remote_copy(
            src_ref=send_ref.at[slot, rows], dst_ref=landing(t, half).at[rows],
            send_sem=z_send.at[slot, part], recv_sem=z_recv.at[slot, part],
            device_id={"seq": other, "head": head}, device_id_type=MESH,
        )

    scale = 1.0 / math.sqrt(HD)
    key_at = lax.broadcasted_iota(jnp.int32, (1, 8 * BLK), 1)

    def attend_block(i):
        for t in range(8):
            code = ctl_ref[AT_CODE + i * 8 + t]
            near = row_kv[jnp.minimum(code, 15)]
            moved = recv_ref[jnp.clip(code - 16, 0, 2 * kv_steps - 1)]
            data = lax.select(code < 16, near, moved)
            kcat[i, t * BLK : (t + 1) * BLK, :] = data[0:BLK]
            vcat[i, t * BLK : (t + 1) * BLK, :] = data[BLK : 2 * BLK]
        q, g = own_qg[i, 0:BLK], own_qg[i, BLK : 2 * BLK]
        s = dot_nt(q, kcat[i]) * scale + jnp.where(key_at < ctl_ref[AT_USED + i] * BLK, 0.0, NEG)
        row_max = jnp.max(s, axis=1, keepdims=True)
        w = jnp.exp(s - row_max)
        row_sum = jnp.sum(w, axis=1, keepdims=True)
        scaled = 1.0 / row_sum
        att = (dot_nn(w.astype(BF16), vcat[i]) * scaled).astype(BF16)
        total = row_max + jnp.log(row_sum)
        grad_dot = jnp.sum(g.astype(F32) * att.astype(F32), axis=1, keepdims=True)
        probs[i] = w * scaled
        dots[i] = jnp.broadcast_to(grad_dot, (BLK, BLK))
        att_ref[i * BLK : (i + 1) * BLK, :] = att
        mine_stats[i : i + 1, :] = jnp.transpose(jnp.broadcast_to(total, (BLK, BLK)))[0:1, :]
        mine_stats[i + 4 : i + 5, :] = jnp.transpose(jnp.broadcast_to(grad_dot, (BLK, BLK)))[0:1, :]

    def query_grad(i):
        g = own_qg[i, BLK : 2 * BLK]
        ds = (probs[i] * (dot_nt(g, vcat[i]) - dots[i, :, 0:1])).astype(BF16)
        dq_ref[i * BLK : (i + 1) * BLK, :] = (dot_nn(ds, kcat[i]) * scale).astype(BF16)

    def stat_copy(shift, origin, target):
        return pltpu.make_async_remote_copy(
            src_ref=mine_stats, dst_ref=stats_ref.at[origin], send_sem=s_send.at[shift], recv_sem=s_recv.at[shift],
            device_id={"seq": target, "head": head}, device_id_type=MESH,
        )

    def keep_own(kind):
        for i in range(4):
            rows[kind][4 * x + i] = owned[kind][i]

    def keep_far(kind):
        for i in range(4, 6):
            x_copy(kind, i, True).wait_recv()
        for i in range(4):
            rows[kind][4 * lax.rem(x + 2, NX) + i] = (far_kv, far_qg)[kind][i]

    wait_head(0)
    wait_head(1)
    for i in range(4):
        x_start(0, i)

    def send_stats():
        for shift in range(1, NX * NZ):
            copy = stat_copy(shift, seq, lax.rem(seq + shift, NX * NZ))
            copy.start()
            started.append(copy)
        own = pltpu.make_async_copy(mine_stats, stats_ref.at[seq], s_recv.at[0])
        own.start()
        own_copies.append(own)

    work = [functools.partial(attend_block, i) for i in range(4)] + [send_stats]
    work += [functools.partial(query_grad, i) for i in range(4)]
    for t in range(steps):
        if t == PASS_KV:
            wait_head(2)
            wait_head(3)
            x_copy(0, 0, True).wait_recv()
            x_start(0, 4)
            x_copy(0, 1, True).wait_recv()
            x_start(0, 5)
            for i in range(4):
                x_start(1, i)
            keep_own(0)
            keep_own(1)
        elif t == NEAR_KV:
            for i in range(2, 4):
                x_copy(0, i, True).wait_recv()
        elif t == ALL_KV:
            keep_far(0)
        elif t == PASS_QG:
            x_copy(1, 0, True).wait_recv()
            x_start(1, 4)
            x_copy(1, 1, True).wait_recv()
            x_start(1, 5)
        elif t == NEAR_QG:
            for i in range(2, 4):
                x_copy(1, i, True).wait_recv()
        elif t == ALL_QG:
            keep_far(1)
        for part in range(2):
            rows_at = slice(part * BLK, part * BLK + BLK)
            for half in range(2):
                slot = 2 * t + half
                value = ctl_ref[slot]
                size = jnp.abs(value)
                index = (127 - (size & 127)) & 15
                data = row_kv[index, rows_at] if t >= NEAR_KV else own_kv[index & 3, rows_at]
                if t >= OWN_QG:
                    other = row_qg[index, rows_at] if t >= NEAR_QG else own_qg[index & 3, rows_at]
                    data = lax.select(size >= 2048, data, other)
                if t >= LAG:
                    z_copy(half, t - LAG, part, True).wait_recv()
                    data = lax.select(value < 0, landing(t - LAG, half)[rows_at], data)
                send_ref[slot, rows_at] = data
            for half in range(2):
                copy = z_copy(half, t, part, False)
                copy.start()
                started.append(copy)
        if t >= kv_steps + LAG - 1 and work:
            work.pop(0)()
    while work:
        work.pop(0)()
    for t in range(steps - LAG, steps):
        for half in range(2):
            for part in range(2):
                z_copy(half, t, part, True).wait_recv()
    for n in range(PACK):
        code = ctl_ref[AT_LIST + n]
        data = lax.select(code < 16, row_qg[jnp.clip(code, 0, 15)], recv_ref[jnp.clip(code - 16, 0, 2 * kv_steps - 1)])
        last = 16 + 2 * kv_steps
        pack_ref[n] = lax.select(code < last, data, late_ref[jnp.clip(code - last, 0, 2 * (steps - kv_steps) - 1)])
    for shift in range(1, NX * NZ):
        peer = lax.rem(seq + NX * NZ - shift, NX * NZ)
        stat_copy(shift, peer, peer).wait_recv()
    own_copies[-1].wait()
    for copy in started:
        copy.wait_send()


def route(variant, ctl, queries, keys, values, out_grad):
    steps, kv_steps = VARIANTS[variant]
    smem = pl.BlockSpec(memory_space=pltpu.SMEM)
    vmem = pl.BlockSpec(memory_space=pltpu.VMEM)
    out = jax.ShapeDtypeStruct((ROWS, HD), BF16)
    own = (4, 2 * BLK, HD)
    near = (16, 2 * BLK, HD)
    moved = (2 * steps, 2 * BLK, HD)
    early = (2 * kv_steps, 2 * BLK, HD)
    late = (2 * (steps - kv_steps), 2 * BLK, HD)
    stats = jax.ShapeDtypeStruct((NX * NZ, 8, BLK), F32)
    dma = pltpu.SemaphoreType.DMA
    return pl.pallas_call(
        functools.partial(route_kernel, steps, kv_steps),
        out_shape=(out, out, jax.ShapeDtypeStruct(own, BF16), jax.ShapeDtypeStruct((PACK, 2 * BLK, HD), BF16), stats),
        in_specs=[smem] + [vmem] * 4,
        out_specs=[vmem] * 5,
        scratch_shapes=[
            pltpu.VMEM(own, BF16),
            pltpu.VMEM(near, BF16),
            pltpu.VMEM(near, BF16),
            pltpu.VMEM(own, BF16),
            pltpu.VMEM(own, BF16),
            pltpu.VMEM(early, BF16),
            pltpu.VMEM(late, BF16),
            pltpu.VMEM(moved, BF16),
            pltpu.VMEM((4, 8 * BLK, HD), BF16),
            pltpu.VMEM((4, 8 * BLK, HD), BF16),
            pltpu.VMEM((4, BLK, 8 * BLK), F32),
            pltpu.VMEM((4, BLK, BLK), F32),
            pltpu.VMEM((8, BLK), F32),
            dma((4, NH)), dma((4, NH)), dma((4,)),
            dma((2, 6)), dma((2, 6)),
            dma((2 * steps, 2)), dma((2 * steps, 2)),
            dma((NX * NZ,)), dma((NX * NZ,)),
        ],
        compiler_params=pltpu.CompilerParams(collective_id=1 + variant, has_side_effects=True),
    )(ctl, queries, keys, values, out_grad)


def keys_kernel(ctl_ref, kv_ref, pack_ref, stats_ref, att_ref, dq_ref, att_out, dq_out, dk_ref, dv_ref, dk_acc, dv_acc):
    scale = 1.0 / math.sqrt(HD)
    att_out[...] = att_ref[...]
    dq_out[...] = dq_ref[...]
    dk_acc[...] = jnp.zeros_like(dk_acc)
    dv_acc[...] = jnp.zeros_like(dv_acc)
    pairs = ctl_ref[AT_COUNT]

    def trip(i, carry):
        sums = []
        for u in range(GROUP):
            at = GROUP * i + u
            word = ctl_ref[AT_PAIRS + jnp.minimum(at, pairs - 1)]
            n, a, j = word & 255, (word >> 8) & 255, word >> 16
            unused = jnp.where(at < pairs, 0.0, 1e30)
            q, g = pack_ref[n, 0:BLK, :], pack_ref[n, BLK : 2 * BLK, :]
            total = stats_ref[a // 4, pl.ds(lax.rem(a, 4), 1), :] + unused
            grad_dot = stats_ref[a // 4, pl.ds(lax.rem(a, 4) + 4, 1), :]
            p = jnp.exp(dot_nt(kv_ref[j, 0:BLK, :], q) * scale - total)
            ds = (p * (dot_nt(kv_ref[j, BLK : 2 * BLK, :], g) - grad_dot)).astype(BF16)
            sums.append((j, dot_nn(ds, q), dot_nn(p.astype(BF16), g)))
        for j, dk, dv in sums:
            dk_acc[j] += dk
            dv_acc[j] += dv
        return carry

    lax.fori_loop(0, (pairs + GROUP - 1) // GROUP, trip, 0)
    for j in range(4):
        dk_ref[j * BLK : (j + 1) * BLK, :] = (dk_acc[j] * scale).astype(BF16)
        dv_ref[j * BLK : (j + 1) * BLK, :] = dv_acc[j].astype(BF16)


def key_grads(ctl, kv, pack, stats, att, dq):
    smem = pl.BlockSpec(memory_space=pltpu.SMEM)
    vmem = pl.BlockSpec(memory_space=pltpu.VMEM)
    out = jax.ShapeDtypeStruct((ROWS, HD), BF16)
    return pl.pallas_call(
        keys_kernel,
        out_shape=(out,) * 4,
        in_specs=[smem] + [vmem] * 5,
        out_specs=[vmem] * 4,
        scratch_shapes=[
            pltpu.VMEM((4, BLK, HD), F32),
            pltpu.VMEM((4, BLK, HD), F32),
        ],
    )(ctl, kv, pack, stats, att, dq)


def on_device(queries, keys, values, out_grad, key_blocks, counts):
    seq = lax.axis_index("seq")
    ctl, choice = make_plan(jnp.transpose(key_blocks), counts[None, :])

    def sparse(variant):
        att, dq, kv, pack, stats = route(variant, ctl, queries, keys, values, out_grad)
        return tuple(key_grads(ctl, kv, pack, stats, att, dq))

    def dense():
        kv, qg = exchange(queries, keys, values, out_grad)
        live = jnp.arange(key_blocks.shape[1])[None, :] < counts[:, None]
        touch = jnp.any(live & (key_blocks // 4 == seq), axis=1)
        touch = (touch & (jnp.arange(key_blocks.shape[0]) // 4 != seq)).astype(jnp.int32)
        first = (seq * 4).reshape(1).astype(jnp.int32)
        return tuple(attend(first, touch, key_blocks, counts, kv, qg))

    branches = [functools.partial(sparse, variant) for variant in range(len(VARIANTS))] + [dense]
    return lax.switch(choice[0], branches)


def solution(mesh):
    rows = P(("seq", "head"), None)
    out = P("seq", "head")
    return jax.shard_map(
        on_device,
        mesh=mesh,
        in_specs=(rows,) * 4 + (P(), P()),
        out_specs=(out,) * 4,
        check_vma=False,
    )
```

```python
import functools
import heapq
import math

import jax
import jax.numpy as jnp
from jax import lax
from jax.experimental import pallas as pl
from jax.experimental.pallas import tpu as pltpu
from jax.sharding import PartitionSpec as P

MESH = pl.DeviceIdType.MESH
BLK = 128
HD = 128
NX = 4
NZ = 8
NH = 8
ROWS = 512
CHUNK = 64
SPLIT = 208
BF16 = jnp.bfloat16
F32 = jnp.float32
NEG = -1e30


def row_range(part):
    half_a, half_b = SPLIT // 32 * 16, SPLIT + (ROWS - SPLIT) // 32 * 16
    return {
        "A": (0, SPLIT),
        "A0": (0, half_a),
        "A1": (half_a, SPLIT),
        "B": (SPLIT, ROWS),
        "B0": (SPLIT, half_b),
        "B1": (half_b, ROWS),
    }[part]


def ring_sends(axis, sources, size, out, kind, prio):
    far = size // 2
    arrived = []
    for (offset, part, dep) in sources:
        if len(part) == 1:
            arrived.append((offset, part, dep))
            halves = [(part, +1, far - 1), (part, -1, far - 1)]
        else:
            arrived.append((offset, part, dep))
            sign = +1 if part[1] == "0" else -1
            halves = [(part, +1, far - 1), (part, -1, far - 1)]
        for (piece, sign, hops) in halves:
            last = dep
            at = offset
            for hop in range(1, hops + 1):
                out.append(dict(kind=kind, axis=axis, sign=sign, origin=at, part=piece, dep=last, left=far - hop, prio=prio))
                last = len(out) - 1
                at = step_offset(at, axis, sign)
                arrived.append((at, piece, last))
            for digit, way in (("0", +1), ("1", -1)):
                if way != sign:
                    continue
                tail = piece if len(piece) == 2 else piece + digit
                if tail[1] != digit:
                    continue
                out.append(dict(kind=kind, axis=axis, sign=sign, origin=at, part=tail, dep=last, left=0, prio=prio))
                arrived.append((step_offset(at, axis, sign), tail, len(out) - 1))
    return arrived


def step_offset(offset, axis, sign):
    ox, oz = offset
    return (ox + sign, oz) if axis == "x" else (ox, oz + sign)


def plan_sends():
    out = []
    for kind in (0, 1):
        own = -1 - kind
        first_a = ring_sends("x", [((0, 0), "A", own)], NX, out, kind, kind * 10)
        first_b = ring_sends("z", [((0, 0), "B", own)], NZ, out, kind, kind * 10)
        ring_sends("z", first_a, NZ, out, kind, kind * 10 + 1)
        ring_sends("x", first_b, NX, out, kind, kind * 10 + 1)
    rate = 46.0e3 * 1.0
    latency = 1.7
    ready_own = {-1: 4.0, -2: 8.0}
    arrival = {}
    free = {}
    start = {}
    waiting = {}
    events = []
    for i, m in enumerate(out):
        if m["dep"] < 0:
            heapq.heappush(events, (ready_own[m["dep"]], i))
    children = {}
    for i, m in enumerate(out):
        if m["dep"] >= 0:
            children.setdefault(m["dep"], []).append(i)
    queues = {("x", 1): [], ("x", -1): [], ("z", 1): [], ("z", -1): []}
    free = {k: 0.0 for k in queues}
    order = []
    while events or any(queues.values()):
        options = []
        for k, q in queues.items():
            if q:
                options.append((max(free[k], q[0][2]), k))
        next_link = min(options) if options else None
        if events and (next_link is None or events[0][0] <= next_link[0]):
            t, i = heapq.heappop(events)
            m = out[i]
            q = queues[(m["axis"], m["sign"])]
            q.append((m["prio"] // 10, -m["left"], t, i))
            q.sort(key=lambda e: (e[0], e[1], e[2], e[3]))
            continue
        t, k = next_link
        _, _, ready, i = queues[k].pop(0)
        m = out[i]
        lo, hi = row_range(m["part"])
        begin = max(free[k], ready)
        free[k] = begin + (hi - lo) * HD * 2 * 2 / rate
        start[i] = begin
        order.append((begin, ready, i))
        for c in children.get(i, []):
            heapq.heappush(events, (free[k] + latency, c))
    order.sort()
    return out, [i for (_, _, i) in order], max(free.values())


SENDS, ORDER, SPAN = plan_sends()


def exchange_kernel(q_ref, k_ref, v_ref, g_ref, kv_ref, qg_ref, send_sem, recv_sem, head_send, head_recv, own_sem):
    seq = lax.axis_index("seq")
    head = lax.axis_index("head")
    x, z = lax.rem(seq, NX), seq // NX

    def chip(cx, cz):
        return lax.rem(cz + 2 * NZ, NZ) * NX + lax.rem(cx + 2 * NX, NX)

    barrier = pltpu.get_barrier_semaphore()
    for shift in range(1, NH):
        pl.semaphore_signal(barrier, inc=1, device_id={"seq": seq, "head": lax.rem(head + shift, NH)}, device_id_type=MESH)
    for (cx, cz) in ((x + 1, z), (x - 1, z), (x, z + 1), (x, z - 1)):
        pl.semaphore_signal(barrier, inc=1, device_id={"seq": chip(cx, cz), "head": head}, device_id_type=MESH)
    pl.semaphore_wait(barrier, NH - 1 + 4)

    targets = ((k_ref, kv_ref, 0), (v_ref, kv_ref, 1), (q_ref, qg_ref, 0), (g_ref, qg_ref, 1))

    def rows_of(dst, which, h):
        return dst.at[seq, which, pl.ds(pl.multiple_of(h * CHUNK, CHUNK), CHUNK), :]

    def columns_of(src, h):
        return src.at[:, pl.ds(pl.multiple_of(h * HD, HD), HD)]

    head_copies = []
    own_copies = []
    for array, (src, dst, which) in enumerate(targets):
        for shift in range(1, NH):
            peer = lax.rem(head + shift, NH)
            copy = pltpu.make_async_remote_copy(
                src_ref=columns_of(src, peer),
                dst_ref=rows_of(dst, which, head),
                send_sem=head_send.at[array, shift],
                recv_sem=head_recv.at[array, shift],
                device_id={"seq": seq, "head": peer},
                device_id_type=MESH,
            )
            copy.start()
            head_copies.append(copy)
        own = pltpu.make_async_copy(columns_of(src, head), rows_of(dst, which, head), own_sem.at[array])
        own.start()
        own_copies.append(own)

    def wait_head(array):
        src, dst, which = targets[array]
        for shift in range(1, NH):
            peer = lax.rem(head + NH - shift, NH)
            pltpu.make_async_remote_copy(
                src_ref=columns_of(src, peer),
                dst_ref=rows_of(dst, which, peer),
                send_sem=head_send.at[array, shift],
                recv_sem=head_recv.at[array, shift],
                device_id={"seq": seq, "head": peer},
                device_id_type=MESH,
            ).wait_recv()
        own_copies[array].wait()

    buffers = (kv_ref, qg_ref)

    def piece(m, ox, oz):
        lo, hi = row_range(m["part"])
        return buffers[m["kind"]].at[chip(x - ox, z - oz), :, lo:hi, :]

    def send(i):
        m = SENDS[i]
        ox, oz = m["origin"]
        target = chip(x + m["sign"], z) if m["axis"] == "x" else chip(x, z + m["sign"])
        return pltpu.make_async_remote_copy(
            src_ref=piece(m, ox, oz),
            dst_ref=piece(m, ox, oz),
            send_sem=send_sem.at[i],
            recv_sem=recv_sem.at[i],
            device_id={"seq": target, "head": head},
            device_id_type=MESH,
        )

    def wait_recv(i):
        m = SENDS[i]
        ox, oz = step_offset(m["origin"], m["axis"], m["sign"])
        source = chip(x - m["sign"], z) if m["axis"] == "x" else chip(x, z - m["sign"])
        pltpu.make_async_remote_copy(
            src_ref=piece(m, ox, oz),
            dst_ref=piece(m, ox, oz),
            send_sem=send_sem.at[i],
            recv_sem=recv_sem.at[i],
            device_id={"seq": source, "head": head},
            device_id_type=MESH,
        ).wait_recv()

    ready = set()
    started = []
    for i in ORDER:
        dep = SENDS[i]["dep"]
        if dep not in ready:
            ready.add(dep)
            if dep < 0:
                wait_head(2 * (-1 - dep))
                wait_head(2 * (-1 - dep) + 1)
            else:
                wait_recv(dep)
        copy = send(i)
        copy.start()
        started.append(copy)
    for i in ORDER:
        if i not in ready:
            wait_recv(i)
    for copy in started:
        copy.wait_send()
    for copy in head_copies:
        copy.wait_send()


def exchange(queries, keys, values, out_grad):
    shape = jax.ShapeDtypeStruct((NX * NZ, 2, ROWS, HD), BF16)
    count = len(SENDS)
    return pl.pallas_call(
        exchange_kernel,
        out_shape=(shape, shape),
        in_specs=[pl.BlockSpec(memory_space=pltpu.VMEM)] * 4,
        out_specs=[pl.BlockSpec(memory_space=pl.ANY)] * 2,
        scratch_shapes=[
            pltpu.SemaphoreType.DMA((count,)),
            pltpu.SemaphoreType.DMA((count,)),
            pltpu.SemaphoreType.DMA((4, NH)),
            pltpu.SemaphoreType.DMA((4, NH)),
            pltpu.SemaphoreType.DMA((4,)),
        ],
        compiler_params=pltpu.CompilerParams(collective_id=0, has_side_effects=True),
    )(queries, keys, values, out_grad)


def dot_nt(a, b):
    return lax.dot_general(a, b, (((1,), (1,)), ((), ())), preferred_element_type=F32)


def dot_nn(a, b):
    return lax.dot_general(a, b, (((1,), (0,)), ((), ())), preferred_element_type=F32)


def dot_tn(a, b):
    return lax.dot_general(a, b, (((0,), (0,)), ((), ())), preferred_element_type=F32)


def attend_kernel(first_ref, touch_ref, blocks_ref, counts_ref, kv_ref, qg_ref, att_ref, dq_ref, dk_ref, dv_ref, s_ref, acc_ref, dk_acc, dv_acc):
    scale = 1.0 / math.sqrt(HD)
    dk_acc[...] = jnp.zeros_like(dk_acc)
    dv_acc[...] = jnp.zeros_like(dv_acc)
    first = first_ref[0]

    def load(ref, which, block):
        return ref[block // 4, which, pl.ds(pl.multiple_of(lax.rem(block, 4) * BLK, BLK), BLK), :]

    def query_block(a, local):
        count = counts_ref[a]
        q = load(qg_ref, 0, a)
        g = load(qg_ref, 1, a)

        def score(t, row_max):
            s = dot_nt(q, load(kv_ref, 0, blocks_ref[a, t])) * scale
            s_ref[t] = s
            return jnp.maximum(row_max, jnp.max(s, axis=1, keepdims=True))

        row_max = lax.fori_loop(0, count, score, jnp.full((BLK, 1), NEG, F32))
        acc_ref[...] = jnp.zeros_like(acc_ref)

        def mix(t, row_sum):
            w = jnp.exp(s_ref[t] - row_max)
            acc_ref[...] += dot_nn(w.astype(BF16), load(kv_ref, 1, blocks_ref[a, t]))
            return row_sum + jnp.sum(w, axis=1, keepdims=True)

        row_sum = lax.fori_loop(0, count, mix, jnp.zeros((BLK, 1), F32))
        att = (acc_ref[...] / row_sum).astype(BF16)
        total = row_max + jnp.log(row_sum)
        grad_dot = jnp.sum(g.astype(F32) * att.astype(F32), axis=1, keepdims=True)

        def pair(t):
            block = blocks_ref[a, t]
            p = jnp.exp(s_ref[t] - total)
            dp = dot_nt(g, load(kv_ref, 1, block))
            return block, p, (p * (dp - grad_dot)).astype(BF16)

        def add_key(slot, p, ds):
            dk_acc[slot] += dot_tn(ds, q)
            dv_acc[slot] += dot_tn(p.astype(BF16), g)

        if local:
            acc_ref[...] = jnp.zeros_like(acc_ref)

            def back(t, carry):
                block, p, ds = pair(t)
                acc_ref[...] += dot_nn(ds, load(kv_ref, 0, block))
                slot = block - first

                @pl.when((slot >= 0) & (slot < 4))
                def _():
                    add_key(slot, p, ds)

                return carry

            lax.fori_loop(0, count, back, 0)
            rows = pl.ds(pl.multiple_of((a - first) * BLK, BLK), BLK)
            att_ref[rows, :] = att
            dq_ref[rows, :] = (acc_ref[...] * scale).astype(BF16)
        else:

            def back(t, carry):
                slot = blocks_ref[a, t] - first

                @pl.when((slot >= 0) & (slot < 4))
                def _():
                    _, p, ds = pair(t)
                    add_key(slot, p, ds)

                return carry

            lax.fori_loop(0, count, back, 0)

    def own(i, carry):
        query_block(first + i, True)
        return carry

    lax.fori_loop(0, 4, own, 0)

    def other(a, carry):
        @pl.when(touch_ref[a] > 0)
        def _():
            query_block(a, False)

        return carry

    lax.fori_loop(0, 128, other, 0)
    for slot in range(4):
        dk_ref[slot * BLK : (slot + 1) * BLK, :] = (dk_acc[slot] * scale).astype(BF16)
        dv_ref[slot * BLK : (slot + 1) * BLK, :] = dv_acc[slot].astype(BF16)


def attend(first, touch, key_blocks, counts, kv, qg):
    shape = jax.ShapeDtypeStruct((ROWS, HD), BF16)
    smem = pl.BlockSpec(memory_space=pltpu.SMEM)
    vmem = pl.BlockSpec(memory_space=pltpu.VMEM)
    return pl.pallas_call(
        attend_kernel,
        out_shape=(shape,) * 4,
        in_specs=[smem] * 4 + [vmem] * 2,
        out_specs=[vmem] * 4,
        scratch_shapes=[
            pltpu.VMEM((8, BLK, BLK), F32),
            pltpu.VMEM((BLK, HD), F32),
            pltpu.VMEM((4, BLK, HD), F32),
            pltpu.VMEM((4, BLK, HD), F32),
        ],
    )(first, touch, key_blocks, counts, kv, qg)


LAG = 2
STEPS = 34
VARIANTS = ((25, 21), (28, 24), (34, 30))
PACK = 24
GROUP = 4
OWN_QG = 4
PASS_KV = 4
NEAR_KV = 6
ALL_KV = 8
PASS_QG = 10
NEAR_QG = 12
ALL_QG = 14
CTL = 2048
AT_CODE = 128
AT_PICK = 160
AT_COUNT = 161
AT_USED = 164
AT_LIST = 256
AT_PAIRS = 1024


def plan_kernel(blocks_ref, counts_ref, ctl_ref, pick_ref, words_ref, words, where_kv, where_qg, sem):
    seq = lax.axis_index("seq")
    x, z = lax.rem(seq, NX), seq // NX
    brow = lax.broadcasted_iota(jnp.int32, (BLK, BLK), 0)
    count = counts_ref[...]
    hits = jnp.zeros((BLK, BLK), F32)
    for t in range(8):
        hits = jnp.where((blocks_ref[t : t + 1, :] == brow) & (count > t), 1.0, hits)
    row = lax.broadcasted_iota(jnp.int32, (32, BLK), 0)
    col = lax.broadcasted_iota(jnp.int32, (32, BLK), 1)
    device = lax.rem(row, NZ) * NX + row // NZ
    group = jnp.where(col // 4 == device, 1.0, 0.0)
    need_kv = dot_nt(group, hits)
    need_qg = dot_nn(group, hits)
    jrow = lax.broadcasted_iota(jnp.int32, (8, BLK), 0)
    jcol = lax.broadcasted_iota(jnp.int32, (8, BLK), 1)
    mine = jcol - seq * 4
    power = jnp.where(mine == 0, 1.0, jnp.where(mine == 1, 2.0, jnp.where(mine == 2, 4.0, jnp.where(mine == 3, 8.0, 0.0))))
    quad = lax.rem(lax.broadcasted_iota(jnp.int32, (BLK, BLK), 1), 4)
    digit = jnp.where(quad == 0, 1.0, jnp.where(quad == 1, 16.0, jnp.where(quad == 2, 256.0, 4096.0)))
    digit = jnp.where(lax.broadcasted_iota(jnp.int32, (BLK, BLK), 1) // 4 == brow, digit, 0.0)
    bits = dot_nt(dot_nn(power, hits), digit)

    origin = jcol // 16
    delta = lax.rem(jrow - origin + NZ, NZ)
    near = (delta >= 1) & (delta < 4)
    back = delta > 4
    tie = delta == 4
    far = delta.astype(F32)
    zero = jnp.zeros((8, BLK), F32)

    hops = [zero, zero]
    for column in range(NX):
        parts = [need[column * NZ : (column + 1) * NZ, :] > 0.5 for need in (need_kv, need_qg)]
        lean = zero
        for part in parts:
            lean = lean + jnp.where(part & near, 1.0, 0.0) - jnp.where(part & back, 1.0, 0.0)
        lean = jnp.broadcast_to(jnp.sum(lean, axis=1, keepdims=True), (8, BLK))
        ahead = near | (tie & (lean < 0.0))
        behind = back | (tie & (lean >= 0.0))
        for kind, part in enumerate(parts):
            for half in range(2):
                hop = jnp.where(part & ahead, far, 0.0) if half == 0 else jnp.where(part & behind, 8.0 - far, 0.0)
                most = jnp.broadcast_to(jnp.max(hop, axis=0, keepdims=True), (8, BLK))
                hops[kind] = jnp.where(jrow == column * 2 + half, most, hops[kind])

    lanes = lax.broadcasted_iota(jnp.int32, (BLK, BLK), 1)
    spread = jnp.where(jcol // 8 == jrow, 1.0, 0.0)
    lands = (brow // 16 == lax.rem(lanes, 8)) & (lanes < 64)
    sub16 = lax.broadcasted_iota(jnp.int32, (16, BLK), 0)
    lane16 = lax.broadcasted_iota(jnp.int32, (16, BLK), 1)
    fold = jnp.where(lax.rem(lane16, 16) == sub16, 1.0, 0.0)
    ident = (127 - lax.rem(lane16, 8) * 16 - sub16).astype(F32)
    apart = lax.rem(sub16 // 4 - lane16 // 16 + 2 * NX, NX)
    own, close = apart == 0, apart != 2
    keys = []
    for kind, base in ((0, 2048.0), (1, 0.0)):
        most = dot_nn(fold, jnp.where(lands, dot_tn(hops[kind], spread), 0.0))
        keys.append(jnp.where(most > 0.5, most * 128.0 + base + ident, 0.0))
    kv, qg = keys
    at_z = lax.rem(jcol, 8)
    forward = lax.rem(jcol // 8, 2) == 0
    history = []
    last_any, last_kv = zero, zero
    for t in range(STEPS):
        best = kv if t >= ALL_KV else jnp.where(close if t >= NEAR_KV else own, kv, 0.0)
        if t >= OWN_QG:
            best = jnp.maximum(best, qg if t >= ALL_QG else jnp.where(close if t >= NEAR_QG else own, qg, 0.0))
        best = jnp.broadcast_to(jnp.max(best, axis=0, keepdims=True), (8, BLK))
        if t >= LAG:
            before = history[t - LAG]
            up = jnp.where(at_z == 0, pltpu.roll(before, BLK - 7, 1), pltpu.roll(before, 1, 1))
            down = jnp.where(at_z == 7, pltpu.roll(before, 7, 1), pltpu.roll(before, BLK - 1, 1))
            passing = jnp.where(forward, up, down) - 128.0
            left = jnp.where(passing >= 2048.0, passing - 2048.0, passing)
            through = left > 127.5
            taken = jnp.where(through, -1.0, best)
            sent = jnp.where(through, passing, best)
            mark = jnp.where(through, -passing, best)
        else:
            taken, sent, mark = best, best, best
        taken = jnp.concatenate([taken, taken], axis=0)
        kv = jnp.where(kv == taken, 0.0, kv)
        qg = jnp.where(qg == taken, 0.0, qg)
        history.append(sent)
        last_any = jnp.where(sent > 0.0, t + 1.0, last_any)
        last_kv = jnp.where(sent >= 2048.0, t + 1.0, last_kv)
        words_ref[t : t + 1, :] = mark[0:1, :].astype(jnp.int32)
    remain = jnp.maximum(kv, qg)
    last_any = jnp.where(jnp.maximum(remain[0:8, :], remain[8:16, :]) > 0.0, 999.0, last_any)
    for t in range(STEPS - LAG, STEPS):
        left = jnp.where(history[t] >= 2048.0, history[t] - 2048.0, history[t])
        last_any = jnp.where(left > 255.5, 999.0, last_any)
    last_any = jnp.max(jnp.max(last_any, axis=1, keepdims=True), axis=0, keepdims=True)
    last_kv = jnp.max(jnp.max(last_kv, axis=1, keepdims=True), axis=0, keepdims=True)
    index = jnp.zeros((1, 1), F32)
    for steps, kv_steps in VARIANTS:
        index = index + jnp.where((last_any > steps + 0.5) | (last_kv > kv_steps + 0.5), 1.0, 0.0)
    crowd = jnp.max(jnp.sum(jnp.where(need_qg > 0.5, 1.0, 0.0), axis=1, keepdims=True), axis=0, keepdims=True)
    index = jnp.where(crowd > PACK + 0.5, float(len(VARIANTS)), index)
    words_ref[40:48, :] = blocks_ref[...]
    misc = jnp.where(jrow == 0, bits.astype(jnp.int32), jnp.broadcast_to(count, (8, BLK)))
    words_ref[48:56, :] = jnp.where(jrow == 2, jnp.broadcast_to(index, (8, BLK)).astype(jnp.int32), misc)
    copy = pltpu.make_async_copy(words_ref, words, sem)
    copy.start()
    copy.wait()

    pick_ref[0] = words[50, 0]
    for i in range(16):
        where_kv[z * 16 + i] = i
        where_qg[z * 16 + i] = i
    sources = (lax.rem(z + NZ - 1, NZ), lax.rem(z + 1, NZ))

    def slot(t, carry):
        for half in range(2):
            ctl_ref[2 * t + half] = words[t, (2 * x + half) * 8 + z]
            value = jnp.abs(words[t, (2 * x + half) * 8 + sources[half]])
            block = 127 - (value & 127)
            spot = 16 + 2 * t + half

            @pl.when(value >= 2048)
            def _():
                where_kv[block] = spot

            @pl.when((value >= 128) & (value < 2048))
            def _():
                where_qg[block] = spot

        return carry

    lax.fori_loop(0, STEPS, slot, 0)
    for i in range(4):
        live = words[49, 4 * seq + i]
        ctl_ref[AT_USED + i] = live
        for t in range(8):
            block = jnp.where(t < live, words[40 + t, 4 * seq + i], 4 * seq + i)
            ctl_ref[AT_CODE + i * 8 + t] = where_kv[block]

    def entry(group, totals):
        word = words[48, group]

        def listed(totals):
            n, pairs = totals
            for r in range(4):
                a = 4 * group + r
                mask = (word >> (4 * r)) & 15
                ctl_ref[AT_LIST + n] = where_qg[a]
                for j in range(4):
                    ctl_ref[AT_PAIRS + pairs] = n + a * 256 + j * 65536
                    pairs = pairs + ((mask >> j) & 1)
                n = n + jnp.where(mask > 0, 1, 0)
            return n, pairs

        return lax.cond(word > 0, listed, lambda totals: totals, totals)

    ctl_ref[AT_COUNT] = lax.fori_loop(0, BLK // 4, entry, (0, 0))[1]


def make_plan(key_blocks, counts):
    vmem = pl.BlockSpec(memory_space=pltpu.VMEM)
    return pl.pallas_call(
        plan_kernel,
        out_shape=(jax.ShapeDtypeStruct((CTL,), jnp.int32), jax.ShapeDtypeStruct((1,), jnp.int32)),
        in_specs=[vmem, vmem],
        out_specs=[pl.BlockSpec(memory_space=pltpu.SMEM)] * 2,
        scratch_shapes=[
            pltpu.VMEM((56, BLK), jnp.int32),
            pltpu.SMEM((56, BLK), jnp.int32),
            pltpu.SMEM((BLK,), jnp.int32),
            pltpu.SMEM((BLK,), jnp.int32),
            pltpu.SemaphoreType.DMA,
        ],
    )(key_blocks, counts)


def route_kernel(
    steps, kv_steps,
    ctl_ref, q_ref, k_ref, v_ref, g_ref,
    att_ref, dq_ref, own_kv, pack_ref, stats_ref,
    own_qg, row_kv, row_qg, far_kv, far_qg, recv_ref, late_ref, send_ref, kcat, vcat, probs, dots, mine_stats,
    head_send, head_recv, own_sem, x_send, x_recv, z_send, z_recv, s_send, s_recv,
):
    seq = lax.axis_index("seq")
    head = lax.axis_index("head")
    x, z = lax.rem(seq, NX), seq // NX

    def chip(cx, cz):
        return lax.rem(cz + 2 * NZ, NZ) * NX + lax.rem(cx + 2 * NX, NX)

    barrier = pltpu.get_barrier_semaphore()
    for shift in range(1, NH):
        pl.semaphore_signal(barrier, inc=1, device_id={"seq": seq, "head": lax.rem(head + shift, NH)}, device_id_type=MESH)
    for (cx, cz) in ((x + 1, z), (x - 1, z), (x, z + 1), (x, z - 1)):
        pl.semaphore_signal(barrier, inc=1, device_id={"seq": chip(cx, cz), "head": head}, device_id_type=MESH)
    pl.semaphore_wait(barrier, NH - 1 + 4)

    targets = ((k_ref, own_kv, 0), (v_ref, own_kv, 1), (q_ref, own_qg, 0), (g_ref, own_qg, 1))

    def rows_of(dst, which, h):
        start = pl.multiple_of(which * BLK + lax.rem(h, 2) * CHUNK, CHUNK)
        return dst.at[h // 2, pl.ds(start, CHUNK), :]

    def columns_of(src, h):
        return src.at[:, pl.ds(pl.multiple_of(h * HD, HD), HD)]

    def head_copy(array, peer_from, peer_to, shift):
        src, dst, which = targets[array]
        return pltpu.make_async_remote_copy(
            src_ref=columns_of(src, peer_to),
            dst_ref=rows_of(dst, which, peer_from),
            send_sem=head_send.at[array, shift],
            recv_sem=head_recv.at[array, shift],
            device_id={"seq": seq, "head": peer_to},
            device_id_type=MESH,
        )

    started = []
    own_copies = []
    for array, (src, dst, which) in enumerate(targets):
        for shift in range(1, NH):
            copy = head_copy(array, head, lax.rem(head + shift, NH), shift)
            copy.start()
            started.append(copy)
        own = pltpu.make_async_copy(columns_of(src, head), rows_of(dst, which, head), own_sem.at[array])
        own.start()
        own_copies.append(own)

    def wait_head(array):
        for shift in range(1, NH):
            peer = lax.rem(head + NH - shift, NH)
            head_copy(array, peer, peer, shift).wait_recv()
        own_copies[array].wait()

    owned = (own_kv, own_qg)
    rows = (row_kv, row_qg)
    x_plan = ((1, 0, 0), (-1, 0, 2), (1, 0, 2), (-1, 0, 0), (1, 1, 0), (-1, -1, 2))

    def x_copy(kind, i, arriving):
        sign, offset, first = x_plan[i]
        origin = lax.rem(x - offset - (sign if arriving else 0) + 2 * NX, NX)
        piece = rows[kind].at[pl.ds(4 * origin + first, 2)]
        landed = (far_kv, far_qg)[kind].at[pl.ds(first, 2)] if offset != 0 else piece
        other = chip(x - sign, z) if arriving else chip(x + sign, z)
        return pltpu.make_async_remote_copy(
            src_ref=landed if arriving else piece if offset != 0 else owned[kind].at[pl.ds(first, 2)],
            dst_ref=landed, send_sem=x_send.at[kind, i], recv_sem=x_recv.at[kind, i],
            device_id={"seq": other, "head": head}, device_id_type=MESH,
        )

    def x_start(kind, i):
        copy = x_copy(kind, i, False)
        copy.start()
        started.append(copy)

    def landing(t, half):
        return recv_ref.at[2 * t + half] if t < kv_steps else late_ref.at[2 * (t - kv_steps) + half]

    def z_copy(half, t, part, arriving):
        sign = 1 if half == 0 else -1
        other = chip(x, z - sign) if arriving else chip(x, z + sign)
        slot = 2 * t + half
        rows = slice(part * BLK, part * BLK + BLK)
        return pltpu.make_async_remote_copy(
            src_ref=send_ref.at[slot, rows], dst_ref=landing(t, half).at[rows],
            send_sem=z_send.at[slot, part], recv_sem=z_recv.at[slot, part],
            device_id={"seq": other, "head": head}, device_id_type=MESH,
        )

    scale = 1.0 / math.sqrt(HD)
    key_at = lax.broadcasted_iota(jnp.int32, (1, 8 * BLK), 1)

    def attend_block(i):
        for t in range(8):
            code = ctl_ref[AT_CODE + i * 8 + t]
            near = row_kv[jnp.minimum(code, 15)]
            moved = recv_ref[jnp.clip(code - 16, 0, 2 * kv_steps - 1)]
            data = lax.select(code < 16, near, moved)
            kcat[i, t * BLK : (t + 1) * BLK, :] = data[0:BLK]
            vcat[i, t * BLK : (t + 1) * BLK, :] = data[BLK : 2 * BLK]
        q, g = own_qg[i, 0:BLK], own_qg[i, BLK : 2 * BLK]
        s = dot_nt(q, kcat[i]) * scale + jnp.where(key_at < ctl_ref[AT_USED + i] * BLK, 0.0, NEG)
        row_max = jnp.max(s, axis=1, keepdims=True)
        w = jnp.exp(s - row_max)
        row_sum = jnp.sum(w, axis=1, keepdims=True)
        scaled = 1.0 / row_sum
        att = (dot_nn(w.astype(BF16), vcat[i]) * scaled).astype(BF16)
        total = row_max + jnp.log(row_sum)
        grad_dot = jnp.sum(g.astype(F32) * att.astype(F32), axis=1, keepdims=True)
        probs[i] = w * scaled
        dots[i] = jnp.broadcast_to(grad_dot, (BLK, BLK))
        att_ref[i * BLK : (i + 1) * BLK, :] = att
        mine_stats[i : i + 1, :] = jnp.transpose(jnp.broadcast_to(total, (BLK, BLK)))[0:1, :]
        mine_stats[i + 4 : i + 5, :] = jnp.transpose(jnp.broadcast_to(grad_dot, (BLK, BLK)))[0:1, :]

    def query_grad(i):
        g = own_qg[i, BLK : 2 * BLK]
        ds = (probs[i] * (dot_nt(g, vcat[i]) - dots[i, :, 0:1])).astype(BF16)
        dq_ref[i * BLK : (i + 1) * BLK, :] = (dot_nn(ds, kcat[i]) * scale).astype(BF16)

    def stat_copy(shift, origin, target):
        return pltpu.make_async_remote_copy(
            src_ref=mine_stats, dst_ref=stats_ref.at[origin], send_sem=s_send.at[shift], recv_sem=s_recv.at[shift],
            device_id={"seq": target, "head": head}, device_id_type=MESH,
        )

    def keep_own(kind):
        for i in range(4):
            rows[kind][4 * x + i] = owned[kind][i]

    def keep_far(kind):
        for i in range(4, 6):
            x_copy(kind, i, True).wait_recv()
        for i in range(4):
            rows[kind][4 * lax.rem(x + 2, NX) + i] = (far_kv, far_qg)[kind][i]

    wait_head(0)
    wait_head(1)
    for i in range(4):
        x_start(0, i)

    def send_stats():
        for shift in range(1, NX * NZ):
            copy = stat_copy(shift, seq, lax.rem(seq + shift, NX * NZ))
            copy.start()
            started.append(copy)
        own = pltpu.make_async_copy(mine_stats, stats_ref.at[seq], s_recv.at[0])
        own.start()
        own_copies.append(own)

    work = [functools.partial(attend_block, i) for i in range(4)] + [send_stats]
    work += [functools.partial(query_grad, i) for i in range(4)]
    for t in range(steps):
        if t == PASS_KV:
            wait_head(2)
            wait_head(3)
            x_copy(0, 0, True).wait_recv()
            x_start(0, 4)
            x_copy(0, 1, True).wait_recv()
            x_start(0, 5)
            for i in range(4):
                x_start(1, i)
            keep_own(0)
            keep_own(1)
        elif t == NEAR_KV:
            for i in range(2, 4):
                x_copy(0, i, True).wait_recv()
        elif t == ALL_KV:
            keep_far(0)
        elif t == PASS_QG:
            x_copy(1, 0, True).wait_recv()
            x_start(1, 4)
            x_copy(1, 1, True).wait_recv()
            x_start(1, 5)
        elif t == NEAR_QG:
            for i in range(2, 4):
                x_copy(1, i, True).wait_recv()
        elif t == ALL_QG:
            keep_far(1)
        for part in range(2):
            rows_at = slice(part * BLK, part * BLK + BLK)
            for half in range(2):
                slot = 2 * t + half
                value = ctl_ref[slot]
                size = jnp.abs(value)
                index = (127 - (size & 127)) & 15
                data = row_kv[index, rows_at] if t >= NEAR_KV else own_kv[index & 3, rows_at]
                if t >= OWN_QG:
                    other = row_qg[index, rows_at] if t >= NEAR_QG else own_qg[index & 3, rows_at]
                    data = lax.select(size >= 2048, data, other)
                if t >= LAG:
                    z_copy(half, t - LAG, part, True).wait_recv()
                    data = lax.select(value < 0, landing(t - LAG, half)[rows_at], data)
                send_ref[slot, rows_at] = data
            for half in range(2):
                copy = z_copy(half, t, part, False)
                copy.start()
                started.append(copy)
        if t >= kv_steps + LAG - 1 and work:
            work.pop(0)()
    while work:
        work.pop(0)()
    for t in range(steps - LAG, steps):
        for half in range(2):
            for part in range(2):
                z_copy(half, t, part, True).wait_recv()
    for n in range(PACK):
        code = ctl_ref[AT_LIST + n]
        data = lax.select(code < 16, row_qg[jnp.clip(code, 0, 15)], recv_ref[jnp.clip(code - 16, 0, 2 * kv_steps - 1)])
        last = 16 + 2 * kv_steps
        pack_ref[n] = lax.select(code < last, data, late_ref[jnp.clip(code - last, 0, 2 * (steps - kv_steps) - 1)])
    for shift in range(1, NX * NZ):
        peer = lax.rem(seq + NX * NZ - shift, NX * NZ)
        stat_copy(shift, peer, peer).wait_recv()
    own_copies[-1].wait()
    for copy in started:
        copy.wait_send()


def route(variant, ctl, queries, keys, values, out_grad):
    steps, kv_steps = VARIANTS[variant]
    smem = pl.BlockSpec(memory_space=pltpu.SMEM)
    vmem = pl.BlockSpec(memory_space=pltpu.VMEM)
    out = jax.ShapeDtypeStruct((ROWS, HD), BF16)
    own = (4, 2 * BLK, HD)
    near = (16, 2 * BLK, HD)
    moved = (2 * steps, 2 * BLK, HD)
    early = (2 * kv_steps, 2 * BLK, HD)
    late = (2 * (steps - kv_steps), 2 * BLK, HD)
    stats = jax.ShapeDtypeStruct((NX * NZ, 8, BLK), F32)
    dma = pltpu.SemaphoreType.DMA
    return pl.pallas_call(
        functools.partial(route_kernel, steps, kv_steps),
        out_shape=(out, out, jax.ShapeDtypeStruct(own, BF16), jax.ShapeDtypeStruct((PACK, 2 * BLK, HD), BF16), stats),
        in_specs=[smem] + [vmem] * 4,
        out_specs=[vmem] * 5,
        scratch_shapes=[
            pltpu.VMEM(own, BF16),
            pltpu.VMEM(near, BF16),
            pltpu.VMEM(near, BF16),
            pltpu.VMEM(own, BF16),
            pltpu.VMEM(own, BF16),
            pltpu.VMEM(early, BF16),
            pltpu.VMEM(late, BF16),
            pltpu.VMEM(moved, BF16),
            pltpu.VMEM((4, 8 * BLK, HD), BF16),
            pltpu.VMEM((4, 8 * BLK, HD), BF16),
            pltpu.VMEM((4, BLK, 8 * BLK), F32),
            pltpu.VMEM((4, BLK, BLK), F32),
            pltpu.VMEM((8, BLK), F32),
            dma((4, NH)), dma((4, NH)), dma((4,)),
            dma((2, 6)), dma((2, 6)),
            dma((2 * steps, 2)), dma((2 * steps, 2)),
            dma((NX * NZ,)), dma((NX * NZ,)),
        ],
        compiler_params=pltpu.CompilerParams(collective_id=1 + variant, has_side_effects=True),
    )(ctl, queries, keys, values, out_grad)


def keys_kernel(ctl_ref, kv_ref, pack_ref, stats_ref, att_ref, dq_ref, att_out, dq_out, dk_ref, dv_ref, dk_acc, dv_acc):
    scale = 1.0 / math.sqrt(HD)
    att_out[...] = att_ref[...]
    dq_out[...] = dq_ref[...]
    dk_acc[...] = jnp.zeros_like(dk_acc)
    dv_acc[...] = jnp.zeros_like(dv_acc)
    pairs = ctl_ref[AT_COUNT]

    def trip(i, carry):
        sums = []
        for u in range(GROUP):
            at = GROUP * i + u
            word = ctl_ref[AT_PAIRS + jnp.minimum(at, pairs - 1)]
            n, a, j = word & 255, (word >> 8) & 255, word >> 16
            unused = jnp.where(at < pairs, 0.0, 1e30)
            q, g = pack_ref[n, 0:BLK, :], pack_ref[n, BLK : 2 * BLK, :]
            total = stats_ref[a // 4, pl.ds(lax.rem(a, 4), 1), :] + unused
            grad_dot = stats_ref[a // 4, pl.ds(lax.rem(a, 4) + 4, 1), :]
            p = jnp.exp(dot_nt(kv_ref[j, 0:BLK, :], q) * scale - total)
            ds = (p * (dot_nt(kv_ref[j, BLK : 2 * BLK, :], g) - grad_dot)).astype(BF16)
            sums.append((j, dot_nn(ds, q), dot_nn(p.astype(BF16), g)))
        for j, dk, dv in sums:
            dk_acc[j] += dk
            dv_acc[j] += dv
        return carry

    lax.fori_loop(0, (pairs + GROUP - 1) // GROUP, trip, 0)
    for j in range(4):
        dk_ref[j * BLK : (j + 1) * BLK, :] = (dk_acc[j] * scale).astype(BF16)
        dv_ref[j * BLK : (j + 1) * BLK, :] = dv_acc[j].astype(BF16)


def key_grads(ctl, kv, pack, stats, att, dq):
    smem = pl.BlockSpec(memory_space=pltpu.SMEM)
    vmem = pl.BlockSpec(memory_space=pltpu.VMEM)
    out = jax.ShapeDtypeStruct((ROWS, HD), BF16)
    return pl.pallas_call(
        keys_kernel,
        out_shape=(out,) * 4,
        in_specs=[smem] + [vmem] * 5,
        out_specs=[vmem] * 4,
        scratch_shapes=[
            pltpu.VMEM((4, BLK, HD), F32),
            pltpu.VMEM((4, BLK, HD), F32),
        ],
    )(ctl, kv, pack, stats, att, dq)


def on_device(queries, keys, values, out_grad, key_blocks, counts):
    seq = lax.axis_index("seq")
    ctl, choice = make_plan(jnp.transpose(key_blocks), counts[None, :])

    def sparse(variant):
        att, dq, kv, pack, stats = route(variant, ctl, queries, keys, values, out_grad)
        return tuple(key_grads(ctl, kv, pack, stats, att, dq))

    def dense():
        kv, qg = exchange(queries, keys, values, out_grad)
        live = jnp.arange(key_blocks.shape[1])[None, :] < counts[:, None]
        touch = jnp.any(live & (key_blocks // 4 == seq), axis=1)
        touch = (touch & (jnp.arange(key_blocks.shape[0]) // 4 != seq)).astype(jnp.int32)
        first = (seq * 4).reshape(1).astype(jnp.int32)
        return tuple(attend(first, touch, key_blocks, counts, kv, qg))

    branches = [functools.partial(sparse, variant) for variant in range(len(VARIANTS))] + [dense]
    return lax.switch(choice[0], branches)


def solution(mesh):
    rows = P(("seq", "head"), None)
    out = P("seq", "head")
    return jax.shard_map(
        on_device,
        mesh=mesh,
        in_specs=(rows,) * 4 + (P(), P()),
        out_specs=(out,) * 4,
        check_vma=False,
    )
```

```python
import functools
import heapq
import math

import jax
import jax.numpy as jnp
from jax import lax
from jax.experimental import pallas as pl
from jax.experimental.pallas import tpu as pltpu
from jax.sharding import PartitionSpec as P

MESH = pl.DeviceIdType.MESH
BLK = 128
HD = 128
NX = 4
NZ = 8
NH = 8
ROWS = 512
CHUNK = 64
SPLIT = 208
BF16 = jnp.bfloat16
F32 = jnp.float32
NEG = -1e30


def row_range(part):
    half_a, half_b = SPLIT // 32 * 16, SPLIT + (ROWS - SPLIT) // 32 * 16
    return {
        "A": (0, SPLIT),
        "A0": (0, half_a),
        "A1": (half_a, SPLIT),
        "B": (SPLIT, ROWS),
        "B0": (SPLIT, half_b),
        "B1": (half_b, ROWS),
    }[part]


def ring_sends(axis, sources, size, out, kind, prio):
    far = size // 2
    arrived = []
    for (offset, part, dep) in sources:
        if len(part) == 1:
            arrived.append((offset, part, dep))
            halves = [(part, +1, far - 1), (part, -1, far - 1)]
        else:
            arrived.append((offset, part, dep))
            sign = +1 if part[1] == "0" else -1
            halves = [(part, +1, far - 1), (part, -1, far - 1)]
        for (piece, sign, hops) in halves:
            last = dep
            at = offset
            for hop in range(1, hops + 1):
                out.append(dict(kind=kind, axis=axis, sign=sign, origin=at, part=piece, dep=last, left=far - hop, prio=prio))
                last = len(out) - 1
                at = step_offset(at, axis, sign)
                arrived.append((at, piece, last))
            for digit, way in (("0", +1), ("1", -1)):
                if way != sign:
                    continue
                tail = piece if len(piece) == 2 else piece + digit
                if tail[1] != digit:
                    continue
                out.append(dict(kind=kind, axis=axis, sign=sign, origin=at, part=tail, dep=last, left=0, prio=prio))
                arrived.append((step_offset(at, axis, sign), tail, len(out) - 1))
    return arrived


def step_offset(offset, axis, sign):
    ox, oz = offset
    return (ox + sign, oz) if axis == "x" else (ox, oz + sign)


def plan_sends():
    out = []
    for kind in (0, 1):
        own = -1 - kind
        first_a = ring_sends("x", [((0, 0), "A", own)], NX, out, kind, kind * 10)
        first_b = ring_sends("z", [((0, 0), "B", own)], NZ, out, kind, kind * 10)
        ring_sends("z", first_a, NZ, out, kind, kind * 10 + 1)
        ring_sends("x", first_b, NX, out, kind, kind * 10 + 1)
    rate = 46.0e3 * 1.0
    latency = 1.7
    ready_own = {-1: 4.0, -2: 8.0}
    arrival = {}
    free = {}
    start = {}
    waiting = {}
    events = []
    for i, m in enumerate(out):
        if m["dep"] < 0:
            heapq.heappush(events, (ready_own[m["dep"]], i))
    children = {}
    for i, m in enumerate(out):
        if m["dep"] >= 0:
            children.setdefault(m["dep"], []).append(i)
    queues = {("x", 1): [], ("x", -1): [], ("z", 1): [], ("z", -1): []}
    free = {k: 0.0 for k in queues}
    order = []
    while events or any(queues.values()):
        options = []
        for k, q in queues.items():
            if q:
                options.append((max(free[k], q[0][2]), k))
        next_link = min(options) if options else None
        if events and (next_link is None or events[0][0] <= next_link[0]):
            t, i = heapq.heappop(events)
            m = out[i]
            q = queues[(m["axis"], m["sign"])]
            q.append((m["prio"] // 10, -m["left"], t, i))
            q.sort(key=lambda e: (e[0], e[1], e[2], e[3]))
            continue
        t, k = next_link
        _, _, ready, i = queues[k].pop(0)
        m = out[i]
        lo, hi = row_range(m["part"])
        begin = max(free[k], ready)
        free[k] = begin + (hi - lo) * HD * 2 * 2 / rate
        start[i] = begin
        order.append((begin, ready, i))
        for c in children.get(i, []):
            heapq.heappush(events, (free[k] + latency, c))
    order.sort()
    return out, [i for (_, _, i) in order], max(free.values())


SENDS, ORDER, SPAN = plan_sends()


def exchange_kernel(q_ref, k_ref, v_ref, g_ref, kv_ref, qg_ref, send_sem, recv_sem, head_send, head_recv, own_sem):
    seq = lax.axis_index("seq")
    head = lax.axis_index("head")
    x, z = lax.rem(seq, NX), seq // NX

    def chip(cx, cz):
        return lax.rem(cz + 2 * NZ, NZ) * NX + lax.rem(cx + 2 * NX, NX)

    barrier = pltpu.get_barrier_semaphore()
    for shift in range(1, NH):
        pl.semaphore_signal(barrier, inc=1, device_id={"seq": seq, "head": lax.rem(head + shift, NH)}, device_id_type=MESH)
    for (cx, cz) in ((x + 1, z), (x - 1, z), (x, z + 1), (x, z - 1)):
        pl.semaphore_signal(barrier, inc=1, device_id={"seq": chip(cx, cz), "head": head}, device_id_type=MESH)
    pl.semaphore_wait(barrier, NH - 1 + 4)

    targets = ((k_ref, kv_ref, 0), (v_ref, kv_ref, 1), (q_ref, qg_ref, 0), (g_ref, qg_ref, 1))

    def rows_of(dst, which, h):
        return dst.at[seq, which, pl.ds(pl.multiple_of(h * CHUNK, CHUNK), CHUNK), :]

    def columns_of(src, h):
        return src.at[:, pl.ds(pl.multiple_of(h * HD, HD), HD)]

    head_copies = []
    own_copies = []
    for array, (src, dst, which) in enumerate(targets):
        for shift in range(1, NH):
            peer = lax.rem(head + shift, NH)
            copy = pltpu.make_async_remote_copy(
                src_ref=columns_of(src, peer),
                dst_ref=rows_of(dst, which, head),
                send_sem=head_send.at[array, shift],
                recv_sem=head_recv.at[array, shift],
                device_id={"seq": seq, "head": peer},
                device_id_type=MESH,
            )
            copy.start()
            head_copies.append(copy)
        own = pltpu.make_async_copy(columns_of(src, head), rows_of(dst, which, head), own_sem.at[array])
        own.start()
        own_copies.append(own)

    def wait_head(array):
        src, dst, which = targets[array]
        for shift in range(1, NH):
            peer = lax.rem(head + NH - shift, NH)
            pltpu.make_async_remote_copy(
                src_ref=columns_of(src, peer),
                dst_ref=rows_of(dst, which, peer),
                send_sem=head_send.at[array, shift],
                recv_sem=head_recv.at[array, shift],
                device_id={"seq": seq, "head": peer},
                device_id_type=MESH,
            ).wait_recv()
        own_copies[array].wait()

    buffers = (kv_ref, qg_ref)

    def piece(m, ox, oz):
        lo, hi = row_range(m["part"])
        return buffers[m["kind"]].at[chip(x - ox, z - oz), :, lo:hi, :]

    def send(i):
        m = SENDS[i]
        ox, oz = m["origin"]
        target = chip(x + m["sign"], z) if m["axis"] == "x" else chip(x, z + m["sign"])
        return pltpu.make_async_remote_copy(
            src_ref=piece(m, ox, oz),
            dst_ref=piece(m, ox, oz),
            send_sem=send_sem.at[i],
            recv_sem=recv_sem.at[i],
            device_id={"seq": target, "head": head},
            device_id_type=MESH,
        )

    def wait_recv(i):
        m = SENDS[i]
        ox, oz = step_offset(m["origin"], m["axis"], m["sign"])
        source = chip(x - m["sign"], z) if m["axis"] == "x" else chip(x, z - m["sign"])
        pltpu.make_async_remote_copy(
            src_ref=piece(m, ox, oz),
            dst_ref=piece(m, ox, oz),
            send_sem=send_sem.at[i],
            recv_sem=recv_sem.at[i],
            device_id={"seq": source, "head": head},
            device_id_type=MESH,
        ).wait_recv()

    ready = set()
    started = []
    for i in ORDER:
        dep = SENDS[i]["dep"]
        if dep not in ready:
            ready.add(dep)
            if dep < 0:
                wait_head(2 * (-1 - dep))
                wait_head(2 * (-1 - dep) + 1)
            else:
                wait_recv(dep)
        copy = send(i)
        copy.start()
        started.append(copy)
    for i in ORDER:
        if i not in ready:
            wait_recv(i)
    for copy in started:
        copy.wait_send()
    for copy in head_copies:
        copy.wait_send()


def exchange(queries, keys, values, out_grad):
    shape = jax.ShapeDtypeStruct((NX * NZ, 2, ROWS, HD), BF16)
    count = len(SENDS)
    return pl.pallas_call(
        exchange_kernel,
        out_shape=(shape, shape),
        in_specs=[pl.BlockSpec(memory_space=pltpu.VMEM)] * 4,
        out_specs=[pl.BlockSpec(memory_space=pl.ANY)] * 2,
        scratch_shapes=[
            pltpu.SemaphoreType.DMA((count,)),
            pltpu.SemaphoreType.DMA((count,)),
            pltpu.SemaphoreType.DMA((4, NH)),
            pltpu.SemaphoreType.DMA((4, NH)),
            pltpu.SemaphoreType.DMA((4,)),
        ],
        compiler_params=pltpu.CompilerParams(collective_id=0, has_side_effects=True),
    )(queries, keys, values, out_grad)


def dot_nt(a, b):
    return lax.dot_general(a, b, (((1,), (1,)), ((), ())), preferred_element_type=F32)


def dot_nn(a, b):
    return lax.dot_general(a, b, (((1,), (0,)), ((), ())), preferred_element_type=F32)


def dot_tn(a, b):
    return lax.dot_general(a, b, (((0,), (0,)), ((), ())), preferred_element_type=F32)


def attend_kernel(first_ref, touch_ref, blocks_ref, counts_ref, kv_ref, qg_ref, att_ref, dq_ref, dk_ref, dv_ref, s_ref, acc_ref, dk_acc, dv_acc):
    scale = 1.0 / math.sqrt(HD)
    dk_acc[...] = jnp.zeros_like(dk_acc)
    dv_acc[...] = jnp.zeros_like(dv_acc)
    first = first_ref[0]

    def load(ref, which, block):
        return ref[block // 4, which, pl.ds(pl.multiple_of(lax.rem(block, 4) * BLK, BLK), BLK), :]

    def query_block(a, local):
        count = counts_ref[a]
        q = load(qg_ref, 0, a)
        g = load(qg_ref, 1, a)

        def score(t, row_max):
            s = dot_nt(q, load(kv_ref, 0, blocks_ref[a, t])) * scale
            s_ref[t] = s
            return jnp.maximum(row_max, jnp.max(s, axis=1, keepdims=True))

        row_max = lax.fori_loop(0, count, score, jnp.full((BLK, 1), NEG, F32))
        acc_ref[...] = jnp.zeros_like(acc_ref)

        def mix(t, row_sum):
            w = jnp.exp(s_ref[t] - row_max)
            acc_ref[...] += dot_nn(w.astype(BF16), load(kv_ref, 1, blocks_ref[a, t]))
            return row_sum + jnp.sum(w, axis=1, keepdims=True)

        row_sum = lax.fori_loop(0, count, mix, jnp.zeros((BLK, 1), F32))
        att = (acc_ref[...] / row_sum).astype(BF16)
        total = row_max + jnp.log(row_sum)
        grad_dot = jnp.sum(g.astype(F32) * att.astype(F32), axis=1, keepdims=True)

        def pair(t):
            block = blocks_ref[a, t]
            p = jnp.exp(s_ref[t] - total)
            dp = dot_nt(g, load(kv_ref, 1, block))
            return block, p, (p * (dp - grad_dot)).astype(BF16)

        def add_key(slot, p, ds):
            dk_acc[slot] += dot_tn(ds, q)
            dv_acc[slot] += dot_tn(p.astype(BF16), g)

        if local:
            acc_ref[...] = jnp.zeros_like(acc_ref)

            def back(t, carry):
                block, p, ds = pair(t)
                acc_ref[...] += dot_nn(ds, load(kv_ref, 0, block))
                slot = block - first

                @pl.when((slot >= 0) & (slot < 4))
                def _():
                    add_key(slot, p, ds)

                return carry

            lax.fori_loop(0, count, back, 0)
            rows = pl.ds(pl.multiple_of((a - first) * BLK, BLK), BLK)
            att_ref[rows, :] = att
            dq_ref[rows, :] = (acc_ref[...] * scale).astype(BF16)
        else:

            def back(t, carry):
                slot = blocks_ref[a, t] - first

                @pl.when((slot >= 0) & (slot < 4))
                def _():
                    _, p, ds = pair(t)
                    add_key(slot, p, ds)

                return carry

            lax.fori_loop(0, count, back, 0)

    def own(i, carry):
        query_block(first + i, True)
        return carry

    lax.fori_loop(0, 4, own, 0)

    def other(a, carry):
        @pl.when(touch_ref[a] > 0)
        def _():
            query_block(a, False)

        return carry

    lax.fori_loop(0, 128, other, 0)
    for slot in range(4):
        dk_ref[slot * BLK : (slot + 1) * BLK, :] = (dk_acc[slot] * scale).astype(BF16)
        dv_ref[slot * BLK : (slot + 1) * BLK, :] = dv_acc[slot].astype(BF16)


def attend(first, touch, key_blocks, counts, kv, qg):
    shape = jax.ShapeDtypeStruct((ROWS, HD), BF16)
    smem = pl.BlockSpec(memory_space=pltpu.SMEM)
    vmem = pl.BlockSpec(memory_space=pltpu.VMEM)
    return pl.pallas_call(
        attend_kernel,
        out_shape=(shape,) * 4,
        in_specs=[smem] * 4 + [vmem] * 2,
        out_specs=[vmem] * 4,
        scratch_shapes=[
            pltpu.VMEM((8, BLK, BLK), F32),
            pltpu.VMEM((BLK, HD), F32),
            pltpu.VMEM((4, BLK, HD), F32),
            pltpu.VMEM((4, BLK, HD), F32),
        ],
    )(first, touch, key_blocks, counts, kv, qg)


LAG = 2
STEPS = 33
VARIANTS = ((24, 20), (27, 23), (33, 30))
PACK = 24
GROUP = 4
OWN_QG = 3
PASS_KV = 4
NEAR_KV = 6
ALL_KV = 8
PASS_QG = 10
NEAR_QG = 12
ALL_QG = 14
CTL = 2048
AT_CODE = 128
AT_PICK = 160
AT_COUNT = 161
AT_USED = 164
AT_LIST = 256
AT_PAIRS = 1024


def plan_kernel(blocks_ref, counts_ref, ctl_ref, pick_ref, words_ref, words, where_kv, where_qg, sem):
    seq = lax.axis_index("seq")
    x, z = lax.rem(seq, NX), seq // NX
    brow = lax.broadcasted_iota(jnp.int32, (BLK, BLK), 0)
    count = counts_ref[...]
    hits = jnp.zeros((BLK, BLK), F32)
    for t in range(8):
        hits = jnp.where((blocks_ref[t : t + 1, :] == brow) & (count > t), 1.0, hits)
    row = lax.broadcasted_iota(jnp.int32, (32, BLK), 0)
    col = lax.broadcasted_iota(jnp.int32, (32, BLK), 1)
    device = lax.rem(row, NZ) * NX + row // NZ
    group = jnp.where(col // 4 == device, 1.0, 0.0)
    need_kv = dot_nt(group, hits)
    need_qg = dot_nn(group, hits)
    jrow = lax.broadcasted_iota(jnp.int32, (8, BLK), 0)
    jcol = lax.broadcasted_iota(jnp.int32, (8, BLK), 1)
    mine = jcol - seq * 4
    power = jnp.where(mine == 0, 1.0, jnp.where(mine == 1, 2.0, jnp.where(mine == 2, 4.0, jnp.where(mine == 3, 8.0, 0.0))))
    quad = lax.rem(lax.broadcasted_iota(jnp.int32, (BLK, BLK), 1), 4)
    digit = jnp.where(quad == 0, 1.0, jnp.where(quad == 1, 16.0, jnp.where(quad == 2, 256.0, 4096.0)))
    digit = jnp.where(lax.broadcasted_iota(jnp.int32, (BLK, BLK), 1) // 4 == brow, digit, 0.0)
    bits = dot_nt(dot_nn(power, hits), digit)

    origin = jcol // 16
    delta = lax.rem(jrow - origin + NZ, NZ)
    near = (delta >= 1) & (delta < 4)
    back = delta > 4
    tie = delta == 4
    far = delta.astype(F32)
    zero = jnp.zeros((8, BLK), F32)

    hops = [zero, zero]
    for column in range(NX):
        parts = [need[column * NZ : (column + 1) * NZ, :] > 0.5 for need in (need_kv, need_qg)]
        lean = zero
        for part in parts:
            lean = lean + jnp.where(part & near, 1.0, 0.0) - jnp.where(part & back, 1.0, 0.0)
        lean = jnp.broadcast_to(jnp.sum(lean, axis=1, keepdims=True), (8, BLK))
        ahead = near | (tie & (lean < 0.0))
        behind = back | (tie & (lean >= 0.0))
        for kind, part in enumerate(parts):
            for half in range(2):
                hop = jnp.where(part & ahead, far, 0.0) if half == 0 else jnp.where(part & behind, 8.0 - far, 0.0)
                most = jnp.broadcast_to(jnp.max(hop, axis=0, keepdims=True), (8, BLK))
                hops[kind] = jnp.where(jrow == column * 2 + half, most, hops[kind])

    lanes = lax.broadcasted_iota(jnp.int32, (BLK, BLK), 1)
    spread = jnp.where(jcol // 8 == jrow, 1.0, 0.0)
    lands = (brow // 16 == lax.rem(lanes, 8)) & (lanes < 64)
    sub16 = lax.broadcasted_iota(jnp.int32, (16, BLK), 0)
    lane16 = lax.broadcasted_iota(jnp.int32, (16, BLK), 1)
    fold = jnp.where(lax.rem(lane16, 16) == sub16, 1.0, 0.0)
    ident = (127 - lax.rem(lane16, 8) * 16 - sub16).astype(F32)
    apart = lax.rem(sub16 // 4 - lane16 // 16 + 2 * NX, NX)
    own, close = apart == 0, apart != 2
    low = lax.rem(sub16, 4) < 2
    first = own | ((apart == 3) & low) | ((apart == 1) & jnp.logical_not(low))
    keys = []
    for kind, base in ((0, 2048.0), (1, 0.0)):
        most = dot_nn(fold, jnp.where(lands, dot_tn(hops[kind], spread), 0.0))
        keys.append(jnp.where(most > 0.5, most * 128.0 + base + ident, 0.0))
    kv, qg = keys
    at_z = lax.rem(jcol, 8)
    forward = lax.rem(jcol // 8, 2) == 0
    history = []
    last_any, last_kv = zero, zero
    for t in range(STEPS):
        best = kv if t >= ALL_KV else jnp.where(close if t >= NEAR_KV else first if t >= PASS_KV else own, kv, 0.0)
        if t >= OWN_QG:
            best = jnp.maximum(best, qg if t >= ALL_QG else jnp.where(close if t >= NEAR_QG else first if t >= PASS_QG else own, qg, 0.0))
        best = jnp.broadcast_to(jnp.max(best, axis=0, keepdims=True), (8, BLK))
        if t >= LAG:
            before = history[t - LAG]
            up = jnp.where(at_z == 0, pltpu.roll(before, BLK - 7, 1), pltpu.roll(before, 1, 1))
            down = jnp.where(at_z == 7, pltpu.roll(before, 7, 1), pltpu.roll(before, BLK - 1, 1))
            passing = jnp.where(forward, up, down) - 128.0
            left = jnp.where(passing >= 2048.0, passing - 2048.0, passing)
            through = left > 127.5
            taken = jnp.where(through, -1.0, best)
            sent = jnp.where(through, passing, best)
            mark = jnp.where(through, -passing, best)
        else:
            taken, sent, mark = best, best, best
        taken = jnp.concatenate([taken, taken], axis=0)
        kv = jnp.where(kv == taken, 0.0, kv)
        qg = jnp.where(qg == taken, 0.0, qg)
        history.append(sent)
        last_any = jnp.where(sent > 0.0, t + 1.0, last_any)
        last_kv = jnp.where(sent >= 2048.0, t + 1.0, last_kv)
        words_ref[t : t + 1, :] = mark[0:1, :].astype(jnp.int32)
    remain = jnp.maximum(kv, qg)
    last_any = jnp.where(jnp.maximum(remain[0:8, :], remain[8:16, :]) > 0.0, 999.0, last_any)
    for t in range(STEPS - LAG, STEPS):
        left = jnp.where(history[t] >= 2048.0, history[t] - 2048.0, history[t])
        last_any = jnp.where(left > 255.5, 999.0, last_any)
    last_any = jnp.max(jnp.max(last_any, axis=1, keepdims=True), axis=0, keepdims=True)
    last_kv = jnp.max(jnp.max(last_kv, axis=1, keepdims=True), axis=0, keepdims=True)
    index = jnp.zeros((1, 1), F32)
    for steps, kv_steps in VARIANTS:
        index = index + jnp.where((last_any > steps + 0.5) | (last_kv > kv_steps + 0.5), 1.0, 0.0)
    crowd = jnp.max(jnp.sum(jnp.where(need_qg > 0.5, 1.0, 0.0), axis=1, keepdims=True), axis=0, keepdims=True)
    index = jnp.where(crowd > PACK + 0.5, float(len(VARIANTS)), index)
    words_ref[40:48, :] = blocks_ref[...]
    misc = jnp.where(jrow == 0, bits.astype(jnp.int32), jnp.broadcast_to(count, (8, BLK)))
    words_ref[48:56, :] = jnp.where(jrow == 2, jnp.broadcast_to(index, (8, BLK)).astype(jnp.int32), misc)
    copy = pltpu.make_async_copy(words_ref, words, sem)
    copy.start()
    copy.wait()

    pick_ref[0] = words[50, 0]
    for i in range(16):
        where_kv[z * 16 + i] = i
        where_qg[z * 16 + i] = i
    sources = (lax.rem(z + NZ - 1, NZ), lax.rem(z + 1, NZ))

    def slot(t, carry):
        for half in range(2):
            ctl_ref[2 * t + half] = words[t, (2 * x + half) * 8 + z]
            value = jnp.abs(words[t, (2 * x + half) * 8 + sources[half]])
            block = 127 - (value & 127)
            spot = 16 + 2 * t + half

            @pl.when(value >= 2048)
            def _():
                where_kv[block] = spot

            @pl.when((value >= 128) & (value < 2048))
            def _():
                where_qg[block] = spot

        return carry

    lax.fori_loop(0, STEPS, slot, 0)
    for i in range(4):
        live = words[49, 4 * seq + i]
        ctl_ref[AT_USED + i] = live
        for t in range(8):
            block = jnp.where(t < live, words[40 + t, 4 * seq + i], 4 * seq + i)
            ctl_ref[AT_CODE + i * 8 + t] = where_kv[block]

    def entry(group, totals):
        word = words[48, group]

        def listed(totals):
            n, pairs = totals
            for r in range(4):
                a = 4 * group + r
                mask = (word >> (4 * r)) & 15
                ctl_ref[AT_LIST + n] = where_qg[a]
                for j in range(4):
                    ctl_ref[AT_PAIRS + pairs] = n + a * 256 + j * 65536
                    pairs = pairs + ((mask >> j) & 1)
                n = n + jnp.where(mask > 0, 1, 0)
            return n, pairs

        return lax.cond(word > 0, listed, lambda totals: totals, totals)

    ctl_ref[AT_COUNT] = lax.fori_loop(0, BLK // 4, entry, (0, 0))[1]


def make_plan(key_blocks, counts):
    vmem = pl.BlockSpec(memory_space=pltpu.VMEM)
    return pl.pallas_call(
        plan_kernel,
        out_shape=(jax.ShapeDtypeStruct((CTL,), jnp.int32), jax.ShapeDtypeStruct((1,), jnp.int32)),
        in_specs=[vmem, vmem],
        out_specs=[pl.BlockSpec(memory_space=pltpu.SMEM)] * 2,
        scratch_shapes=[
            pltpu.VMEM((56, BLK), jnp.int32),
            pltpu.SMEM((56, BLK), jnp.int32),
            pltpu.SMEM((BLK,), jnp.int32),
            pltpu.SMEM((BLK,), jnp.int32),
            pltpu.SemaphoreType.DMA,
        ],
    )(key_blocks, counts)


def route_kernel(
    steps, kv_steps,
    ctl_ref, q_ref, k_ref, v_ref, g_ref,
    att_ref, dq_ref, own_kv, pack_ref, stats_ref,
    own_qg, row_kv, row_qg, land_kv, land_qg, recv_ref, late_ref, send_ref, kcat, vcat, probs, dots, mine_stats,
    head_send, head_recv, own_sem, x_send, x_recv, z_send, z_recv, s_send, s_recv,
):
    seq = lax.axis_index("seq")
    head = lax.axis_index("head")
    x, z = lax.rem(seq, NX), seq // NX

    def chip(cx, cz):
        return lax.rem(cz + 2 * NZ, NZ) * NX + lax.rem(cx + 2 * NX, NX)

    barrier = pltpu.get_barrier_semaphore()
    for shift in range(1, NH):
        pl.semaphore_signal(barrier, inc=1, device_id={"seq": seq, "head": lax.rem(head + shift, NH)}, device_id_type=MESH)
    for (cx, cz) in ((x + 1, z), (x - 1, z), (x, z + 1), (x, z - 1)):
        pl.semaphore_signal(barrier, inc=1, device_id={"seq": chip(cx, cz), "head": head}, device_id_type=MESH)
    pl.semaphore_wait(barrier, NH - 1 + 4)

    targets = ((k_ref, own_kv, 0), (v_ref, own_kv, 1), (q_ref, own_qg, 0), (g_ref, own_qg, 1))

    def rows_of(dst, which, h):
        start = pl.multiple_of(which * BLK + lax.rem(h, 2) * CHUNK, CHUNK)
        return dst.at[h // 2, pl.ds(start, CHUNK), :]

    def columns_of(src, h):
        return src.at[:, pl.ds(pl.multiple_of(h * HD, HD), HD)]

    def head_copy(array, peer_from, peer_to, shift):
        src, dst, which = targets[array]
        return pltpu.make_async_remote_copy(
            src_ref=columns_of(src, peer_to),
            dst_ref=rows_of(dst, which, peer_from),
            send_sem=head_send.at[array, shift],
            recv_sem=head_recv.at[array, shift],
            device_id={"seq": seq, "head": peer_to},
            device_id_type=MESH,
        )

    started = []
    own_copies = []
    for array, (src, dst, which) in enumerate(targets):
        for shift in range(1, NH):
            copy = head_copy(array, head, lax.rem(head + shift, NH), shift)
            copy.start()
            started.append(copy)
        own = pltpu.make_async_copy(columns_of(src, head), rows_of(dst, which, head), own_sem.at[array])
        own.start()
        own_copies.append(own)

    def wait_head(array):
        for shift in range(1, NH):
            peer = lax.rem(head + NH - shift, NH)
            head_copy(array, peer, peer, shift).wait_recv()
        own_copies[array].wait()

    owned = (own_kv, own_qg)
    rows = (row_kv, row_qg)
    x_plan = ((1, 0, 0), (-1, 0, 2), (1, 0, 2), (-1, 0, 0), (1, 1, 0), (-1, -1, 2))

    lands = (land_kv, land_qg)

    def x_copy(kind, i, arriving):
        sign, offset, first = x_plan[i]
        landed = lands[kind].at[2 * i : 2 * i + 2]
        source = landed if arriving else lands[kind].at[2 * i - 8 : 2 * i - 6] if offset != 0 else owned[kind].at[pl.ds(first, 2)]
        other = chip(x - sign, z) if arriving else chip(x + sign, z)
        return pltpu.make_async_remote_copy(
            src_ref=source, dst_ref=landed, send_sem=x_send.at[kind, i], recv_sem=x_recv.at[kind, i],
            device_id={"seq": other, "head": head}, device_id_type=MESH,
        )

    def keep_piece(kind, i):
        sign, offset, first = x_plan[i]
        origin = lax.rem(x - offset - sign + 2 * NX, NX)
        for r in range(2):
            rows[kind][4 * origin + first + r] = lands[kind][2 * i + r]

    def x_start(kind, i):
        copy = x_copy(kind, i, False)
        copy.start()
        started.append(copy)

    def landing(t, half):
        return recv_ref.at[2 * t + half] if t < kv_steps else late_ref.at[2 * (t - kv_steps) + half]

    def z_copy(half, t, part, arriving):
        sign = 1 if half == 0 else -1
        other = chip(x, z - sign) if arriving else chip(x, z + sign)
        slot = 2 * t + half
        rows = slice(part * BLK, part * BLK + BLK)
        return pltpu.make_async_remote_copy(
            src_ref=send_ref.at[slot, rows], dst_ref=landing(t, half).at[rows],
            send_sem=z_send.at[slot, part], recv_sem=z_recv.at[slot, part],
            device_id={"seq": other, "head": head}, device_id_type=MESH,
        )

    scale = 1.0 / math.sqrt(HD)
    key_at = lax.broadcasted_iota(jnp.int32, (1, 8 * BLK), 1)

    def attend_block(i):
        for t in range(8):
            code = ctl_ref[AT_CODE + i * 8 + t]
            near = row_kv[jnp.minimum(code, 15)]
            moved = recv_ref[jnp.clip(code - 16, 0, 2 * kv_steps - 1)]
            data = lax.select(code < 16, near, moved)
            kcat[i, t * BLK : (t + 1) * BLK, :] = data[0:BLK]
            vcat[i, t * BLK : (t + 1) * BLK, :] = data[BLK : 2 * BLK]
        q, g = own_qg[i, 0:BLK], own_qg[i, BLK : 2 * BLK]
        s = dot_nt(q, kcat[i]) * scale + jnp.where(key_at < ctl_ref[AT_USED + i] * BLK, 0.0, NEG)
        row_max = jnp.max(s, axis=1, keepdims=True)
        w = jnp.exp(s - row_max)
        row_sum = jnp.sum(w, axis=1, keepdims=True)
        scaled = 1.0 / row_sum
        att = (dot_nn(w.astype(BF16), vcat[i]) * scaled).astype(BF16)
        total = row_max + jnp.log(row_sum)
        grad_dot = jnp.sum(g.astype(F32) * att.astype(F32), axis=1, keepdims=True)
        probs[i] = w * scaled
        dots[i] = jnp.broadcast_to(grad_dot, (BLK, BLK))
        att_ref[i * BLK : (i + 1) * BLK, :] = att
        mine_stats[i : i + 1, :] = jnp.transpose(jnp.broadcast_to(total, (BLK, BLK)))[0:1, :]
        mine_stats[i + 4 : i + 5, :] = jnp.transpose(jnp.broadcast_to(grad_dot, (BLK, BLK)))[0:1, :]

    def query_grad(i):
        g = own_qg[i, BLK : 2 * BLK]
        ds = (probs[i] * (dot_nt(g, vcat[i]) - dots[i, :, 0:1])).astype(BF16)
        dq_ref[i * BLK : (i + 1) * BLK, :] = (dot_nn(ds, kcat[i]) * scale).astype(BF16)

    def stat_copy(shift, origin, target):
        return pltpu.make_async_remote_copy(
            src_ref=mine_stats, dst_ref=stats_ref.at[origin], send_sem=s_send.at[shift], recv_sem=s_recv.at[shift],
            device_id={"seq": target, "head": head}, device_id_type=MESH,
        )

    def keep_own(kind):
        for i in range(4):
            rows[kind][4 * x + i] = owned[kind][i]

    def take(kind, *pieces):
        for i in pieces:
            x_copy(kind, i, True).wait_recv()
            if i < 2:
                x_start(kind, i + 4)
        for i in pieces:
            keep_piece(kind, i)

    wait_head(0)
    wait_head(1)
    for i in range(4):
        x_start(0, i)

    def send_stats():
        for shift in range(1, NX * NZ):
            copy = stat_copy(shift, seq, lax.rem(seq + shift, NX * NZ))
            copy.start()
            started.append(copy)
        own = pltpu.make_async_copy(mine_stats, stats_ref.at[seq], s_recv.at[0])
        own.start()
        own_copies.append(own)

    work = [functools.partial(attend_block, i) for i in range(4)] + [send_stats]
    work += [functools.partial(query_grad, i) for i in range(4)]
    for t in range(steps):
        if t == OWN_QG:
            wait_head(2)
            wait_head(3)
        elif t == PASS_KV:
            take(0, 0, 1)
            for i in range(4):
                x_start(1, i)
            keep_own(0)
            keep_own(1)
        elif t == NEAR_KV:
            take(0, 2, 3)
        elif t == ALL_KV:
            take(0, 4, 5)
        elif t == PASS_QG:
            take(1, 0, 1)
        elif t == NEAR_QG:
            take(1, 2, 3)
        elif t == ALL_QG:
            take(1, 4, 5)
        for part in range(2):
            rows_at = slice(part * BLK, part * BLK + BLK)
            for half in range(2):
                slot = 2 * t + half
                value = ctl_ref[slot]
                size = jnp.abs(value)
                index = (127 - (size & 127)) & 15
                data = row_kv[index, rows_at] if t >= PASS_KV else own_kv[index & 3, rows_at]
                if t >= OWN_QG:
                    other = row_qg[index, rows_at] if t >= PASS_QG else own_qg[index & 3, rows_at]
                    data = lax.select(size >= 2048, data, other)
                if t >= LAG:
                    z_copy(half, t - LAG, part, True).wait_recv()
                    data = lax.select(value < 0, landing(t - LAG, half)[rows_at], data)
                send_ref[slot, rows_at] = data
            for half in range(2):
                copy = z_copy(half, t, part, False)
                copy.start()
                started.append(copy)
        if t >= kv_steps + LAG - 1 and work:
            work.pop(0)()
    while work:
        work.pop(0)()
    for t in range(steps - LAG, steps):
        for half in range(2):
            for part in range(2):
                z_copy(half, t, part, True).wait_recv()
    for n in range(PACK):
        code = ctl_ref[AT_LIST + n]
        data = lax.select(code < 16, row_qg[jnp.clip(code, 0, 15)], recv_ref[jnp.clip(code - 16, 0, 2 * kv_steps - 1)])
        last = 16 + 2 * kv_steps
        pack_ref[n] = lax.select(code < last, data, late_ref[jnp.clip(code - last, 0, 2 * (steps - kv_steps) - 1)])
    for shift in range(1, NX * NZ):
        peer = lax.rem(seq + NX * NZ - shift, NX * NZ)
        stat_copy(shift, peer, peer).wait_recv()
    own_copies[-1].wait()
    for copy in started:
        copy.wait_send()


def route(variant, ctl, queries, keys, values, out_grad):
    steps, kv_steps = VARIANTS[variant]
    smem = pl.BlockSpec(memory_space=pltpu.SMEM)
    vmem = pl.BlockSpec(memory_space=pltpu.VMEM)
    out = jax.ShapeDtypeStruct((ROWS, HD), BF16)
    own = (4, 2 * BLK, HD)
    near = (16, 2 * BLK, HD)
    moved = (2 * steps, 2 * BLK, HD)
    early = (2 * kv_steps, 2 * BLK, HD)
    late = (2 * (steps - kv_steps), 2 * BLK, HD)
    stats = jax.ShapeDtypeStruct((NX * NZ, 8, BLK), F32)
    dma = pltpu.SemaphoreType.DMA
    return pl.pallas_call(
        functools.partial(route_kernel, steps, kv_steps),
        out_shape=(out, out, jax.ShapeDtypeStruct(own, BF16), jax.ShapeDtypeStruct((PACK, 2 * BLK, HD), BF16), stats),
        in_specs=[smem] + [vmem] * 4,
        out_specs=[vmem] * 5,
        scratch_shapes=[
            pltpu.VMEM(own, BF16),
            pltpu.VMEM(near, BF16),
            pltpu.VMEM(near, BF16),
            pltpu.VMEM((12, 2 * BLK, HD), BF16),
            pltpu.VMEM((12, 2 * BLK, HD), BF16),
            pltpu.VMEM(early, BF16),
            pltpu.VMEM(late, BF16),
            pltpu.VMEM(moved, BF16),
            pltpu.VMEM((4, 8 * BLK, HD), BF16),
            pltpu.VMEM((4, 8 * BLK, HD), BF16),
            pltpu.VMEM((4, BLK, 8 * BLK), F32),
            pltpu.VMEM((4, BLK, BLK), F32),
            pltpu.VMEM((8, BLK), F32),
            dma((4, NH)), dma((4, NH)), dma((4,)),
            dma((2, 6)), dma((2, 6)),
            dma((2 * steps, 2)), dma((2 * steps, 2)),
            dma((NX * NZ,)), dma((NX * NZ,)),
        ],
        compiler_params=pltpu.CompilerParams(collective_id=1 + variant, has_side_effects=True),
    )(ctl, queries, keys, values, out_grad)


def keys_kernel(ctl_ref, kv_ref, pack_ref, stats_ref, att_ref, dq_ref, att_out, dq_out, dk_ref, dv_ref, dk_acc, dv_acc):
    scale = 1.0 / math.sqrt(HD)
    att_out[...] = att_ref[...]
    dq_out[...] = dq_ref[...]
    dk_acc[...] = jnp.zeros_like(dk_acc)
    dv_acc[...] = jnp.zeros_like(dv_acc)
    pairs = ctl_ref[AT_COUNT]

    def trip(i, carry):
        sums = []
        for u in range(GROUP):
            at = GROUP * i + u
            word = ctl_ref[AT_PAIRS + jnp.minimum(at, pairs - 1)]
            n, a, j = word & 255, (word >> 8) & 255, word >> 16
            unused = jnp.where(at < pairs, 0.0, 1e30)
            q, g = pack_ref[n, 0:BLK, :], pack_ref[n, BLK : 2 * BLK, :]
            total = stats_ref[a // 4, pl.ds(lax.rem(a, 4), 1), :] + unused
            grad_dot = stats_ref[a // 4, pl.ds(lax.rem(a, 4) + 4, 1), :]
            p = jnp.exp(dot_nt(kv_ref[j, 0:BLK, :], q) * scale - total)
            ds = (p * (dot_nt(kv_ref[j, BLK : 2 * BLK, :], g) - grad_dot)).astype(BF16)
            sums.append((j, dot_nn(ds, q), dot_nn(p.astype(BF16), g)))
        for j, dk, dv in sums:
            dk_acc[j] += dk
            dv_acc[j] += dv
        return carry

    lax.fori_loop(0, (pairs + GROUP - 1) // GROUP, trip, 0)
    for j in range(4):
        dk_ref[j * BLK : (j + 1) * BLK, :] = (dk_acc[j] * scale).astype(BF16)
        dv_ref[j * BLK : (j + 1) * BLK, :] = dv_acc[j].astype(BF16)


def key_grads(ctl, kv, pack, stats, att, dq):
    smem = pl.BlockSpec(memory_space=pltpu.SMEM)
    vmem = pl.BlockSpec(memory_space=pltpu.VMEM)
    out = jax.ShapeDtypeStruct((ROWS, HD), BF16)
    return pl.pallas_call(
        keys_kernel,
        out_shape=(out,) * 4,
        in_specs=[smem] + [vmem] * 5,
        out_specs=[vmem] * 4,
        scratch_shapes=[
            pltpu.VMEM((4, BLK, HD), F32),
            pltpu.VMEM((4, BLK, HD), F32),
        ],
    )(ctl, kv, pack, stats, att, dq)


def on_device(queries, keys, values, out_grad, key_blocks, counts):
    seq = lax.axis_index("seq")
    ctl, choice = make_plan(jnp.transpose(key_blocks), counts[None, :])

    def sparse(variant):
        att, dq, kv, pack, stats = route(variant, ctl, queries, keys, values, out_grad)
        return tuple(key_grads(ctl, kv, pack, stats, att, dq))

    def dense():
        kv, qg = exchange(queries, keys, values, out_grad)
        live = jnp.arange(key_blocks.shape[1])[None, :] < counts[:, None]
        touch = jnp.any(live & (key_blocks // 4 == seq), axis=1)
        touch = (touch & (jnp.arange(key_blocks.shape[0]) // 4 != seq)).astype(jnp.int32)
        first = (seq * 4).reshape(1).astype(jnp.int32)
        return tuple(attend(first, touch, key_blocks, counts, kv, qg))

    branches = [functools.partial(sparse, variant) for variant in range(len(VARIANTS))] + [dense]
    return lax.switch(choice[0], branches)


def solution(mesh):
    rows = P(("seq", "head"), None)
    out = P("seq", "head")
    return jax.shard_map(
        on_device,
        mesh=mesh,
        in_specs=(rows,) * 4 + (P(), P()),
        out_specs=(out,) * 4,
        check_vma=False,
    )
```

```python
import functools
import heapq
import math

import jax
import jax.numpy as jnp
from jax import lax
from jax.experimental import pallas as pl
from jax.experimental.pallas import tpu as pltpu
from jax.sharding import PartitionSpec as P

MESH = pl.DeviceIdType.MESH
BLK = 128
HD = 128
NX = 4
NZ = 8
NH = 8
ROWS = 512
CHUNK = 64
SPLIT = 208
BF16 = jnp.bfloat16
F32 = jnp.float32
NEG = -1e30


def row_range(part):
    half_a, half_b = SPLIT // 32 * 16, SPLIT + (ROWS - SPLIT) // 32 * 16
    return {
        "A": (0, SPLIT),
        "A0": (0, half_a),
        "A1": (half_a, SPLIT),
        "B": (SPLIT, ROWS),
        "B0": (SPLIT, half_b),
        "B1": (half_b, ROWS),
    }[part]


def ring_sends(axis, sources, size, out, kind, prio):
    far = size // 2
    arrived = []
    for (offset, part, dep) in sources:
        if len(part) == 1:
            arrived.append((offset, part, dep))
            halves = [(part, +1, far - 1), (part, -1, far - 1)]
        else:
            arrived.append((offset, part, dep))
            sign = +1 if part[1] == "0" else -1
            halves = [(part, +1, far - 1), (part, -1, far - 1)]
        for (piece, sign, hops) in halves:
            last = dep
            at = offset
            for hop in range(1, hops + 1):
                out.append(dict(kind=kind, axis=axis, sign=sign, origin=at, part=piece, dep=last, left=far - hop, prio=prio))
                last = len(out) - 1
                at = step_offset(at, axis, sign)
                arrived.append((at, piece, last))
            for digit, way in (("0", +1), ("1", -1)):
                if way != sign:
                    continue
                tail = piece if len(piece) == 2 else piece + digit
                if tail[1] != digit:
                    continue
                out.append(dict(kind=kind, axis=axis, sign=sign, origin=at, part=tail, dep=last, left=0, prio=prio))
                arrived.append((step_offset(at, axis, sign), tail, len(out) - 1))
    return arrived


def step_offset(offset, axis, sign):
    ox, oz = offset
    return (ox + sign, oz) if axis == "x" else (ox, oz + sign)


def plan_sends():
    out = []
    for kind in (0, 1):
        own = -1 - kind
        first_a = ring_sends("x", [((0, 0), "A", own)], NX, out, kind, kind * 10)
        first_b = ring_sends("z", [((0, 0), "B", own)], NZ, out, kind, kind * 10)
        ring_sends("z", first_a, NZ, out, kind, kind * 10 + 1)
        ring_sends("x", first_b, NX, out, kind, kind * 10 + 1)
    rate = 46.0e3 * 1.0
    latency = 1.7
    ready_own = {-1: 4.0, -2: 8.0}
    arrival = {}
    free = {}
    start = {}
    waiting = {}
    events = []
    for i, m in enumerate(out):
        if m["dep"] < 0:
            heapq.heappush(events, (ready_own[m["dep"]], i))
    children = {}
    for i, m in enumerate(out):
        if m["dep"] >= 0:
            children.setdefault(m["dep"], []).append(i)
    queues = {("x", 1): [], ("x", -1): [], ("z", 1): [], ("z", -1): []}
    free = {k: 0.0 for k in queues}
    order = []
    while events or any(queues.values()):
        options = []
        for k, q in queues.items():
            if q:
                options.append((max(free[k], q[0][2]), k))
        next_link = min(options) if options else None
        if events and (next_link is None or events[0][0] <= next_link[0]):
            t, i = heapq.heappop(events)
            m = out[i]
            q = queues[(m["axis"], m["sign"])]
            q.append((m["prio"] // 10, -m["left"], t, i))
            q.sort(key=lambda e: (e[0], e[1], e[2], e[3]))
            continue
        t, k = next_link
        _, _, ready, i = queues[k].pop(0)
        m = out[i]
        lo, hi = row_range(m["part"])
        begin = max(free[k], ready)
        free[k] = begin + (hi - lo) * HD * 2 * 2 / rate
        start[i] = begin
        order.append((begin, ready, i))
        for c in children.get(i, []):
            heapq.heappush(events, (free[k] + latency, c))
    order.sort()
    return out, [i for (_, _, i) in order], max(free.values())


SENDS, ORDER, SPAN = plan_sends()


def exchange_kernel(q_ref, k_ref, v_ref, g_ref, kv_ref, qg_ref, send_sem, recv_sem, head_send, head_recv, own_sem):
    seq = lax.axis_index("seq")
    head = lax.axis_index("head")
    x, z = lax.rem(seq, NX), seq // NX

    def chip(cx, cz):
        return lax.rem(cz + 2 * NZ, NZ) * NX + lax.rem(cx + 2 * NX, NX)

    barrier = pltpu.get_barrier_semaphore()
    for shift in range(1, NH):
        pl.semaphore_signal(barrier, inc=1, device_id={"seq": seq, "head": lax.rem(head + shift, NH)}, device_id_type=MESH)
    for (cx, cz) in ((x + 1, z), (x - 1, z), (x, z + 1), (x, z - 1)):
        pl.semaphore_signal(barrier, inc=1, device_id={"seq": chip(cx, cz), "head": head}, device_id_type=MESH)
    pl.semaphore_wait(barrier, NH - 1 + 4)

    targets = ((k_ref, kv_ref, 0), (v_ref, kv_ref, 1), (q_ref, qg_ref, 0), (g_ref, qg_ref, 1))

    def rows_of(dst, which, h):
        return dst.at[seq, which, pl.ds(pl.multiple_of(h * CHUNK, CHUNK), CHUNK), :]

    def columns_of(src, h):
        return src.at[:, pl.ds(pl.multiple_of(h * HD, HD), HD)]

    head_copies = []
    own_copies = []
    for array, (src, dst, which) in enumerate(targets):
        for shift in range(1, NH):
            peer = lax.rem(head + shift, NH)
            copy = pltpu.make_async_remote_copy(
                src_ref=columns_of(src, peer),
                dst_ref=rows_of(dst, which, head),
                send_sem=head_send.at[array, shift],
                recv_sem=head_recv.at[array, shift],
                device_id={"seq": seq, "head": peer},
                device_id_type=MESH,
            )
            copy.start()
            head_copies.append(copy)
        own = pltpu.make_async_copy(columns_of(src, head), rows_of(dst, which, head), own_sem.at[array])
        own.start()
        own_copies.append(own)

    def wait_head(array):
        src, dst, which = targets[array]
        for shift in range(1, NH):
            peer = lax.rem(head + NH - shift, NH)
            pltpu.make_async_remote_copy(
                src_ref=columns_of(src, peer),
                dst_ref=rows_of(dst, which, peer),
                send_sem=head_send.at[array, shift],
                recv_sem=head_recv.at[array, shift],
                device_id={"seq": seq, "head": peer},
                device_id_type=MESH,
            ).wait_recv()
        own_copies[array].wait()

    buffers = (kv_ref, qg_ref)

    def piece(m, ox, oz):
        lo, hi = row_range(m["part"])
        return buffers[m["kind"]].at[chip(x - ox, z - oz), :, lo:hi, :]

    def send(i):
        m = SENDS[i]
        ox, oz = m["origin"]
        target = chip(x + m["sign"], z) if m["axis"] == "x" else chip(x, z + m["sign"])
        return pltpu.make_async_remote_copy(
            src_ref=piece(m, ox, oz),
            dst_ref=piece(m, ox, oz),
            send_sem=send_sem.at[i],
            recv_sem=recv_sem.at[i],
            device_id={"seq": target, "head": head},
            device_id_type=MESH,
        )

    def wait_recv(i):
        m = SENDS[i]
        ox, oz = step_offset(m["origin"], m["axis"], m["sign"])
        source = chip(x - m["sign"], z) if m["axis"] == "x" else chip(x, z - m["sign"])
        pltpu.make_async_remote_copy(
            src_ref=piece(m, ox, oz),
            dst_ref=piece(m, ox, oz),
            send_sem=send_sem.at[i],
            recv_sem=recv_sem.at[i],
            device_id={"seq": source, "head": head},
            device_id_type=MESH,
        ).wait_recv()

    ready = set()
    started = []
    for i in ORDER:
        dep = SENDS[i]["dep"]
        if dep not in ready:
            ready.add(dep)
            if dep < 0:
                wait_head(2 * (-1 - dep))
                wait_head(2 * (-1 - dep) + 1)
            else:
                wait_recv(dep)
        copy = send(i)
        copy.start()
        started.append(copy)
    for i in ORDER:
        if i not in ready:
            wait_recv(i)
    for copy in started:
        copy.wait_send()
    for copy in head_copies:
        copy.wait_send()


def exchange(queries, keys, values, out_grad):
    shape = jax.ShapeDtypeStruct((NX * NZ, 2, ROWS, HD), BF16)
    count = len(SENDS)
    return pl.pallas_call(
        exchange_kernel,
        out_shape=(shape, shape),
        in_specs=[pl.BlockSpec(memory_space=pltpu.VMEM)] * 4,
        out_specs=[pl.BlockSpec(memory_space=pl.ANY)] * 2,
        scratch_shapes=[
            pltpu.SemaphoreType.DMA((count,)),
            pltpu.SemaphoreType.DMA((count,)),
            pltpu.SemaphoreType.DMA((4, NH)),
            pltpu.SemaphoreType.DMA((4, NH)),
            pltpu.SemaphoreType.DMA((4,)),
        ],
        compiler_params=pltpu.CompilerParams(collective_id=0, has_side_effects=True),
    )(queries, keys, values, out_grad)


def dot_nt(a, b):
    return lax.dot_general(a, b, (((1,), (1,)), ((), ())), preferred_element_type=F32)


def dot_nn(a, b):
    return lax.dot_general(a, b, (((1,), (0,)), ((), ())), preferred_element_type=F32)


def dot_tn(a, b):
    return lax.dot_general(a, b, (((0,), (0,)), ((), ())), preferred_element_type=F32)


def attend_kernel(first_ref, touch_ref, blocks_ref, counts_ref, kv_ref, qg_ref, att_ref, dq_ref, dk_ref, dv_ref, s_ref, acc_ref, dk_acc, dv_acc):
    scale = 1.0 / math.sqrt(HD)
    dk_acc[...] = jnp.zeros_like(dk_acc)
    dv_acc[...] = jnp.zeros_like(dv_acc)
    first = first_ref[0]

    def load(ref, which, block):
        return ref[block // 4, which, pl.ds(pl.multiple_of(lax.rem(block, 4) * BLK, BLK), BLK), :]

    def query_block(a, local):
        count = counts_ref[a]
        q = load(qg_ref, 0, a)
        g = load(qg_ref, 1, a)

        def score(t, row_max):
            s = dot_nt(q, load(kv_ref, 0, blocks_ref[a, t])) * scale
            s_ref[t] = s
            return jnp.maximum(row_max, jnp.max(s, axis=1, keepdims=True))

        row_max = lax.fori_loop(0, count, score, jnp.full((BLK, 1), NEG, F32))
        acc_ref[...] = jnp.zeros_like(acc_ref)

        def mix(t, row_sum):
            w = jnp.exp(s_ref[t] - row_max)
            acc_ref[...] += dot_nn(w.astype(BF16), load(kv_ref, 1, blocks_ref[a, t]))
            return row_sum + jnp.sum(w, axis=1, keepdims=True)

        row_sum = lax.fori_loop(0, count, mix, jnp.zeros((BLK, 1), F32))
        att = (acc_ref[...] / row_sum).astype(BF16)
        total = row_max + jnp.log(row_sum)
        grad_dot = jnp.sum(g.astype(F32) * att.astype(F32), axis=1, keepdims=True)

        def pair(t):
            block = blocks_ref[a, t]
            p = jnp.exp(s_ref[t] - total)
            dp = dot_nt(g, load(kv_ref, 1, block))
            return block, p, (p * (dp - grad_dot)).astype(BF16)

        def add_key(slot, p, ds):
            dk_acc[slot] += dot_tn(ds, q)
            dv_acc[slot] += dot_tn(p.astype(BF16), g)

        if local:
            acc_ref[...] = jnp.zeros_like(acc_ref)

            def back(t, carry):
                block, p, ds = pair(t)
                acc_ref[...] += dot_nn(ds, load(kv_ref, 0, block))
                slot = block - first

                @pl.when((slot >= 0) & (slot < 4))
                def _():
                    add_key(slot, p, ds)

                return carry

            lax.fori_loop(0, count, back, 0)
            rows = pl.ds(pl.multiple_of((a - first) * BLK, BLK), BLK)
            att_ref[rows, :] = att
            dq_ref[rows, :] = (acc_ref[...] * scale).astype(BF16)
        else:

            def back(t, carry):
                slot = blocks_ref[a, t] - first

                @pl.when((slot >= 0) & (slot < 4))
                def _():
                    _, p, ds = pair(t)
                    add_key(slot, p, ds)

                return carry

            lax.fori_loop(0, count, back, 0)

    def own(i, carry):
        query_block(first + i, True)
        return carry

    lax.fori_loop(0, 4, own, 0)

    def other(a, carry):
        @pl.when(touch_ref[a] > 0)
        def _():
            query_block(a, False)

        return carry

    lax.fori_loop(0, 128, other, 0)
    for slot in range(4):
        dk_ref[slot * BLK : (slot + 1) * BLK, :] = (dk_acc[slot] * scale).astype(BF16)
        dv_ref[slot * BLK : (slot + 1) * BLK, :] = dv_acc[slot].astype(BF16)


def attend(first, touch, key_blocks, counts, kv, qg):
    shape = jax.ShapeDtypeStruct((ROWS, HD), BF16)
    smem = pl.BlockSpec(memory_space=pltpu.SMEM)
    vmem = pl.BlockSpec(memory_space=pltpu.VMEM)
    return pl.pallas_call(
        attend_kernel,
        out_shape=(shape,) * 4,
        in_specs=[smem] * 4 + [vmem] * 2,
        out_specs=[vmem] * 4,
        scratch_shapes=[
            pltpu.VMEM((8, BLK, BLK), F32),
            pltpu.VMEM((BLK, HD), F32),
            pltpu.VMEM((4, BLK, HD), F32),
            pltpu.VMEM((4, BLK, HD), F32),
        ],
    )(first, touch, key_blocks, counts, kv, qg)


LAG = 2
STEPS = 33
VARIANTS = ((24, 20), (27, 23), (33, 30))
PACK = 24
GROUP = 4
OWN_QG = 3
PASS_KV = 4
NEAR_KV = 6
ALL_KV = 8
PASS_QG = 10
NEAR_QG = 12
ALL_QG = 14
CTL = 2048
AT_CODE = 128
AT_PICK = 160
AT_COUNT = 161
AT_USED = 164
AT_LIST = 256
AT_PAIRS = 1024


def plan_kernel(blocks_ref, counts_ref, ctl_ref, pick_ref, words_ref, words, where_kv, where_qg, sem):
    seq = lax.axis_index("seq")
    x, z = lax.rem(seq, NX), seq // NX
    brow = lax.broadcasted_iota(jnp.int32, (BLK, BLK), 0)
    count = counts_ref[...]
    hits = jnp.zeros((BLK, BLK), F32)
    for t in range(8):
        hits = jnp.where((blocks_ref[t : t + 1, :] == brow) & (count > t), 1.0, hits)
    row = lax.broadcasted_iota(jnp.int32, (32, BLK), 0)
    col = lax.broadcasted_iota(jnp.int32, (32, BLK), 1)
    device = lax.rem(row, NZ) * NX + row // NZ
    group = jnp.where(col // 4 == device, 1.0, 0.0)
    need_kv = dot_nt(group, hits)
    need_qg = dot_nn(group, hits)
    jrow = lax.broadcasted_iota(jnp.int32, (8, BLK), 0)
    jcol = lax.broadcasted_iota(jnp.int32, (8, BLK), 1)
    mine = jcol - seq * 4
    power = jnp.where(mine == 0, 1.0, jnp.where(mine == 1, 2.0, jnp.where(mine == 2, 4.0, jnp.where(mine == 3, 8.0, 0.0))))
    quad = lax.rem(lax.broadcasted_iota(jnp.int32, (BLK, BLK), 1), 4)
    digit = jnp.where(quad == 0, 1.0, jnp.where(quad == 1, 16.0, jnp.where(quad == 2, 256.0, 4096.0)))
    digit = jnp.where(lax.broadcasted_iota(jnp.int32, (BLK, BLK), 1) // 4 == brow, digit, 0.0)
    bits = dot_nt(dot_nn(power, hits), digit)

    origin = jcol // 16
    delta = lax.rem(jrow - origin + NZ, NZ)
    near = (delta >= 1) & (delta < 4)
    back = delta > 4
    tie = delta == 4
    far = delta.astype(F32)
    zero = jnp.zeros((8, BLK), F32)

    hops = [zero, zero]
    for column in range(NX):
        parts = [need[column * NZ : (column + 1) * NZ, :] > 0.5 for need in (need_kv, need_qg)]
        lean = zero
        for part in parts:
            lean = lean + jnp.where(part & near, 1.0, 0.0) - jnp.where(part & back, 1.0, 0.0)
        lean = jnp.broadcast_to(jnp.sum(lean, axis=1, keepdims=True), (8, BLK))
        ahead = near | (tie & (lean < 0.0))
        behind = back | (tie & (lean >= 0.0))
        for kind, part in enumerate(parts):
            for half in range(2):
                hop = jnp.where(part & ahead, far, 0.0) if half == 0 else jnp.where(part & behind, 8.0 - far, 0.0)
                most = jnp.broadcast_to(jnp.max(hop, axis=0, keepdims=True), (8, BLK))
                hops[kind] = jnp.where(jrow == column * 2 + half, most, hops[kind])

    lanes = lax.broadcasted_iota(jnp.int32, (BLK, BLK), 1)
    spread = jnp.where(jcol // 8 == jrow, 1.0, 0.0)
    lands = (brow // 16 == lax.rem(lanes, 8)) & (lanes < 64)
    sub16 = lax.broadcasted_iota(jnp.int32, (16, BLK), 0)
    lane16 = lax.broadcasted_iota(jnp.int32, (16, BLK), 1)
    fold = jnp.where(lax.rem(lane16, 16) == sub16, 1.0, 0.0)
    ident = (127 - lax.rem(lane16, 8) * 16 - sub16).astype(F32)
    apart = lax.rem(sub16 // 4 - lane16 // 16 + 2 * NX, NX)
    own, close = apart == 0, apart != 2
    low = lax.rem(sub16, 4) < 2
    first = own | ((apart == 3) & low) | ((apart == 1) & jnp.logical_not(low))
    keys = []
    for kind, base in ((0, 2048.0), (1, 0.0)):
        most = dot_nn(fold, jnp.where(lands, dot_tn(hops[kind], spread), 0.0))
        keys.append(jnp.where(most > 0.5, most * 128.0 + base + ident, 0.0))
    kv, qg = keys
    at_z = lax.rem(jcol, 8)
    forward = lax.rem(jcol // 8, 2) == 0
    history = []
    last_any, last_kv = zero, zero
    for t in range(STEPS):
        best = kv if t >= ALL_KV else jnp.where(close if t >= NEAR_KV else first if t >= PASS_KV else own, kv, 0.0)
        if t >= OWN_QG:
            best = jnp.maximum(best, qg if t >= ALL_QG else jnp.where(close if t >= NEAR_QG else first if t >= PASS_QG else own, qg, 0.0))
        best = jnp.broadcast_to(jnp.max(best, axis=0, keepdims=True), (8, BLK))
        if t >= LAG:
            before = history[t - LAG]
            up = jnp.where(at_z == 0, pltpu.roll(before, BLK - 7, 1), pltpu.roll(before, 1, 1))
            down = jnp.where(at_z == 7, pltpu.roll(before, 7, 1), pltpu.roll(before, BLK - 1, 1))
            passing = jnp.where(forward, up, down) - 128.0
            left = jnp.where(passing >= 2048.0, passing - 2048.0, passing)
            through = left > 127.5
            taken = jnp.where(through, -1.0, best)
            sent = jnp.where(through, passing, best)
            mark = jnp.where(through, -passing, best)
        else:
            taken, sent, mark = best, best, best
        taken = jnp.concatenate([taken, taken], axis=0)
        kv = jnp.where(kv == taken, 0.0, kv)
        qg = jnp.where(qg == taken, 0.0, qg)
        history.append(sent)
        last_any = jnp.where(sent > 0.0, t + 1.0, last_any)
        last_kv = jnp.where(sent >= 2048.0, t + 1.0, last_kv)
        words_ref[t : t + 1, :] = mark[0:1, :].astype(jnp.int32)
    remain = jnp.maximum(kv, qg)
    last_any = jnp.where(jnp.maximum(remain[0:8, :], remain[8:16, :]) > 0.0, 999.0, last_any)
    for t in range(STEPS - LAG, STEPS):
        left = jnp.where(history[t] >= 2048.0, history[t] - 2048.0, history[t])
        last_any = jnp.where(left > 255.5, 999.0, last_any)
    last_any = jnp.max(jnp.max(last_any, axis=1, keepdims=True), axis=0, keepdims=True)
    last_kv = jnp.max(jnp.max(last_kv, axis=1, keepdims=True), axis=0, keepdims=True)
    index = jnp.zeros((1, 1), F32)
    for steps, kv_steps in VARIANTS:
        index = index + jnp.where((last_any > steps + 0.5) | (last_kv > kv_steps + 0.5), 1.0, 0.0)
    crowd = jnp.max(jnp.sum(jnp.where(need_qg > 0.5, 1.0, 0.0), axis=1, keepdims=True), axis=0, keepdims=True)
    index = jnp.where(crowd > PACK + 0.5, float(len(VARIANTS)), index)
    words_ref[40:48, :] = blocks_ref[...]
    misc = jnp.where(jrow == 0, bits.astype(jnp.int32), jnp.broadcast_to(count, (8, BLK)))
    words_ref[48:56, :] = jnp.where(jrow == 2, jnp.broadcast_to(index, (8, BLK)).astype(jnp.int32), misc)
    copy = pltpu.make_async_copy(words_ref, words, sem)
    copy.start()
    copy.wait()

    pick_ref[0] = words[50, 0]
    for i in range(16):
        where_kv[z * 16 + i] = i
        where_qg[z * 16 + i] = i
    sources = (lax.rem(z + NZ - 1, NZ), lax.rem(z + 1, NZ))

    def slot(t, carry):
        for half in range(2):
            ctl_ref[2 * t + half] = words[t, (2 * x + half) * 8 + z]
            value = jnp.abs(words[t, (2 * x + half) * 8 + sources[half]])
            block = 127 - (value & 127)
            spot = 16 + 2 * t + half

            where_kv[jnp.where(value >= 2048, block, BLK)] = spot
            where_qg[jnp.where((value >= 128) & (value < 2048), block, BLK)] = spot
        return carry

    lax.fori_loop(0, STEPS, slot, 0, unroll=3)
    for i in range(4):
        live = words[49, 4 * seq + i]
        ctl_ref[AT_USED + i] = live
        for t in range(8):
            block = jnp.where(t < live, words[40 + t, 4 * seq + i], 4 * seq + i)
            ctl_ref[AT_CODE + i * 8 + t] = where_kv[block]

    def entry(group, totals):
        word = words[48, group]

        def listed(totals):
            n, pairs = totals
            for r in range(4):
                a = 4 * group + r
                mask = (word >> (4 * r)) & 15
                ctl_ref[AT_LIST + n] = where_qg[a]
                for j in range(4):
                    ctl_ref[AT_PAIRS + pairs] = n + a * 256 + j * 65536
                    pairs = pairs + ((mask >> j) & 1)
                n = n + jnp.where(mask > 0, 1, 0)
            return n, pairs

        return lax.cond(word > 0, listed, lambda totals: totals, totals)

    ctl_ref[AT_COUNT] = lax.fori_loop(0, BLK // 4, entry, (0, 0))[1]


def make_plan(key_blocks, counts):
    vmem = pl.BlockSpec(memory_space=pltpu.VMEM)
    return pl.pallas_call(
        plan_kernel,
        out_shape=(jax.ShapeDtypeStruct((CTL,), jnp.int32), jax.ShapeDtypeStruct((1,), jnp.int32)),
        in_specs=[vmem, vmem],
        out_specs=[pl.BlockSpec(memory_space=pltpu.SMEM)] * 2,
        scratch_shapes=[
            pltpu.VMEM((56, BLK), jnp.int32),
            pltpu.SMEM((56, BLK), jnp.int32),
            pltpu.SMEM((2 * BLK,), jnp.int32),
            pltpu.SMEM((2 * BLK,), jnp.int32),
            pltpu.SemaphoreType.DMA,
        ],
    )(key_blocks, counts)


def route_kernel(
    steps, kv_steps,
    ctl_ref, q_ref, k_ref, v_ref, g_ref,
    att_ref, dq_ref, own_kv, pack_ref, stats_ref,
    own_qg, row_kv, row_qg, land_kv, land_qg, recv_ref, late_ref, send_ref, kcat, vcat, probs, dots, mine_stats,
    head_send, head_recv, own_sem, x_send, x_recv, z_send, z_recv, s_send, s_recv,
):
    seq = lax.axis_index("seq")
    head = lax.axis_index("head")
    x, z = lax.rem(seq, NX), seq // NX

    def chip(cx, cz):
        return lax.rem(cz + 2 * NZ, NZ) * NX + lax.rem(cx + 2 * NX, NX)

    barrier = pltpu.get_barrier_semaphore()
    for shift in range(1, NH):
        pl.semaphore_signal(barrier, inc=1, device_id={"seq": seq, "head": lax.rem(head + shift, NH)}, device_id_type=MESH)
    for (cx, cz) in ((x + 1, z), (x - 1, z), (x, z + 1), (x, z - 1)):
        pl.semaphore_signal(barrier, inc=1, device_id={"seq": chip(cx, cz), "head": head}, device_id_type=MESH)
    pl.semaphore_wait(barrier, NH - 1 + 4)

    targets = ((k_ref, own_kv, 0), (v_ref, own_kv, 1), (q_ref, own_qg, 0), (g_ref, own_qg, 1))

    def rows_of(dst, which, h):
        start = pl.multiple_of(which * BLK + lax.rem(h, 2) * CHUNK, CHUNK)
        return dst.at[h // 2, pl.ds(start, CHUNK), :]

    def columns_of(src, h):
        return src.at[:, pl.ds(pl.multiple_of(h * HD, HD), HD)]

    def head_copy(array, peer_from, peer_to, shift):
        src, dst, which = targets[array]
        return pltpu.make_async_remote_copy(
            src_ref=columns_of(src, peer_to),
            dst_ref=rows_of(dst, which, peer_from),
            send_sem=head_send.at[array, shift],
            recv_sem=head_recv.at[array, shift],
            device_id={"seq": seq, "head": peer_to},
            device_id_type=MESH,
        )

    started = []
    own_copies = []
    for array, (src, dst, which) in enumerate(targets):
        for shift in (4, 3, 5, 2, 6, 1, 7):
            copy = head_copy(array, head, lax.rem(head + shift, NH), shift)
            copy.start()
            started.append(copy)
        own = pltpu.make_async_copy(columns_of(src, head), rows_of(dst, which, head), own_sem.at[array])
        own.start()
        own_copies.append(own)

    def wait_head(array):
        for shift in range(1, NH):
            peer = lax.rem(head + NH - shift, NH)
            head_copy(array, peer, peer, shift).wait_recv()
        own_copies[array].wait()

    owned = (own_kv, own_qg)
    rows = (row_kv, row_qg)
    x_plan = ((1, 0, 0), (-1, 0, 2), (1, 0, 2), (-1, 0, 0), (1, 1, 0), (-1, -1, 2))

    lands = (land_kv, land_qg)

    def x_copy(kind, i, arriving):
        sign, offset, first = x_plan[i]
        landed = lands[kind].at[2 * i : 2 * i + 2]
        source = landed if arriving else lands[kind].at[2 * i - 8 : 2 * i - 6] if offset != 0 else owned[kind].at[pl.ds(first, 2)]
        other = chip(x - sign, z) if arriving else chip(x + sign, z)
        return pltpu.make_async_remote_copy(
            src_ref=source, dst_ref=landed, send_sem=x_send.at[kind, i], recv_sem=x_recv.at[kind, i],
            device_id={"seq": other, "head": head}, device_id_type=MESH,
        )

    def keep_piece(kind, i):
        sign, offset, first = x_plan[i]
        origin = lax.rem(x - offset - sign + 2 * NX, NX)
        for r in range(2):
            rows[kind][4 * origin + first + r] = lands[kind][2 * i + r]

    def x_start(kind, i):
        copy = x_copy(kind, i, False)
        copy.start()
        started.append(copy)

    def landing(t, half):
        return recv_ref.at[2 * t + half] if t < kv_steps else late_ref.at[2 * (t - kv_steps) + half]

    def z_copy(half, t, part, arriving):
        sign = 1 if half == 0 else -1
        other = chip(x, z - sign) if arriving else chip(x, z + sign)
        slot = 2 * t + half
        rows = slice(part * BLK, part * BLK + BLK)
        return pltpu.make_async_remote_copy(
            src_ref=send_ref.at[slot, rows], dst_ref=landing(t, half).at[rows],
            send_sem=z_send.at[slot, part], recv_sem=z_recv.at[slot, part],
            device_id={"seq": other, "head": head}, device_id_type=MESH,
        )

    scale = 1.0 / math.sqrt(HD)
    key_at = lax.broadcasted_iota(jnp.int32, (1, 8 * BLK), 1)

    def attend_block(i):
        for t in range(8):
            code = ctl_ref[AT_CODE + i * 8 + t]
            near = row_kv[jnp.minimum(code, 15)]
            moved = recv_ref[jnp.clip(code - 16, 0, 2 * kv_steps - 1)]
            data = lax.select(code < 16, near, moved)
            kcat[i, t * BLK : (t + 1) * BLK, :] = data[0:BLK]
            vcat[i, t * BLK : (t + 1) * BLK, :] = data[BLK : 2 * BLK]
        q, g = own_qg[i, 0:BLK], own_qg[i, BLK : 2 * BLK]
        s = dot_nt(q, kcat[i]) * scale + jnp.where(key_at < ctl_ref[AT_USED + i] * BLK, 0.0, NEG)
        row_max = jnp.max(s, axis=1, keepdims=True)
        w = jnp.exp(s - row_max)
        row_sum = jnp.sum(w, axis=1, keepdims=True)
        scaled = 1.0 / row_sum
        att = (dot_nn(w.astype(BF16), vcat[i]) * scaled).astype(BF16)
        total = row_max + jnp.log(row_sum)
        grad_dot = jnp.sum(g.astype(F32) * att.astype(F32), axis=1, keepdims=True)
        probs[i] = w * scaled
        dots[i] = jnp.broadcast_to(grad_dot, (BLK, BLK))
        att_ref[i * BLK : (i + 1) * BLK, :] = att
        mine_stats[i : i + 1, :] = jnp.transpose(jnp.broadcast_to(total, (BLK, BLK)))[0:1, :]
        mine_stats[i + 4 : i + 5, :] = jnp.transpose(jnp.broadcast_to(grad_dot, (BLK, BLK)))[0:1, :]

    def query_grad(i):
        g = own_qg[i, BLK : 2 * BLK]
        ds = (probs[i] * (dot_nt(g, vcat[i]) - dots[i, :, 0:1])).astype(BF16)
        dq_ref[i * BLK : (i + 1) * BLK, :] = (dot_nn(ds, kcat[i]) * scale).astype(BF16)

    def stat_copy(shift, origin, target):
        return pltpu.make_async_remote_copy(
            src_ref=mine_stats, dst_ref=stats_ref.at[origin], send_sem=s_send.at[shift], recv_sem=s_recv.at[shift],
            device_id={"seq": target, "head": head}, device_id_type=MESH,
        )

    def keep_own(kind):
        for i in range(4):
            rows[kind][4 * x + i] = owned[kind][i]

    def take(kind, *pieces):
        for i in pieces:
            x_copy(kind, i, True).wait_recv()
            if i < 2:
                x_start(kind, i + 4)
        for i in pieces:
            keep_piece(kind, i)

    wait_head(0)
    wait_head(1)
    for i in range(4):
        x_start(0, i)

    def send_stats():
        for shift in range(1, NX * NZ):
            copy = stat_copy(shift, seq, lax.rem(seq + shift, NX * NZ))
            copy.start()
            started.append(copy)
        own = pltpu.make_async_copy(mine_stats, stats_ref.at[seq], s_recv.at[0])
        own.start()
        own_copies.append(own)

    work = [functools.partial(attend_block, i) for i in range(4)] + [send_stats]
    work += [functools.partial(query_grad, i) for i in range(4)]
    for t in range(steps):
        if t == OWN_QG:
            wait_head(2)
            wait_head(3)
        elif t == PASS_KV:
            take(0, 0, 1)
            for i in range(4):
                x_start(1, i)
            keep_own(0)
            keep_own(1)
        elif t == NEAR_KV:
            take(0, 2, 3)
        elif t == ALL_KV:
            take(0, 4, 5)
        elif t == PASS_QG:
            take(1, 0, 1)
        elif t == NEAR_QG:
            take(1, 2, 3)
        elif t == ALL_QG:
            take(1, 4, 5)
        for part in range(2):
            rows_at = slice(part * BLK, part * BLK + BLK)
            for half in range(2):
                slot = 2 * t + half
                value = ctl_ref[slot]
                size = jnp.abs(value)
                index = (127 - (size & 127)) & 15
                data = row_kv[index, rows_at] if t >= PASS_KV else own_kv[index & 3, rows_at]
                if t >= OWN_QG:
                    other = row_qg[index, rows_at] if t >= PASS_QG else own_qg[index & 3, rows_at]
                    data = lax.select(size >= 2048, data, other)
                if t >= LAG:
                    z_copy(half, t - LAG, part, True).wait_recv()
                    data = lax.select(value < 0, landing(t - LAG, half)[rows_at], data)
                send_ref[slot, rows_at] = data
            for half in range(2):
                copy = z_copy(half, t, part, False)
                copy.start()
                started.append(copy)
        if t >= kv_steps + LAG - 1 and work:
            work.pop(0)()
    while work:
        work.pop(0)()
    for t in range(steps - LAG, steps):
        for half in range(2):
            for part in range(2):
                z_copy(half, t, part, True).wait_recv()
    for n in range(PACK):
        code = ctl_ref[AT_LIST + n]
        data = lax.select(code < 16, row_qg[jnp.clip(code, 0, 15)], recv_ref[jnp.clip(code - 16, 0, 2 * kv_steps - 1)])
        last = 16 + 2 * kv_steps
        pack_ref[n] = lax.select(code < last, data, late_ref[jnp.clip(code - last, 0, 2 * (steps - kv_steps) - 1)])
    for shift in range(1, NX * NZ):
        peer = lax.rem(seq + NX * NZ - shift, NX * NZ)
        stat_copy(shift, peer, peer).wait_recv()
    own_copies[-1].wait()
    for copy in started:
        copy.wait_send()


def route(variant, ctl, queries, keys, values, out_grad):
    steps, kv_steps = VARIANTS[variant]
    smem = pl.BlockSpec(memory_space=pltpu.SMEM)
    vmem = pl.BlockSpec(memory_space=pltpu.VMEM)
    out = jax.ShapeDtypeStruct((ROWS, HD), BF16)
    own = (4, 2 * BLK, HD)
    near = (16, 2 * BLK, HD)
    moved = (2 * steps, 2 * BLK, HD)
    early = (2 * kv_steps, 2 * BLK, HD)
    late = (2 * (steps - kv_steps), 2 * BLK, HD)
    stats = jax.ShapeDtypeStruct((NX * NZ, 8, BLK), F32)
    dma = pltpu.SemaphoreType.DMA
    return pl.pallas_call(
        functools.partial(route_kernel, steps, kv_steps),
        out_shape=(out, out, jax.ShapeDtypeStruct(own, BF16), jax.ShapeDtypeStruct((PACK, 2 * BLK, HD), BF16), stats),
        in_specs=[smem] + [vmem] * 4,
        out_specs=[vmem] * 5,
        scratch_shapes=[
            pltpu.VMEM(own, BF16),
            pltpu.VMEM(near, BF16),
            pltpu.VMEM(near, BF16),
            pltpu.VMEM((12, 2 * BLK, HD), BF16),
            pltpu.VMEM((12, 2 * BLK, HD), BF16),
            pltpu.VMEM(early, BF16),
            pltpu.VMEM(late, BF16),
            pltpu.VMEM(moved, BF16),
            pltpu.VMEM((4, 8 * BLK, HD), BF16),
            pltpu.VMEM((4, 8 * BLK, HD), BF16),
            pltpu.VMEM((4, BLK, 8 * BLK), F32),
            pltpu.VMEM((4, BLK, BLK), F32),
            pltpu.VMEM((8, BLK), F32),
            dma((4, NH)), dma((4, NH)), dma((4,)),
            dma((2, 6)), dma((2, 6)),
            dma((2 * steps, 2)), dma((2 * steps, 2)),
            dma((NX * NZ,)), dma((NX * NZ,)),
        ],
        compiler_params=pltpu.CompilerParams(collective_id=1 + variant, has_side_effects=True),
    )(ctl, queries, keys, values, out_grad)


def keys_kernel(ctl_ref, kv_ref, pack_ref, stats_ref, att_ref, dq_ref, att_out, dq_out, dk_ref, dv_ref, dk_acc, dv_acc):
    scale = 1.0 / math.sqrt(HD)
    att_out[...] = att_ref[...]
    dq_out[...] = dq_ref[...]
    dk_acc[...] = jnp.zeros_like(dk_acc)
    dv_acc[...] = jnp.zeros_like(dv_acc)
    pairs = ctl_ref[AT_COUNT]

    def trip(i, carry):
        sums = []
        for u in range(GROUP):
            at = GROUP * i + u
            word = ctl_ref[AT_PAIRS + jnp.minimum(at, pairs - 1)]
            n, a, j = word & 255, (word >> 8) & 255, word >> 16
            unused = jnp.where(at < pairs, 0.0, 1e30)
            q, g = pack_ref[n, 0:BLK, :], pack_ref[n, BLK : 2 * BLK, :]
            total = stats_ref[a // 4, pl.ds(lax.rem(a, 4), 1), :] + unused
            grad_dot = stats_ref[a // 4, pl.ds(lax.rem(a, 4) + 4, 1), :]
            p = jnp.exp(dot_nt(kv_ref[j, 0:BLK, :], q) * scale - total)
            ds = (p * (dot_nt(kv_ref[j, BLK : 2 * BLK, :], g) - grad_dot)).astype(BF16)
            sums.append((j, dot_nn(ds, q), dot_nn(p.astype(BF16), g)))
        for j, dk, dv in sums:
            dk_acc[j] += dk
            dv_acc[j] += dv
        return carry

    lax.fori_loop(0, (pairs + GROUP - 1) // GROUP, trip, 0)
    for j in range(4):
        dk_ref[j * BLK : (j + 1) * BLK, :] = (dk_acc[j] * scale).astype(BF16)
        dv_ref[j * BLK : (j + 1) * BLK, :] = dv_acc[j].astype(BF16)


def key_grads(ctl, kv, pack, stats, att, dq):
    smem = pl.BlockSpec(memory_space=pltpu.SMEM)
    vmem = pl.BlockSpec(memory_space=pltpu.VMEM)
    out = jax.ShapeDtypeStruct((ROWS, HD), BF16)
    return pl.pallas_call(
        keys_kernel,
        out_shape=(out,) * 4,
        in_specs=[smem] + [vmem] * 5,
        out_specs=[vmem] * 4,
        scratch_shapes=[
            pltpu.VMEM((4, BLK, HD), F32),
            pltpu.VMEM((4, BLK, HD), F32),
        ],
    )(ctl, kv, pack, stats, att, dq)


def on_device(queries, keys, values, out_grad, key_blocks, counts):
    seq = lax.axis_index("seq")
    ctl, choice = make_plan(jnp.transpose(key_blocks), counts[None, :])

    def sparse(variant):
        att, dq, kv, pack, stats = route(variant, ctl, queries, keys, values, out_grad)
        return tuple(key_grads(ctl, kv, pack, stats, att, dq))

    def dense():
        kv, qg = exchange(queries, keys, values, out_grad)
        live = jnp.arange(key_blocks.shape[1])[None, :] < counts[:, None]
        touch = jnp.any(live & (key_blocks // 4 == seq), axis=1)
        touch = (touch & (jnp.arange(key_blocks.shape[0]) // 4 != seq)).astype(jnp.int32)
        first = (seq * 4).reshape(1).astype(jnp.int32)
        return tuple(attend(first, touch, key_blocks, counts, kv, qg))

    branches = [functools.partial(sparse, variant) for variant in range(len(VARIANTS))] + [dense]
    return lax.switch(choice[0], branches)


def solution(mesh):
    rows = P(("seq", "head"), None)
    out = P("seq", "head")
    return jax.shard_map(
        on_device,
        mesh=mesh,
        in_specs=(rows,) * 4 + (P(), P()),
        out_specs=(out,) * 4,
        check_vma=False,
    )
```
